32 devices in a mesh: groups: 2 (over y), region: 4 (over z), stn: 2 (over x), chan: 2 (over core).
Axes of the slice: x: 2, y: 2, z: 4, core: 2. Of those that a mesh axis runs over, the one named last changes fastest.
Arguments:
- archive: bfloat16 [20, 3, 65536], P('stn', None, ('groups', 'region')), parts along dimension 2, may hold values from -10 to 10
- starts: int32 [512], P(('groups', 'region')), parts along dimension 0, may hold values from 0 to 32368, as said below
- event_owner: int32 [512], P('groups'), parts along dimension 0, may hold values from 0 to 3, as said below
- station_mask: int32 [512, 20], P('groups'), parts along dimension 0, may hold values 0 or 1
- pair_first: int32 [4096], P(('groups', 'region')), parts along dimension 0, may hold values from 0 to 255, as said below
- pair_second: int32 [4096], P(('groups', 'region')), parts along dimension 0, may hold values from 0 to 255, as said below
- pair_count: int32 [8], P(('groups', 'region')), parts along dimension 0, may hold values from 128 to 512, as said below
Outputs:
- pair_stack: float32 [101, 4096], P(None, ('groups', 'region')), parts along dimension 1
- event_profile: float32 [101, 1024], P(None, ('groups', 'region')), parts along dimension 1
The draws below stay inside these ranges and needn't reach their ends.
There are 2 independent parts, one for each index of `groups`. The reference program is written for one: setup_inputs(seed, part) draws one part's arguments, and reference() takes and returns one part's arrays. A program takes and returns all parts, laid end to end along the dimension named above; each array names one. Nothing has to cross between parts.
Inputs may be any that keep to these rules, and one draw needn't show every extreme that they name: The window of event e lies in time segment e // 64: starts[e] - (e // 64) * 8192 is between 0 and 7792; in every segment some window starts at the segment's first sample and another ends at its last sample. `event_owner`: among the 64 events of one time segment at most 32 have the same owner; every owner holds at least one event of each segment, and one owner holds exactly 32 of every segment. `pair_first`: entry p names an event owned by region p // 512. `pair_second`: entry p names an event other than pair_first[p], owned by region p // 512 or the next region. Entries of region r at or past pair_count[r] are padding; some region uses all 512.
All inputs are finite; a program needn't handle non-finite values.
Results may differ from the reference program's by a relative error of at most 0.0047.
Values may be sent and summed in bfloat16 or wider, within the bound.
No kernel may reach another device: no remote copies, remote signals or barrier semaphores. Data moves between devices by JAX's collectives and lax.ppermute only.
A program may use at most 64 MiB of HBM per device.

```python
import math
import jax
import jax.numpy as jnp
from jax import lax

STATIONS = 20
COMP = 3
WIN = 400
MAXLAG = 50
NFFT = 512
EV_DEV = 64
SEG_DEV = 8192
PAIR_CAP = 512
LAGS = 101
BUCKET = 32
SLOTS = 128
EVENTS = 256
SAMPLES = 32768
PAIRS = 2048
N_REGION = 4
N_CHAN = 2


def owner_table(key):
    root_key = jax.random.fold_in(key, 101)
    busiest = jax.random.randint(jax.random.fold_in(root_key, 1), (), 0, N_REGION)
    block_keys = jax.random.split(jax.random.fold_in(root_key, 2), N_REGION)
    candidates = jnp.arange(N_REGION * (BUCKET - 1), dtype=jnp.int32) // (BUCKET - 1)
    remaining = EV_DEV - BUCKET + 1 - N_REGION

    def one_block(block_key):
        first_key, second_key = jax.random.split(block_key)
        ranking = jax.random.permutation(first_key, N_REGION * (BUCKET - 1)).astype(jnp.int32)
        ranking = ranking + jnp.where(candidates == busiest, N_REGION * BUCKET, 0)
        chosen = candidates[jnp.argsort(ranking)[:remaining]]
        labels = jnp.concatenate([jnp.full((BUCKET - 1,), busiest, jnp.int32), jnp.arange(N_REGION, dtype=jnp.int32), chosen])
        return jax.random.permutation(second_key, labels)
    return (jax.vmap(one_block)(block_keys).reshape(-1).astype(jnp.int32), busiest)


def pair_lists(key):
    owners, busiest = owner_table(key)
    root_key = jax.random.fold_in(key, 202)
    region_keys = jax.random.split(root_key, N_REGION)

    def one_region(region, region_key):
        key_one, key_two, key_three, key_four = jax.random.split(region_key, 4)
        mine = owners == region
        nearby = mine | (owners == region + 1)
        first_rank = jax.random.permutation(key_one, EVENTS).astype(jnp.int32) + jnp.where(mine, 0, EVENTS)
        second_rank = jax.random.permutation(key_two, EVENTS).astype(jnp.int32) + jnp.where(nearby, 0, EVENTS)
        first_list = jnp.argsort(first_rank).astype(jnp.int32)
        second_list = jnp.argsort(second_rank).astype(jnp.int32)
        count_mine = jnp.sum(mine.astype(jnp.int32))
        count_near = jnp.sum(nearby.astype(jnp.int32))
        first_pick = jax.random.randint(key_three, (PAIR_CAP,), 0, count_mine)
        second_pick = jax.random.randint(key_four, (PAIR_CAP,), 0, count_near)
        firsts = first_list[first_pick]
        seconds = second_list[second_pick]
        seconds = jnp.where(seconds == firsts, second_list[(second_pick + 1) % count_near], seconds)
        return (firsts, seconds)
    firsts, seconds = jax.vmap(one_region)(jnp.arange(N_REGION, dtype=jnp.int32), region_keys)
    counts = jax.random.randint(jax.random.fold_in(root_key, 3), (N_REGION,), PAIR_CAP // 4, PAIR_CAP + 1)
    counts = jnp.where(jnp.arange(N_REGION, dtype=jnp.int32) == busiest, PAIR_CAP, counts)
    return (firsts.reshape(-1).astype(jnp.int32), seconds.reshape(-1).astype(jnp.int32), counts.astype(jnp.int32))


def draw_event_owner(key, part):
    return owner_table(key)[0]


def draw_pair_first(key, part):
    return pair_lists(key)[0]


def draw_pair_second(key, part):
    return pair_lists(key)[1]


def draw_pair_count(key, part):
    return pair_lists(key)[2]


def draw_starts(key, part):
    base_key = jax.random.fold_in(key, 303)
    segment = jnp.arange(EVENTS, dtype=jnp.int32) // EV_DEV
    within = jnp.arange(EVENTS, dtype=jnp.int32) % EV_DEV
    offset = jax.random.randint(jax.random.fold_in(base_key, 1), (EVENTS,), 0, SEG_DEV - WIN + 1)
    high_pos = jax.random.randint(jax.random.fold_in(base_key, 2), (N_REGION,), 0, EV_DEV)
    step_pos = jax.random.randint(jax.random.fold_in(base_key, 3), (N_REGION,), 1, EV_DEV)
    low_pos = (high_pos + step_pos) % EV_DEV
    offset = jnp.where(within == high_pos[segment], SEG_DEV - WIN, offset)
    offset = jnp.where(within == low_pos[segment], 0, offset)
    return (segment * SEG_DEV + offset).astype(jnp.int32)


def draw_archive(key, part):
    noise_key, gain_key = jax.random.split(jax.random.fold_in(key, 404))
    noise = jnp.clip(jax.random.normal(noise_key, (STATIONS, COMP, SAMPLES), jnp.float32), -5.0, 5.0)
    gains = jnp.exp(jax.random.uniform(gain_key, (STATIONS, COMP, 1), jnp.float32, math.log(0.5), math.log(2.0)))
    return (noise * gains).astype(jnp.bfloat16)


def place_ends(result, rng, low, high):
    extent = result.shape
    place = [jax.random.randint(jax.random.fold_in(rng, axis), (), 0, extent[axis]) for axis in range(len(extent))]
    result = result.at[tuple(place)].set(low)
    longest = extent.index(max(extent))
    place[longest] = (place[longest] + 1) % extent[longest]
    return result.at[tuple(place)].set(high)


def setup_inputs(seed: int = 0, part: int = 0) -> dict:
    key_of = jax.random.split(jax.random.key(seed), 8)
    part_splits = jax.random.split(jax.random.fold_in(key_of[7], part), 8)
    return {
        "archive": draw_archive(jax.random.fold_in(jax.random.fold_in(key_of[7], part), 71), part),
        "starts": draw_starts(jax.random.fold_in(jax.random.fold_in(key_of[7], part), 71), part),
        "event_owner": draw_event_owner(jax.random.fold_in(jax.random.fold_in(key_of[7], part), 71), part),
        "station_mask": place_ends((jax.random.randint(part_splits[3], (EVENTS, STATIONS), 0, 2) < 1).astype(jnp.int32), jax.random.fold_in(part_splits[3], 1), 0, 1),
        "pair_first": draw_pair_first(jax.random.fold_in(jax.random.fold_in(key_of[7], part), 71), part),
        "pair_second": draw_pair_second(jax.random.fold_in(jax.random.fold_in(key_of[7], part), 71), part),
        "pair_count": draw_pair_count(jax.random.fold_in(jax.random.fold_in(key_of[7], part), 71), part),
    }


def forward_table(chan_index, half):
    sample = jnp.arange(WIN, dtype=jnp.int32)[:, None]
    column = jnp.arange(2 * half, dtype=jnp.int32)[None, :]
    freq = chan_index * half + column % half
    phase = (sample * freq % NFFT).astype(jnp.float32) * jnp.float32(2.0 * math.pi / NFFT)
    nyquist = (sample * (NFFT // 2) % NFFT).astype(jnp.float32) * jnp.float32(2.0 * math.pi / NFFT)
    sine = jnp.where((chan_index == 0) & (column == half), jnp.cos(nyquist), jnp.sin(phase))
    return jnp.where(column < half, jnp.cos(phase), sine).astype(jnp.bfloat16)

def lag_table(chan_index, half):
    shift_lag = jnp.arange(LAGS, dtype=jnp.int32)[:, None] - MAXLAG
    freq = chan_index * half + jnp.arange(half, dtype=jnp.int32)[None, :]
    phase = (freq * shift_lag % NFFT).astype(jnp.float32) * jnp.float32(2.0 * math.pi / NFFT)
    nyquist = (shift_lag * (NFFT // 2) % NFFT).astype(jnp.float32) * jnp.float32(2.0 * math.pi / NFFT)
    weight = jnp.where(freq == 0, jnp.float32(1.0 / NFFT), jnp.float32(2.0 / NFFT))
    first_part = weight * jnp.cos(phase)
    second_part = jnp.where(freq == 0, jnp.cos(nyquist) * jnp.float32(1.0 / NFFT), weight * jnp.cos(phase))
    third_part = jnp.where(freq == 0, jnp.float32(0.0), -weight * jnp.sin(phase))
    return jnp.concatenate([first_part, second_part, third_part], axis=1)

def slot_table(event_owner, regions, per_block, bucket, slots):
    blocks = event_owner.reshape(regions, per_block)
    onehot = (blocks[:, :, None] == jnp.arange(regions, dtype=jnp.int32)[None, None, :]).astype(jnp.int32)
    before = jnp.cumsum(onehot, axis=1) - onehot
    ranking = lax.optimization_barrier(jnp.sum(before * onehot, axis=2))
    block_index = jnp.arange(regions, dtype=jnp.int32)[:, None]
    return (blocks * slots + block_index * bucket + ranking).reshape(-1)

def reference(archive, starts, event_owner, station_mask, pair_first, pair_second, pair_count):
    half = NFFT // (2 * N_CHAN)
    fwd = jnp.concatenate([forward_table(index, half) for index in range(N_CHAN)], axis=1)
    lag_weights = jnp.stack([lag_table(index, half) for index in range(N_CHAN)], axis=0)

    def cut_window(start):
        return lax.dynamic_slice_in_dim(archive, start, WIN, axis=2)
    windows = jax.vmap(cut_window)(starts)
    windows = windows * station_mask[:, :, None, None].astype(jnp.bfloat16)
    flat = windows.reshape(-1, WIN)
    wide = flat.astype(jnp.float32)
    energy = lax.optimization_barrier(jnp.sum(wide * wide, axis=1, keepdims=True))
    coefs = jnp.dot(flat, fwd, preferred_element_type=jnp.float32)
    spectra = (coefs * lax.rsqrt(energy + WIN * 1e-05)).astype(jnp.bfloat16)
    spectra = spectra.reshape(EVENTS, STATIONS, COMP, N_CHAN, 2 * half)

    def block_cross(indices):
        firsts, seconds = indices
        left = spectra[firsts].astype(jnp.float32)
        right = spectra[seconds].astype(jnp.float32)
        left_cos, left_sin = (left[..., :half], left[..., half:])
        right_cos, right_sin = (right[..., :half], right[..., half:])
        prod_one = lax.optimization_barrier(jnp.sum(left_cos * right_cos, axis=(1, 2)))
        prod_two = lax.optimization_barrier(jnp.sum(left_sin * right_sin, axis=(1, 2)))
        prod_three = lax.optimization_barrier(jnp.sum(left_sin * right_cos - left_cos * right_sin, axis=(1, 2)))
        stacked = jnp.concatenate([prod_one, prod_two, prod_three], axis=-1)
        return jnp.einsum('pjk,jlk->pl', stacked, lag_weights, precision=lax.Precision.HIGHEST)
    cross = lax.map(block_cross, (pair_first.reshape(-1, 128), pair_second.reshape(-1, 128)))
    cross = cross.reshape(PAIRS, LAGS)
    live = COMP * lax.optimization_barrier(jnp.sum(station_mask[pair_first] * station_mask[pair_second], axis=1))
    valid = jnp.arange(PAIRS, dtype=jnp.int32) % PAIR_CAP < jnp.repeat(pair_count, PAIR_CAP)
    scaled = jnp.float32(math.sqrt(WIN)) * cross / jnp.sqrt(jnp.maximum(live, 1).astype(jnp.float32))[:, None]
    stack = jnp.where(valid[:, None], scaled, jnp.float32(0.0))
    slot_of = slot_table(event_owner, N_REGION, EV_DEV, BUCKET, SLOTS)
    profile = jnp.zeros((N_REGION * SLOTS, LAGS), jnp.float32)
    profile = profile.at[slot_of[pair_first]].add(stack)
    profile = profile.at[slot_of[pair_second]].add(stack[:, ::-1])
    return (stack.T, profile.T)
```

```python
import math

import jax
import jax.numpy as jnp
import numpy as np
from jax import lax
from jax.experimental import pallas as pl
from jax.experimental.pallas import tpu as pltpu
from jax.sharding import PartitionSpec as P

COMP = 3
WIN = 400
MAXLAG = 50
NFFT = 512
LAGS = 101
BINS = NFFT // 2
LANES = 128
LAG_ROWS = 112
NT = (((1,), (1,)), ((), ()))


def forward_table():
    sample = np.arange(NFFT)[:, None]
    freq = np.arange(BINS)[None, :]
    angle = (sample * freq % NFFT) * (2.0 * math.pi / NFFT)
    sine = np.sin(angle)
    sine[:, 0] = np.cos(math.pi * (np.arange(NFFT) % 2))
    table = np.concatenate([np.cos(angle), sine], axis=1)
    table[WIN:] = 0.0
    return jnp.asarray(table, jnp.float32).astype(jnp.bfloat16)


def lag_table():
    shift = np.arange(LANES)[:, None] - MAXLAG
    freq = np.arange(BINS)[None, :]
    angle = (freq * shift % NFFT) * (2.0 * math.pi / NFFT)
    weight = np.where(freq == 0, 1.0 / NFFT, 2.0 / NFFT)
    even = weight * np.cos(angle)
    odd = -weight * np.sin(angle)
    odd[:, 0] = np.cos(math.pi * (shift[:, 0] % 2)) / NFFT
    table = np.concatenate([even, odd], axis=1) * math.sqrt(WIN)
    table[LAGS:] = 0.0
    high = jnp.asarray(table, jnp.float32).astype(jnp.bfloat16)
    low = (jnp.asarray(table, jnp.float32) - high.astype(jnp.float32)).astype(jnp.bfloat16)
    return jnp.concatenate([high, low], axis=0)


def slot_table(event_owner, regions, per_block, bucket, slots):
    blocks = event_owner.reshape(regions, per_block)
    owned = blocks[:, :, None] == jnp.arange(regions, dtype=jnp.int32)[None, None, :]
    onehot = owned.astype(jnp.int32)
    before = jnp.cumsum(onehot, axis=1) - onehot
    ranking = jnp.sum(before * onehot, axis=2)
    block_index = jnp.arange(regions, dtype=jnp.int32)[:, None]
    return (blocks * slots + block_index * bucket + ranking).reshape(-1)


def split(value):
    high = value.astype(jnp.bfloat16)
    return high, (value - high.astype(jnp.float32)).astype(jnp.bfloat16)


def correlate(regions, per_block, pair_cap, segment, slots, nch):
    rows = 2 * nch
    tiles = segment // LANES + 2

    def kernel(recv, mask, slot_event, table, weights, out, shifted, windows, cos_rows, sin_rows, even, odd,
               index_vmem, index, profile, sem):
        for part in range(regions):
            digits = recv[part, :, segment:].astype(jnp.float32)
            first = digits[0:1, :pair_cap] * 128.0 + digits[1:2, :pair_cap]
            second = digits[2:3, :pair_cap] * 128.0 + digits[3:4, :pair_cap]
            index_vmem[part, 0:1, :] = first.astype(jnp.int32) * rows
            index_vmem[part, 1:2, :] = second.astype(jnp.int32) * rows
            offset = digits[1:2, pair_cap:] * 128.0 + digits[2:3, pair_cap:]
            index_vmem[part, 2:3, :] = offset.astype(jnp.int32)
        copy = pltpu.make_async_copy(index_vmem, index, sem)
        copy.start()

        half = 2 * LANES

        def widen(part, carry):
            for k in range(tiles + 2):
                data = recv[part, :, k * LANES : (k + 1) * LANES].astype(jnp.float32)
                if k < tiles:
                    shifted[part, k, pl.ds(0, nch, stride=2), :] = data
                if k >= 2:
                    shifted[part, k - 2, pl.ds(1, nch, stride=2), :] = data
            return carry

        lax.fori_loop(0, regions, widen, 0)
        copy.wait()

        lane = lax.broadcasted_iota(jnp.int32, (rows, LANES), 1)
        odd_row = lax.broadcasted_iota(jnp.int32, (rows, LANES), 0) % 2
        keep = odd_row * half + LANES + lane < WIN

        def one_segment(part, carry):
            def one_event(group, inner):
                for step in range(4):
                    event = group * 4 + step
                    start = index[part, 2, event]
                    base = start // LANES
                    off = start % LANES
                    turn = (LANES - off) % LANES
                    data = [shifted[part, base + k] for k in range(3)]
                    later = lane >= off
                    row = pl.multiple_of(event * rows, rows)
                    near = pltpu.roll(jnp.where(later, data[0], data[1]), turn, 1)
                    far = pltpu.roll(jnp.where(later, data[1], data[2]), turn, 1)
                    windows[0, pl.ds(row, rows), :] = near
                    windows[1, pl.ds(row, rows), :] = jnp.where(keep, far, 0.0)
                return inner

            lax.fori_loop(0, per_block // 4, one_event, 0)
            count = per_block * nch
            early, late = (
                jnp.concatenate([windows[t, pl.ds(k, count, stride=2), :] for t in range(2)], axis=1)
                for k in range(2))
            energy = jnp.sum(early * early + late * late, axis=1, keepdims=True)
            coefs = jnp.dot(early.astype(jnp.bfloat16), table[:half, :], preferred_element_type=jnp.float32)
            coefs += jnp.dot(late.astype(jnp.bfloat16), table[half:, :], preferred_element_type=jnp.float32)
            place = pl.multiple_of(part * count, count)
            factor = mask[pl.ds(place, count), :] * lax.rsqrt(energy + WIN * 1e-05)
            for k in range(2):
                piece = coefs[:, k * LANES : (k + 1) * LANES] * factor
                cos_rows[pl.ds(2 * place + k, count, stride=2), :] = piece.astype(jnp.bfloat16).astype(jnp.float32)
                piece = coefs[:, BINS + k * LANES : BINS + (k + 1) * LANES] * factor
                sin_rows[pl.ds(2 * place + k, count, stride=2), :] = piece.astype(jnp.bfloat16).astype(jnp.float32)
            return carry

        lax.fori_loop(0, regions, one_segment, 0)

        special = (odd_row == 0) & (lane == 0)
        profile[...] = jnp.zeros_like(profile)

        def one_region(part, carry):
            def some_pairs(group, inner):
                for step in range(8):
                    pair = group * 8 + step
                    a = pl.multiple_of(index[part, 0, pair], rows)
                    b = pl.multiple_of(index[part, 1, pair], rows)
                    cos_a, sin_a = cos_rows[pl.ds(a, rows), :], sin_rows[pl.ds(a, rows), :]
                    cos_b, sin_b = cos_rows[pl.ds(b, rows), :], sin_rows[pl.ds(b, rows), :]
                    sines = sin_a * sin_b
                    place = pl.multiple_of(pair * rows, rows)
                    even[pl.ds(place, rows), :] = cos_a * cos_b + jnp.where(special, 0.0, sines)
                    odd[pl.ds(place, rows), :] = jnp.where(special, sines, sin_a * cos_b - cos_a * sin_b)
                return inner

            lax.fori_loop(0, pair_cap // 8, some_pairs, 0)
            sums = []
            for store in (even, odd):
                for k in range(2):
                    total = store[pl.ds(k, pair_cap, stride=rows), :]
                    for c in range(1, nch):
                        total += store[pl.ds(2 * c + k, pair_cap, stride=rows), :]
                    sums.append(total)
            high, low = split(jnp.concatenate(sums, axis=1))
            both = lax.dot_general(weights[...], high, NT, preferred_element_type=jnp.float32)
            rest = lax.dot_general(weights[:LANES, :], low, NT, preferred_element_type=jnp.float32)
            cross = both[:LANES] + both[LANES:] + rest
            digits = recv[part, :, segment:].astype(jnp.float32)
            code = digits[0:1, pair_cap:]
            live = jnp.maximum((code - 1.0) * COMP, 1.0)
            stack = cross * jnp.where(code > 0.0, lax.rsqrt(live), 0.0)
            out[part, :, :pair_cap] = stack[:LAG_ROWS]
            first = digits[0:1, :pair_cap] * 128.0 + digits[1:2, :pair_cap]
            second = digits[2:3, :pair_cap] * 128.0 + digits[3:4, :pair_cap]
            high, low = split(stack)

            def gathered(names, event):
                hot = (jnp.concatenate([names] * (pair_cap // LANES), axis=1) == event).astype(jnp.float32)
                hot = hot.astype(jnp.bfloat16)
                return lax.dot_general(high, hot, NT, preferred_element_type=jnp.float32) + lax.dot_general(
                    low, hot, NT, preferred_element_type=jnp.float32)

            own = slot_event[pl.ds(pl.multiple_of(part * slots, slots), slots), :]
            profile[0, part] += gathered(own, first)
            profile[1, part] += gathered(own, second)

            @pl.when(part + 1 < regions)
            def _():
                then = slot_event[pl.ds(pl.multiple_of((part + 1) * slots, slots), slots), :]
                profile[1, part + 1] += gathered(then, second)
            return carry

        lax.fori_loop(0, regions, one_region, 0)
        mirrored = lax.broadcasted_iota(jnp.int32, (LANES, LANES), 0) + lax.broadcasted_iota(
            jnp.int32, (LANES, LANES), 1) == LAGS - 1
        mirror = mirrored.astype(jnp.float32).astype(jnp.bfloat16)

        def finish(part, carry):
            high, low = split(profile[1, part])
            flipped = jnp.dot(mirror, high, preferred_element_type=jnp.float32) + jnp.dot(
                mirror, low, preferred_element_type=jnp.float32)
            out[part, :, pair_cap:] = (profile[0, part] + flipped)[:LAG_ROWS]
            return carry

        lax.fori_loop(0, regions, finish, 0)

    events = regions * per_block
    return pl.pallas_call(
        kernel,
        out_shape=jax.ShapeDtypeStruct((regions, LAG_ROWS, pair_cap + slots), jnp.float32),
        in_specs=[pl.BlockSpec(memory_space=pltpu.VMEM)] * 5,
        out_specs=pl.BlockSpec(memory_space=pltpu.VMEM),
        scratch_shapes=[
            pltpu.VMEM((regions, tiles, rows, LANES), jnp.float32),
            pltpu.VMEM((2, per_block * rows, LANES), jnp.float32),
            pltpu.VMEM((events * rows, LANES), jnp.float32),
            pltpu.VMEM((events * rows, LANES), jnp.float32),
            pltpu.VMEM((pair_cap * rows, LANES), jnp.float32),
            pltpu.VMEM((pair_cap * rows, LANES), jnp.float32),
            pltpu.VMEM((regions, 3, pair_cap), jnp.int32),
            pltpu.SMEM((regions, 3, pair_cap), jnp.int32),
            pltpu.VMEM((2, regions, LANES, slots), jnp.float32),
            pltpu.SemaphoreType.DMA(()),
        ],
        name="correlate",
    )


def on_device(archive, starts, event_owner, station_mask, pair_first, pair_second, pair_count):
    regions = lax.axis_size("region")
    region_index = lax.axis_index("region")
    station_index = lax.axis_index("stn")
    chan_index = lax.axis_index("chan")
    chans = lax.axis_size("chan")
    per_block = starts.shape[0]
    pair_cap = pair_first.shape[0]
    station_count = archive.shape[0]
    segment = archive.shape[2]
    channels = station_count * COMP
    bucket = max(2, 2 * per_block // regions)
    slots = regions * bucket
    nch = 4 * -(-channels // (4 * chans * regions))
    events = regions * per_block

    offsets = starts - region_index * segment
    mask_bf16 = station_mask.astype(jnp.bfloat16)
    names = jnp.arange(events, dtype=jnp.int32)[None, :]
    mask_first = jnp.dot((pair_first[:, None] == names).astype(jnp.bfloat16), mask_bf16,
                         preferred_element_type=jnp.float32)
    mask_second = jnp.dot((pair_second[:, None] == names).astype(jnp.bfloat16), mask_bf16,
                          preferred_element_type=jnp.float32)
    common = jnp.sum(mask_first * mask_second, axis=1)
    valid = jnp.arange(pair_cap, dtype=jnp.int32) < pair_count[0]
    code = jnp.where(valid, common + 1.0, 0.0).astype(jnp.bfloat16)
    pad = jnp.zeros((pair_cap - per_block,), jnp.bfloat16)
    digit_rows = jnp.stack([
        jnp.concatenate([(pair_first // 128).astype(jnp.bfloat16), code]),
        jnp.concatenate([(pair_first % 128).astype(jnp.bfloat16), (offsets // 128).astype(jnp.bfloat16), pad]),
        jnp.concatenate([(pair_second // 128).astype(jnp.bfloat16), (offsets % 128).astype(jnp.bfloat16), pad]),
        jnp.concatenate([(pair_second % 128).astype(jnp.bfloat16), jnp.zeros((pair_cap,), jnp.bfloat16)]),
    ])
    if nch > 4:
        digit_rows = jnp.pad(digit_rows, ((0, nch - 4), (0, 0)))
    flat = archive.reshape(channels, segment)
    flat = jnp.pad(flat, ((0, chans * regions * nch - channels), (0, 0)))
    mine = lax.dynamic_slice_in_dim(flat, chan_index * regions * nch, regions * nch)
    digits = jnp.broadcast_to(digit_rows[None], (regions,) + digit_rows.shape)
    payload = jnp.concatenate([mine.reshape(regions, nch, segment), digits], axis=2)
    received = lax.all_to_all(payload, "region", split_axis=0, concat_axis=0, tiled=True)

    slot_of = slot_table(event_owner, regions, per_block, bucket, slots)
    hit = slot_of[None, :] == jnp.arange(regions * slots, dtype=jnp.int32)[:, None]
    slot_event = jnp.sum(jnp.where(hit, names + 1, 0), axis=1) - 1
    slot_event = jnp.broadcast_to(slot_event.astype(jnp.float32)[:, None], (regions * slots, LANES))
    channel = (chan_index * regions + region_index) * nch + jnp.arange(nch, dtype=jnp.int32)
    station = station_index * station_count + channel // COMP
    pick = (jnp.arange(station_mask.shape[1], dtype=jnp.int32)[:, None] == station[None, :]) & (
        channel < channels)[None, :]
    picked = jnp.dot(mask_bf16, pick.astype(jnp.bfloat16), preferred_element_type=jnp.float32)
    event_mask = jnp.broadcast_to(picked[:, :, None], (events, nch, LANES)).reshape(events * nch, LANES)

    partial = correlate(regions, per_block, pair_cap, segment, slots, nch)(
        received, event_mask, slot_event, forward_table(), lag_table())

    share = LAG_ROWS // chans
    swap = [(0, 1), (1, 0)]
    keep = lax.dynamic_slice_in_dim(partial, chan_index * share, share, axis=1)
    give = lax.dynamic_slice_in_dim(partial, (1 - chan_index) * share, share, axis=1)
    keep = keep + lax.ppermute(give, "chan", swap)
    spread = lax.all_to_all(keep.astype(jnp.bfloat16), "region", split_axis=0, concat_axis=0, tiled=True)
    total = jnp.sum(spread.astype(jnp.float32), axis=0)
    count = lax.axis_size("stn")
    step = 1
    whole = total
    while step < count:
        whole = whole + lax.ppermute(whole, "stn", [(i, i ^ step) for i in range(count)])
        step *= 2
    other = lax.ppermute(whole, "chan", swap)
    low = jnp.where(chan_index == 0, whole, other)
    high = jnp.where(chan_index == 0, other, whole)
    full = jnp.concatenate([low, high], axis=0)[:LAGS]
    return full[:, :pair_cap], full[:, pair_cap:]


def solution(mesh):
    placed = (
        P("stn", None, ("groups", "region")),
        P(("groups", "region")),
        P("groups"),
        P("groups", None),
        P(("groups", "region")),
        P(("groups", "region")),
        P(("groups", "region")),
    )
    return jax.shard_map(
        on_device,
        mesh=mesh,
        in_specs=placed,
        out_specs=(P(None, ("groups", "region")), P(None, ("groups", "region"))),
        check_vma=False,
    )
```

```python
import math

import jax
import jax.numpy as jnp
import numpy as np
from jax import lax
from jax.experimental import pallas as pl
from jax.experimental.pallas import tpu as pltpu
from jax.sharding import PartitionSpec as P

COMP = 3
WIN = 400
MAXLAG = 50
NFFT = 512
LAGS = 101
BINS = NFFT // 2
LANES = 128
LAG_ROWS = 112
VMEM_ONLY = pl.BlockSpec(memory_space=pltpu.VMEM)
SMEM_ONLY = pl.BlockSpec(memory_space=pltpu.SMEM)
NT = (((1,), (1,)), ((), ()))
TN = (((0,), (0,)), ((), ()))


def forward_table():
    sample = np.arange(NFFT)[:, None]
    freq = np.arange(BINS)[None, :]
    angle = (sample * freq % NFFT) * (2.0 * math.pi / NFFT)
    sine = np.sin(angle)
    sine[:, 0] = np.cos(math.pi * (np.arange(NFFT) % 2))
    table = np.concatenate([np.cos(angle), sine], axis=1)
    table[WIN:] = 0.0
    return jnp.asarray(table, jnp.float32).astype(jnp.bfloat16)


def lag_table():
    shift = np.arange(LANES)[:, None] - MAXLAG
    freq = np.arange(BINS)[None, :]
    angle = (freq * shift % NFFT) * (2.0 * math.pi / NFFT)
    weight = np.where(freq == 0, 1.0 / NFFT, 2.0 / NFFT)
    even = weight * np.cos(angle)
    odd = -weight * np.sin(angle)
    odd[:, 0] = (np.cos(math.pi * (shift[:, 0] % 2)) - 1.0) / NFFT
    table = np.concatenate([even, odd], axis=1) * math.sqrt(WIN)
    table[LAGS:] = 0.0
    return jnp.asarray(table, jnp.float32).astype(jnp.bfloat16)


def slot_table(event_owner, regions, per_block, bucket, slots):
    blocks = event_owner.reshape(regions, per_block)
    owned = blocks[:, :, None] == jnp.arange(regions, dtype=jnp.int32)[None, None, :]
    onehot = owned.astype(jnp.int32)
    before = jnp.cumsum(onehot, axis=1) - onehot
    ranking = jnp.sum(before * onehot, axis=2)
    block_index = jnp.arange(regions, dtype=jnp.int32)[:, None]
    return (blocks * slots + block_index * bucket + ranking).reshape(-1)


def as_bf16(flags):
    return flags.astype(jnp.float32).astype(jnp.bfloat16)


def digits_of(value):
    return (value >> 7).astype(jnp.float32).astype(jnp.bfloat16), (value & 127).astype(jnp.float32).astype(jnp.bfloat16)


def station_share(stations, chans):
    return -(-stations // chans)


def pack(archive, starts, station_mask, pair_first, pair_second, pair_count, regions, chans, nch):
    stations, _, segment = archive.shape
    events, listed = station_mask.shape
    per_block = starts.shape[1]
    pair_cap = pair_first.shape[1]
    share = station_share(stations, chans)
    total = regions * nch

    def kernel(archive, starts, mask, first, second, count, out, flat):
        chan = lax.axis_index("chan")
        base = jnp.minimum(chan * share, stations - share)
        flat[pl.ds(total - nch, nch), :] = jnp.zeros((nch, segment), jnp.float32)
        for station in range(share):
            flat[pl.ds(station * COMP, COMP), :] = archive[base + station].astype(jnp.float32)
        if share * COMP < total - nch:
            flat[share * COMP : total - nch, :] = jnp.zeros((total - nch - share * COMP, segment), jnp.float32)
        names = lax.broadcasted_iota(jnp.int32, (events, pair_cap), 0)
        usable = mask[...].astype(jnp.float32).astype(jnp.bfloat16)
        chosen = [lax.dot_general(usable, as_bf16(names == ref[...]), TN, preferred_element_type=jnp.float32)
                  for ref in (first, second)]
        common = jnp.sum(chosen[0] * chosen[1], axis=0, keepdims=True)
        position = lax.broadcasted_iota(jnp.int32, (1, pair_cap), 1)
        code = jnp.where(position < count[0], common + 1.0, 0.0).astype(jnp.bfloat16)
        offset = digits_of(starts[...] - lax.axis_index("region") * segment)
        rows = digits_of(first[...]) + digits_of(second[...])
        for part in range(regions):
            out[part, :, :segment] = flat[pl.ds(part * nch, nch), :].astype(jnp.bfloat16)
            for k in range(4):
                out[part, k : k + 1, segment : segment + pair_cap] = rows[k]
            out[part, 0:1, segment + pair_cap :] = code
            out[part, 1:2, segment + pair_cap : segment + pair_cap + per_block] = offset[0]
            out[part, 2:3, segment + pair_cap : segment + pair_cap + per_block] = offset[1]

    return pl.pallas_call(
        kernel,
        out_shape=jax.ShapeDtypeStruct((regions, nch, segment + 2 * pair_cap), jnp.bfloat16),
        in_specs=[VMEM_ONLY] * 5 + [SMEM_ONLY],
        out_specs=VMEM_ONLY,
        scratch_shapes=[pltpu.VMEM((total, segment), jnp.float32)],
        name="pack",
    )(archive, starts, station_mask, pair_first, pair_second, pair_count)


def correlate(regions, per_block, pair_cap, segment, slots, nch):
    rows = 2 * nch
    tiles = segment // LANES + 2
    events = regions * per_block
    half = 2 * LANES
    cols = pair_cap // LANES
    per_row = min(per_block, LANES)
    share = LAG_ROWS // 2

    def kernel(recv, mask, station, slot_of, table, weights, kept, given, shifted, windows, spec, prod, weight_rows,
               index_vmem, index, whole, profile, sem):
        for part in range(regions):
            digits = recv[part, :, segment:].astype(jnp.float32)
            for k in range(2):
                event = (digits[2 * k : 2 * k + 1, :pair_cap] * 128.0 + digits[2 * k + 1 : 2 * k + 2, :pair_cap])
                event = event.astype(jnp.int32) * rows
                for c in range(cols):
                    row = k * cols + c
                    index_vmem[part, row : row + 1, :] = event[:, c * LANES : (c + 1) * LANES]
            for k in range(2):
                row = 2 * cols + k
                digit = digits[k + 1 : k + 2, pair_cap : pair_cap + LANES]
                index_vmem[part, row : row + 1, :] = digit.astype(jnp.int32)
        copy = pltpu.make_async_copy(index_vmem, index, sem)
        copy.start()

        def widen(part, carry):
            for k in range(tiles + 2):
                data = recv[part, :, k * LANES : (k + 1) * LANES].astype(jnp.float32)
                if k < tiles:
                    shifted[part, k, pl.ds(0, nch, stride=2), :] = data
                if k >= 2:
                    shifted[part, k - 2, pl.ds(1, nch, stride=2), :] = data
            return carry

        lax.fori_loop(0, regions, widen, 0)

        listed = lax.broadcasted_iota(jnp.int32, (mask.shape[1], LANES), 0)
        usable = mask[...].astype(jnp.float32).astype(jnp.bfloat16)
        for c in range(nch):
            weight_rows[pl.ds(c, events, stride=nch), :] = jnp.dot(
                usable, as_bf16(listed == station[c]), preferred_element_type=jnp.float32)
        copy.wait()

        lane = lax.broadcasted_iota(jnp.int32, (rows, LANES), 1)
        sublane = lax.broadcasted_iota(jnp.int32, (rows, LANES), 0)
        count = per_block * nch
        inside = lax.broadcasted_iota(jnp.int32, (count, LANES), 1) < WIN - half - LANES

        def one_segment(part, carry):
            def some_events(group, inner):
                for step in range(per_row):
                    base = index[part, 2 * cols, group * per_row + step]
                    off = index[part, 2 * cols + 1, group * per_row + step]
                    turn = (LANES - off) & (LANES - 1)
                    data = [shifted[part, base + k] for k in range(3)]
                    later = lane >= off
                    row = pl.multiple_of((group * per_row + step) * rows, rows)
                    windows[0, pl.ds(row, rows), :] = pltpu.roll(jnp.where(later, data[0], data[1]), turn, 1)
                    windows[1, pl.ds(row, rows), :] = pltpu.roll(jnp.where(later, data[1], data[2]), turn, 1)
                return inner

            if per_block == per_row:
                some_events(0, 0)
            else:
                lax.fori_loop(0, per_block // per_row, some_events, 0)
            pieces = [[windows[t, pl.ds(k, count, stride=2), :] for t in range(2)] for k in range(2)]
            squares = pieces[0][0] * pieces[0][0] + pieces[0][1] * pieces[0][1] + pieces[1][0] * pieces[1][0]
            squares += jnp.where(inside, pieces[1][1] * pieces[1][1], 0.0)
            energy = jnp.sum(squares, axis=1, keepdims=True)
            early, late = (jnp.concatenate(piece, axis=1).astype(jnp.bfloat16) for piece in pieces)
            coefs = jnp.dot(early, table[:half, :], preferred_element_type=jnp.float32)
            coefs += jnp.dot(late, table[half:, :], preferred_element_type=jnp.float32)
            place = pl.multiple_of(part * count, count)
            factor = weight_rows[pl.ds(place, count), :] * lax.rsqrt(energy + WIN * 1e-05)
            for s in range(2):
                for k in range(2):
                    column = s * BINS + k * LANES
                    piece = (coefs[:, column : column + LANES] * factor).astype(jnp.bfloat16)
                    spec[s, pl.ds(2 * place + k, count, stride=2), :] = piece.astype(jnp.float32)
            return carry

        lax.fori_loop(0, regions, one_segment, 0)

        special = (sublane % 2 == 0) & (lane == 0)
        upper = sublane < nch
        profile[...] = jnp.zeros_like(profile)
        names = lax.broadcasted_iota(jnp.int32, (events, LANES), 0) + 1
        name_digits = digits_of(names)
        slot_lane = slot_of[...]
        place_of = lax.broadcasted_iota(jnp.int32, (slots, events), 0)

        def names_in(part):
            hit = as_bf16(place_of + part * slots == slot_lane)
            high, low = (jnp.dot(hit, digit, preferred_element_type=jnp.float32) for digit in name_digits)
            return high * 128.0 + low - 1.0

        def one_region(part, carry):
            def some_pairs(row, inner):
                for step in range(LANES):
                    a = pl.multiple_of(index[part, row, step], rows)
                    b = pl.multiple_of(index[part, cols + row, step], rows)
                    cos_a, sin_a = spec[0, pl.ds(a, rows), :], spec[1, pl.ds(a, rows), :]
                    cos_b, sin_b = spec[0, pl.ds(b, rows), :], spec[1, pl.ds(b, rows), :]
                    sines = sin_a * sin_b
                    even = cos_a * cos_b + sines
                    odd = jnp.where(special, sines, sin_a * cos_b - cos_a * sin_b)
                    even += pltpu.roll(even, nch, 0)
                    odd += pltpu.roll(odd, nch, 0)
                    both = jnp.where(upper, even, odd)
                    place = pl.multiple_of((row * LANES + step) * rows, rows)
                    prod[pl.ds(place, rows), :] = both + pltpu.roll(both, rows - 2, 0)
                return inner

            lax.fori_loop(0, cols, some_pairs, 0)
            sums = [prod[pl.ds(k, pair_cap, stride=rows), :] for k in (0, 1, nch, nch + 1)]
            sums = jnp.concatenate(sums, axis=1).astype(jnp.bfloat16)
            cross = lax.dot_general(weights[...], sums, NT, preferred_element_type=jnp.float32)
            digits = recv[part, :, segment:].astype(jnp.float32)
            code = digits[0:1, pair_cap:]
            live = jnp.maximum((code - 1.0) * COMP, 1.0)
            stack = cross * jnp.where(code > 0.0, lax.rsqrt(live), 0.0)
            whole[part, :, :pair_cap] = stack[:LAG_ROWS]
            first = digits[0:1, :pair_cap] * 128.0 + digits[1:2, :pair_cap]
            second = digits[2:3, :pair_cap] * 128.0 + digits[3:4, :pair_cap]
            stack = stack.astype(jnp.bfloat16)

            def gathered(column, event):
                hot = as_bf16(jnp.concatenate([column] * cols, axis=1) == event)
                return lax.dot_general(stack, hot, NT, preferred_element_type=jnp.float32)

            own = names_in(part)
            profile[0, part] += gathered(own, first)
            profile[1, part] += gathered(own, second)

            @pl.when(part + 1 < regions)
            def _():
                profile[1, part + 1] += gathered(names_in(part + 1), second)
            return carry

        lax.fori_loop(0, regions, one_region, 0)
        mirror = as_bf16(lax.broadcasted_iota(jnp.int32, (LANES, LANES), 0) + lax.broadcasted_iota(
            jnp.int32, (LANES, LANES), 1) == LAGS - 1)
        chan = lax.axis_index("chan")
        mine = pl.multiple_of(chan * share, 8)
        theirs = pl.multiple_of((1 - chan) * share, 8)

        def finish(part, carry):
            value = profile[1, part]
            high = value.astype(jnp.bfloat16)
            low = (value - high.astype(jnp.float32)).astype(jnp.bfloat16)
            flipped = jnp.dot(mirror, high, preferred_element_type=jnp.float32) + jnp.dot(
                mirror, low, preferred_element_type=jnp.float32)
            whole[part, :, pair_cap:] = (profile[0, part] + flipped)[:LAG_ROWS]
            kept[part] = whole[part, pl.ds(mine, share), :]
            given[part] = whole[part, pl.ds(theirs, share), :].astype(jnp.bfloat16)
            return carry

        lax.fori_loop(0, regions, finish, 0)

    shape = (regions, share, pair_cap + slots)
    index_rows = 8 * -(-(2 * cols + 2) // 8)
    return pl.pallas_call(
        kernel,
        out_shape=(jax.ShapeDtypeStruct(shape, jnp.float32), jax.ShapeDtypeStruct(shape, jnp.bfloat16)),
        in_specs=[VMEM_ONLY, VMEM_ONLY, SMEM_ONLY] + [VMEM_ONLY] * 3,
        out_specs=(VMEM_ONLY, VMEM_ONLY),
        scratch_shapes=[
            pltpu.VMEM((regions, tiles, rows, LANES), jnp.float32),
            pltpu.VMEM((2, per_block * rows, LANES), jnp.float32),
            pltpu.VMEM((2, events * rows, LANES), jnp.float32),
            pltpu.VMEM((pair_cap * rows, LANES), jnp.float32),
            pltpu.VMEM((events * nch, LANES), jnp.float32),
            pltpu.VMEM((regions, index_rows, LANES), jnp.int32),
            pltpu.SMEM((regions, index_rows, LANES), jnp.int32),
            pltpu.VMEM((regions, LAG_ROWS, pair_cap + slots), jnp.float32),
            pltpu.VMEM((2, regions, LANES, slots), jnp.float32),
            pltpu.SemaphoreType.DMA(()),
        ],
        name="correlate",
    )


def on_device(archive, starts, event_owner, station_mask, pair_first, pair_second, pair_count):
    regions = lax.axis_size("region")
    chans = lax.axis_size("chan")
    chan_index = lax.axis_index("chan")
    per_block = starts.shape[0]
    pair_cap = pair_first.shape[0]
    stations = archive.shape[0]
    segment = archive.shape[2]
    bucket = max(2, 2 * per_block // regions)
    slots = regions * bucket
    share = station_share(stations, chans)
    nch = 4 * -(-share * COMP // (4 * regions))

    payload = pack(archive, starts.reshape(1, -1), station_mask, pair_first.reshape(1, -1),
                   pair_second.reshape(1, -1), pair_count, regions, chans, nch)
    received = lax.all_to_all(payload, "region", split_axis=0, concat_axis=0, tiled=True)

    slot_of = slot_table(event_owner, regions, per_block, bucket, slots).reshape(1, -1)
    channel = lax.axis_index("region") * nch + jnp.arange(nch, dtype=jnp.int32)
    local = jnp.minimum(chan_index * share, stations - share) + channel // COMP
    used = (channel < share * COMP) & (local >= chan_index * share)
    station = jnp.where(used, lax.axis_index("stn") * stations + local, -1)

    kept, given = correlate(regions, per_block, pair_cap, segment, slots, nch)(
        received, station_mask, station, slot_of, forward_table(), lag_table())

    swap = [(0, 1), (1, 0)]
    kept = kept + lax.ppermute(given, "chan", swap).astype(jnp.float32)
    spread = lax.all_to_all(kept.astype(jnp.bfloat16), "region", split_axis=0, concat_axis=0, tiled=True)
    whole = jnp.sum(spread.astype(jnp.float32), axis=0)
    count = lax.axis_size("stn")
    step = 1
    while step < count:
        sent = whole.astype(jnp.bfloat16)
        other = lax.ppermute(sent, "stn", [(i, i ^ step) for i in range(count)])
        whole = sent.astype(jnp.float32) + other.astype(jnp.float32)
        step *= 2
    other = lax.ppermute(whole, "chan", swap)
    low = jnp.where(chan_index == 0, whole, other)
    high = jnp.where(chan_index == 0, other, whole)
    full = jnp.concatenate([low, high], axis=0)[:LAGS]
    return full[:, :pair_cap], full[:, pair_cap:]


def solution(mesh):
    placed = (
        P("stn", None, ("groups", "region")),
        P(("groups", "region")),
        P("groups"),
        P("groups", None),
        P(("groups", "region")),
        P(("groups", "region")),
        P(("groups", "region")),
    )
    return jax.shard_map(
        on_device,
        mesh=mesh,
        in_specs=placed,
        out_specs=(P(None, ("groups", "region")), P(None, ("groups", "region"))),
        check_vma=False,
    )
```

```python
import math

import jax
import jax.numpy as jnp
import numpy as np
from jax import lax
from jax.experimental import pallas as pl
from jax.experimental.pallas import tpu as pltpu
from jax.sharding import PartitionSpec as P

COMP = 3
WIN = 400
MAXLAG = 50
NFFT = 512
LAGS = 101
BINS = NFFT // 2
LANES = 128
LAG_ROWS = 112
VMEM_ONLY = pl.BlockSpec(memory_space=pltpu.VMEM)
SMEM_ONLY = pl.BlockSpec(memory_space=pltpu.SMEM)
NT = (((1,), (1,)), ((), ()))
TN = (((0,), (0,)), ((), ()))


def forward_table():
    sample = np.arange(NFFT)[:, None]
    freq = np.arange(BINS)[None, :]
    angle = (sample * freq % NFFT) * (2.0 * math.pi / NFFT)
    sine = np.sin(angle)
    sine[:, 0] = np.cos(math.pi * (np.arange(NFFT) % 2))
    table = np.concatenate([np.cos(angle), sine], axis=1)
    table[WIN:] = 0.0
    return jnp.asarray(table, jnp.float32).astype(jnp.bfloat16)


def lag_table():
    shift = np.arange(LANES)[:, None] - MAXLAG
    freq = np.arange(BINS)[None, :]
    angle = (freq * shift % NFFT) * (2.0 * math.pi / NFFT)
    weight = np.where(freq == 0, 1.0 / NFFT, 2.0 / NFFT)
    even = weight * np.cos(angle)
    odd = -weight * np.sin(angle)
    odd[:, 0] = (np.cos(math.pi * (shift[:, 0] % 2)) - 1.0) / NFFT
    table = np.concatenate([even, odd], axis=1) * math.sqrt(WIN)
    table[LAGS:] = 0.0
    table = jnp.asarray(table, jnp.float32)
    high = table.astype(jnp.bfloat16)
    return jnp.concatenate([high, (table - high.astype(jnp.float32)).astype(jnp.bfloat16)], axis=0)


def slot_table(event_owner, regions, per_block, bucket, slots):
    blocks = event_owner.reshape(regions, per_block)
    owned = blocks[:, :, None] == jnp.arange(regions, dtype=jnp.int32)[None, None, :]
    onehot = owned.astype(jnp.int32)
    before = jnp.cumsum(onehot, axis=1) - onehot
    ranking = jnp.sum(before * onehot, axis=2)
    block_index = jnp.arange(regions, dtype=jnp.int32)[:, None]
    return (blocks * slots + block_index * bucket + ranking).reshape(-1)


def as_bf16(flags):
    return flags.astype(jnp.float32).astype(jnp.bfloat16)


def digits_of(value):
    return (value >> 7).astype(jnp.float32).astype(jnp.bfloat16), (value & 127).astype(jnp.float32).astype(jnp.bfloat16)


def station_share(stations, chans):
    return -(-stations // chans)


def pack(archive, starts, station_mask, pair_first, pair_second, pair_count, regions, chans, nch):
    stations, _, segment = archive.shape
    events = station_mask.shape[1]
    per_block = starts.shape[1]
    pair_cap = pair_first.shape[1]
    share = station_share(stations, chans)
    total = regions * nch

    def kernel(archive, starts, mask, first, second, count, out, flat):
        chan = lax.axis_index("chan")
        base = jnp.minimum(chan * share, stations - share)
        flat[pl.ds(total - nch, nch), :] = jnp.zeros((nch, segment), jnp.float32)
        for station in range(share):
            flat[pl.ds(station * COMP, COMP), :] = archive[base + station].astype(jnp.float32)
        if share * COMP < total - nch:
            flat[share * COMP : total - nch, :] = jnp.zeros((total - nch - share * COMP, segment), jnp.float32)
        names = lax.broadcasted_iota(jnp.int32, (events, pair_cap), 0)
        usable = mask[...].astype(jnp.float32).astype(jnp.bfloat16)
        chosen = [jnp.dot(usable, as_bf16(names == ref[...]), preferred_element_type=jnp.float32)
                  for ref in (first, second)]
        common = jnp.sum(chosen[0] * chosen[1], axis=0, keepdims=True)
        position = lax.broadcasted_iota(jnp.int32, (1, pair_cap), 1)
        code = jnp.where(position < count[0], common + 1.0, 0.0).astype(jnp.bfloat16)
        offset = digits_of(starts[...] - lax.axis_index("region") * segment)
        rows = digits_of(first[...]) + digits_of(second[...])
        for part in range(regions):
            out[part, :, :segment] = flat[pl.ds(part * nch, nch), :].astype(jnp.bfloat16)
            for k in range(4):
                out[part, k : k + 1, segment : segment + pair_cap] = rows[k]
            out[part, 0:1, segment + pair_cap :] = code
            out[part, 1:2, segment + pair_cap : segment + pair_cap + per_block] = offset[0]
            out[part, 2:3, segment + pair_cap : segment + pair_cap + per_block] = offset[1]

    return pl.pallas_call(
        kernel,
        out_shape=jax.ShapeDtypeStruct((regions, nch, segment + 2 * pair_cap), jnp.bfloat16),
        in_specs=[VMEM_ONLY] * 5 + [SMEM_ONLY],
        out_specs=VMEM_ONLY,
        scratch_shapes=[pltpu.VMEM((total, segment), jnp.float32)],
        compiler_params=pltpu.CompilerParams(
            vmem_limit_bytes=grant((3 * total + 5 * stations) * segment // LANES + events * pair_cap * 2 // LANES)),
        name="pack",
    )(archive, starts, station_mask, pair_first, pair_second, pair_count)


def describe(station_mask, station, slot_of, regions, slots, nch):
    events = station_mask.shape[1]
    per_block = events // regions

    def kernel(mask, station, slot_of, slot_event, weight_rows):
        listed = lax.broadcasted_iota(jnp.int32, (mask.shape[0], LANES), 0)
        usable = mask[...].astype(jnp.float32).astype(jnp.bfloat16)
        for c in range(nch):
            value = lax.dot_general(usable, as_bf16(listed == station[c]), TN, preferred_element_type=jnp.float32)
            for part in range(regions):
                row = (part * nch + c) * per_block
                weight_rows[row : row + per_block, :] = value[part * per_block : (part + 1) * per_block]
        names = digits_of(lax.broadcasted_iota(jnp.int32, (events, LANES), 0) + 1)
        place = lax.broadcasted_iota(jnp.int32, (slots, events), 0)
        slot_lane = slot_of[...]

        def one_region(part, carry):
            hit = as_bf16(place + part * slots == slot_lane)
            high, low = (jnp.dot(hit, digit, preferred_element_type=jnp.float32) for digit in names)
            slot_event[pl.ds(pl.multiple_of(part * slots, slots), slots), :] = high * 128.0 + low - 1.0
            return carry

        lax.fori_loop(0, regions, one_region, 0)

    return pl.pallas_call(
        kernel,
        out_shape=(jax.ShapeDtypeStruct((regions * slots, LANES), jnp.float32),
                   jax.ShapeDtypeStruct((events * nch, LANES), jnp.float32)),
        in_specs=[VMEM_ONLY, SMEM_ONLY, VMEM_ONLY],
        out_specs=(VMEM_ONLY, VMEM_ONLY),
        compiler_params=pltpu.CompilerParams(vmem_limit_bytes=grant(regions * slots + 2 * events * nch)),
        name="describe",
    )(station_mask, station, slot_of)


def grant(rows):
    return min(rows * LANES * 4 * 5 // 4 + (4 << 20), 60 * 1024 * 1024)


def correlate(regions, per_block, pair_cap, segment, slots, nch):
    rows = 2 * nch
    tiles = segment // LANES + 2
    events = regions * per_block
    half = 2 * LANES
    cols = pair_cap // LANES
    per_row = min(per_block, LANES)
    share = LAG_ROWS // 2
    batch = regions if regions <= 4 else 1

    def kernel(recv, slot_event, weight_rows, table, weights, kept, given, shifted, windows, spec, prod,
               index_vmem, index, whole, profile, sem):
        for part in range(regions):
            digits = recv[part, :, segment:].astype(jnp.float32)
            for k in range(2):
                event = (digits[2 * k : 2 * k + 1, :pair_cap] * 128.0 + digits[2 * k + 1 : 2 * k + 2, :pair_cap])
                event = event.astype(jnp.int32) * (2 * rows)
                for c in range(cols):
                    row = k * cols + c
                    index_vmem[part, row : row + 1, :] = event[:, c * LANES : (c + 1) * LANES]
            for k in range(2):
                row = 2 * cols + k
                digit = digits[k + 1 : k + 2, pair_cap : pair_cap + LANES]
                index_vmem[part, row : row + 1, :] = digit.astype(jnp.int32)
        copy = pltpu.make_async_copy(index_vmem, index, sem)
        copy.start()

        def widen(part, carry):
            for k in range(tiles + 2):
                data = recv[part, :, k * LANES : (k + 1) * LANES].astype(jnp.float32)
                if k < tiles:
                    shifted[part, k, pl.ds(0, nch, stride=2), :] = data
                if k >= 2:
                    shifted[part, k - 2, pl.ds(1, nch, stride=2), :] = data
            return carry

        lax.fori_loop(0, regions, widen, 0)

        copy.wait()

        lane = lax.broadcasted_iota(jnp.int32, (rows, LANES), 1)
        sublane = lax.broadcasted_iota(jnp.int32, (rows, LANES), 0)
        count = per_block * nch
        inside = lax.broadcasted_iota(jnp.int32, (count, LANES), 1) < WIN - half - LANES

        def one_segment(part, carry):
            def some_events(group, inner):
                for step in range(per_row):
                    base = index[part, 2 * cols, group * per_row + step]
                    off = index[part, 2 * cols + 1, group * per_row + step]
                    turn = (LANES - off) & (LANES - 1)
                    data = [shifted[part, base + k] for k in range(3)]
                    later = lane >= off
                    row = pl.multiple_of((group * per_row + step) * rows, rows)
                    windows[0, pl.ds(row, rows), :] = pltpu.roll(jnp.where(later, data[0], data[1]), turn, 1)
                    windows[1, pl.ds(row, rows), :] = pltpu.roll(jnp.where(later, data[1], data[2]), turn, 1)
                return inner

            if per_block == per_row:
                some_events(0, 0)
            else:
                lax.fori_loop(0, per_block // per_row, some_events, 0)
            pieces = [[jnp.concatenate([windows[t, pl.ds(2 * c + k, per_block, stride=rows), :] for c in range(nch)])
                       for t in range(2)] for k in range(2)]
            squares = pieces[0][0] * pieces[0][0] + pieces[0][1] * pieces[0][1] + pieces[1][0] * pieces[1][0]
            squares += jnp.where(inside, pieces[1][1] * pieces[1][1], 0.0)
            energy = jnp.sum(squares, axis=1, keepdims=True)
            early, late = (jnp.concatenate(piece, axis=1).astype(jnp.bfloat16) for piece in pieces)
            coefs = jnp.dot(early, table[:half, :], preferred_element_type=jnp.float32)
            coefs += jnp.dot(late, table[half:, :], preferred_element_type=jnp.float32)
            place = pl.multiple_of(part * count, count)
            factor = weight_rows[pl.ds(place, count), :] * lax.rsqrt(energy + WIN * 1e-05)
            for s in range(2):
                for k in range(2):
                    column = s * BINS + k * LANES
                    piece = (coefs[:, column : column + LANES] * factor).astype(jnp.bfloat16).astype(jnp.float32)
                    for c in range(nch):
                        row = 2 * rows * per_block * part + s * rows + 2 * c + k
                        spec[pl.ds(row, per_block, stride=2 * rows), :] = piece[c * per_block : (c + 1) * per_block]
            return carry

        lax.fori_loop(0, regions, one_segment, 0)

        special = (sublane % 2 == 0) & (lane == 0)
        upper = sublane < nch
        profile[...] = jnp.zeros_like(profile)

        def one_group(group, carry):
            def some_pairs(line, inner):
                part = group * batch + line // cols
                row = line % cols
                for step in range(LANES):
                    a = pl.multiple_of(index[part, row, step], 2 * rows)
                    b = pl.multiple_of(index[part, cols + row, step], 2 * rows)
                    cos_a, sin_a = spec[pl.ds(a, rows), :], spec[pl.ds(a + rows, rows), :]
                    cos_b, sin_b = spec[pl.ds(b, rows), :], spec[pl.ds(b + rows, rows), :]
                    sines = sin_a * sin_b
                    even = cos_a * cos_b + sines
                    odd = jnp.where(special, sines, sin_a * cos_b - cos_a * sin_b)
                    even += pltpu.roll(even, nch, 0)
                    odd += pltpu.roll(odd, nch, 0)
                    place = pl.multiple_of((line * LANES + step) * rows, rows)
                    prod[pl.ds(place, rows), :] = jnp.where(upper, even, odd)
                return inner

            lax.fori_loop(0, batch * cols, some_pairs, 0)
            for member in range(batch):
                part = group * batch + member
                first_row = member * pair_cap * rows
                sums = []
                for k in (0, 1, nch, nch + 1):
                    total = prod[pl.ds(first_row + k, pair_cap, stride=rows), :]
                    for c in range(1, nch // 2):
                        total += prod[pl.ds(first_row + k + 2 * c, pair_cap, stride=rows), :]
                    sums.append(total.astype(jnp.bfloat16))
                both = lax.dot_general(weights[...], jnp.concatenate(sums, axis=1), NT,
                                       preferred_element_type=jnp.float32)
                cross = both[:LANES] + both[LANES:]
                digits = recv[part, :, segment:].astype(jnp.float32)
                code = digits[0:1, pair_cap:]
                live = jnp.maximum((code - 1.0) * COMP, 1.0)
                stack = cross * jnp.where(code > 0.0, lax.rsqrt(live), 0.0)
                whole[part, :, :pair_cap] = stack[:LAG_ROWS]
                first = digits[0:1, :pair_cap] * 128.0 + digits[1:2, :pair_cap]
                second = digits[2:3, :pair_cap] * 128.0 + digits[3:4, :pair_cap]
                stack = stack.astype(jnp.bfloat16)

                def gathered(owner, event):
                    column = slot_event[pl.ds(pl.multiple_of(owner * slots, slots), slots), :]
                    hot = as_bf16(jnp.concatenate([column] * cols, axis=1) == event)
                    return lax.dot_general(stack, hot, NT, preferred_element_type=jnp.float32)

                profile[0, part] += gathered(part, first)
                profile[1, part] += gathered(part, second)
                after = (part + 1) % regions
                profile[1, after] += gathered(after, second)
            return carry

        lax.fori_loop(0, regions // batch, one_group, 0)
        mirror = as_bf16(lax.broadcasted_iota(jnp.int32, (LANES, LANES), 0) + lax.broadcasted_iota(
            jnp.int32, (LANES, LANES), 1) == LAGS - 1)
        chan = lax.axis_index("chan")
        mine = pl.multiple_of(chan * share, 8)
        theirs = pl.multiple_of((1 - chan) * share, 8)

        def finish(part, carry):
            value = profile[1, part]
            high = value.astype(jnp.bfloat16)
            low = (value - high.astype(jnp.float32)).astype(jnp.bfloat16)
            flipped = jnp.dot(mirror, high, preferred_element_type=jnp.float32) + jnp.dot(
                mirror, low, preferred_element_type=jnp.float32)
            whole[part, :, pair_cap:] = (profile[0, part] + flipped)[:LAG_ROWS]
            kept[part] = whole[part, pl.ds(mine, share), :]
            given[part] = whole[part, pl.ds(theirs, share), :].astype(jnp.bfloat16)
            return carry

        lax.fori_loop(0, regions, finish, 0)

    shape = (regions, share, pair_cap + slots)
    index_rows = 8 * -(-(2 * cols + 2) // 8)
    width = (pair_cap + slots) // LANES
    used = regions * (tiles * rows + 2 * LAG_ROWS * width + 2 * LANES + index_rows + 4 * tiles + slots)
    used += (2 * per_block + 2 * events + batch * pair_cap) * rows + events * nch + 2 * NFFT
    return pl.pallas_call(
        kernel,
        out_shape=(jax.ShapeDtypeStruct(shape, jnp.float32), jax.ShapeDtypeStruct(shape, jnp.bfloat16)),
        in_specs=[VMEM_ONLY] * 5,
        out_specs=(VMEM_ONLY, VMEM_ONLY),
        scratch_shapes=[
            pltpu.VMEM((regions, tiles, rows, LANES), jnp.float32),
            pltpu.VMEM((2, per_block * rows, LANES), jnp.float32),
            pltpu.VMEM((2 * events * rows, LANES), jnp.float32),
            pltpu.VMEM((batch * pair_cap * rows, LANES), jnp.float32),
            pltpu.VMEM((regions, index_rows, LANES), jnp.int32),
            pltpu.SMEM((regions, index_rows, LANES), jnp.int32),
            pltpu.VMEM((regions, LAG_ROWS, pair_cap + slots), jnp.float32),
            pltpu.VMEM((2, regions, LANES, slots), jnp.float32),
            pltpu.SemaphoreType.DMA(()),
        ],
        compiler_params=pltpu.CompilerParams(vmem_limit_bytes=grant(used)),
        name="correlate",
    )


def on_device(archive, starts, event_owner, station_mask, pair_first, pair_second, pair_count):
    regions = lax.axis_size("region")
    chans = lax.axis_size("chan")
    chan_index = lax.axis_index("chan")
    per_block = starts.shape[0]
    pair_cap = pair_first.shape[0]
    stations = archive.shape[0]
    segment = archive.shape[2]
    bucket = max(2, 2 * per_block // regions)
    slots = regions * bucket
    share = station_share(stations, chans)
    nch = 4 * -(-share * COMP // (4 * regions))

    mask = station_mask.T
    payload = pack(archive, starts.reshape(1, -1), mask, pair_first.reshape(1, -1),
                   pair_second.reshape(1, -1), pair_count, regions, chans, nch)
    received = lax.all_to_all(payload, "region", split_axis=0, concat_axis=0, tiled=True)

    slot_of = slot_table(event_owner, regions, per_block, bucket, slots).reshape(1, -1)
    channel = lax.axis_index("region") * nch + jnp.arange(nch, dtype=jnp.int32)
    local = jnp.minimum(chan_index * share, stations - share) + channel // COMP
    used = (channel < share * COMP) & (local >= chan_index * share)
    station = jnp.where(used, lax.axis_index("stn") * stations + local, -1)

    slot_event, weight_rows = describe(mask, station, slot_of, regions, slots, nch)
    kept, given = correlate(regions, per_block, pair_cap, segment, slots, nch)(
        received, slot_event, weight_rows, forward_table(), lag_table())

    swap = [(0, 1), (1, 0)]
    kept = kept + lax.ppermute(given, "chan", swap).astype(jnp.float32)
    spread = lax.all_to_all(kept.astype(jnp.bfloat16), "region", split_axis=0, concat_axis=0, tiled=True)
    whole = jnp.sum(spread.astype(jnp.float32), axis=0)
    count = lax.axis_size("stn")
    step = 1
    while step < count:
        sent = whole.astype(jnp.bfloat16)
        other = lax.ppermute(sent, "stn", [(i, i ^ step) for i in range(count)])
        whole = sent.astype(jnp.float32) + other.astype(jnp.float32)
        step *= 2
    other = lax.ppermute(whole, "chan", swap)
    low = jnp.where(chan_index == 0, whole, other)
    high = jnp.where(chan_index == 0, other, whole)
    full = jnp.concatenate([low, high], axis=0)[:LAGS]
    return full[:, :pair_cap], full[:, pair_cap:]


def solution(mesh):
    placed = (
        P("stn", None, ("groups", "region")),
        P(("groups", "region")),
        P("groups"),
        P("groups", None),
        P(("groups", "region")),
        P(("groups", "region")),
        P(("groups", "region")),
    )
    return jax.shard_map(
        on_device,
        mesh=mesh,
        in_specs=placed,
        out_specs=(P(None, ("groups", "region")), P(None, ("groups", "region"))),
        check_vma=False,
    )
```

```python
import math

import jax
import jax.numpy as jnp
import numpy as np
from jax import lax
from jax.experimental import pallas as pl
from jax.experimental.pallas import tpu as pltpu
from jax.sharding import PartitionSpec as P

COMP = 3
WIN = 400
MAXLAG = 50
NFFT = 512
LAGS = 101
BINS = NFFT // 2
LANES = 128
LAG_ROWS = 112
HALF_ROWS = LAG_ROWS // 2
VMEM_ONLY = pl.BlockSpec(memory_space=pltpu.VMEM)
SMEM_ONLY = pl.BlockSpec(memory_space=pltpu.SMEM)
NT = (((1,), (1,)), ((), ()))
TN = (((0,), (0,)), ((), ()))


def forward_table():
    sample = np.arange(NFFT)[:, None]
    freq = np.arange(BINS)[None, :]
    angle = (sample * freq % NFFT) * (2.0 * math.pi / NFFT)
    sine = np.sin(angle)
    sine[:, 0] = np.cos(math.pi * (np.arange(NFFT) % 2))
    table = np.concatenate([np.cos(angle), sine], axis=1)
    table[WIN:] = 0.0
    return jnp.asarray(table, jnp.float32).astype(jnp.bfloat16)


def lag_table():
    shift = np.arange(LAG_ROWS)[:, None] - MAXLAG
    freq = np.arange(BINS)[None, :]
    angle = (freq * shift % NFFT) * (2.0 * math.pi / NFFT)
    weight = np.where(freq == 0, 1.0 / NFFT, 2.0 / NFFT)
    even = weight * np.cos(angle)
    odd = -weight * np.sin(angle)
    odd[:, 0] = (np.cos(math.pi * (shift[:, 0] % 2)) - 1.0) / NFFT
    table = np.concatenate([even, odd], axis=1) * math.sqrt(WIN)
    table[LAGS:] = 0.0
    filler = np.zeros((LANES - LAG_ROWS, NFFT))
    halves = table[:HALF_ROWS], table[HALF_ROWS:]
    table = np.stack([np.concatenate([halves[c], halves[1 - c], filler]) for c in range(2)])
    table = jnp.asarray(table, jnp.float32)
    high = table.astype(jnp.bfloat16)
    return jnp.concatenate([high, (table - high.astype(jnp.float32)).astype(jnp.bfloat16)], axis=1)


def slot_table(event_owner, regions, per_block, bucket, slots):
    blocks = event_owner.reshape(regions, per_block)
    owned = blocks[:, :, None] == jnp.arange(regions, dtype=jnp.int32)[None, None, :]
    onehot = owned.astype(jnp.int32)
    before = jnp.cumsum(onehot, axis=1) - onehot
    ranking = jnp.sum(before * onehot, axis=2)
    block_index = jnp.arange(regions, dtype=jnp.int32)[:, None]
    return (blocks * slots + block_index * bucket + ranking).reshape(-1)


def as_bf16(flags):
    return flags.astype(jnp.float32).astype(jnp.bfloat16)


def digits_of(value):
    return (value >> 7).astype(jnp.float32).astype(jnp.bfloat16), (value & 127).astype(jnp.float32).astype(jnp.bfloat16)


def digit_count(events):
    return 1 if events <= 256 else 2


def field_width(events, pair_cap):
    return -(-(2 * digit_count(events) + 2) // 4) * pair_cap


def station_share(stations, chans):
    return -(-stations // chans)


def pack(archive, starts, station_mask, pair_first, pair_second, pair_count, regions, chans, nch):
    stations, _, segment = archive.shape
    events = station_mask.shape[1]
    per_block = starts.shape[1]
    pair_cap = pair_first.shape[1]
    share = station_share(stations, chans)
    total = regions * nch

    def kernel(archive, starts, mask, first, second, count, out, flat):
        chan = lax.axis_index("chan")
        base = jnp.minimum(chan * share, stations - share)
        flat[pl.ds(total - nch, nch), :] = jnp.zeros((nch, segment), jnp.float32)
        for station in range(share):
            flat[pl.ds(station * COMP, COMP), :] = archive[base + station].astype(jnp.float32)
        if share * COMP < total - nch:
            flat[share * COMP : total - nch, :] = jnp.zeros((total - nch - share * COMP, segment), jnp.float32)
        names = lax.broadcasted_iota(jnp.int32, (events, pair_cap), 0)
        usable = mask[...].astype(jnp.float32).astype(jnp.bfloat16)
        chosen = [jnp.dot(usable, as_bf16(names == ref[...]), preferred_element_type=jnp.float32)
                  for ref in (first, second)]
        common = jnp.sum(chosen[0] * chosen[1], axis=0, keepdims=True)
        position = lax.broadcasted_iota(jnp.int32, (1, pair_cap), 1)
        code = jnp.where(position < count[0], common + 1.0, 0.0).astype(jnp.bfloat16)
        offset = digits_of(starts[...] - lax.axis_index("region") * segment)
        used = [jnp.full((1, per_block), digit, jnp.int32) for digit in (count[0] >> 7, count[0] & 127)]
        used = [digit.astype(jnp.float32).astype(jnp.bfloat16) for digit in used]
        rest = jnp.zeros((1, pair_cap - 4 * per_block), jnp.bfloat16)
        scalars = jnp.concatenate(list(offset) + used + [rest], axis=1)
        if digit_count(events) == 1:
            fields = [first[...].astype(jnp.float32).astype(jnp.bfloat16), second[...].astype(jnp.float32).astype(jnp.bfloat16)]
        else:
            fields = list(digits_of(first[...]) + digits_of(second[...]))
        fields += [code, scalars]
        for part in range(regions):
            out[part, :, :segment] = flat[pl.ds(part * nch, nch), :].astype(jnp.bfloat16)
            for k, field in enumerate(fields):
                lane = segment + k // 4 * pair_cap
                out[part, k % 4 : k % 4 + 1, lane : lane + pair_cap] = field

    return pl.pallas_call(
        kernel,
        out_shape=jax.ShapeDtypeStruct((regions, nch, segment + field_width(events, pair_cap)), jnp.bfloat16),
        in_specs=[VMEM_ONLY] * 5 + [SMEM_ONLY],
        out_specs=VMEM_ONLY,
        scratch_shapes=[pltpu.VMEM((total, segment), jnp.float32)],
        name="pack",
    )(archive, starts, station_mask, pair_first, pair_second, pair_count)


def describe(station_mask, station, slot_of, regions, slots, nch):
    events = station_mask.shape[1]
    per_block = events // regions

    def kernel(mask, station, slot_of, slot_event, weight_rows):
        listed = lax.broadcasted_iota(jnp.int32, (mask.shape[0], LANES), 0)
        usable = mask[...].astype(jnp.float32).astype(jnp.bfloat16)
        for c in range(nch):
            value = lax.dot_general(usable, as_bf16(listed == station[c]), TN, preferred_element_type=jnp.float32)
            for part in range(regions):
                row = (part * nch + c) * per_block
                weight_rows[row : row + per_block, :] = value[part * per_block : (part + 1) * per_block]
        names = digits_of(lax.broadcasted_iota(jnp.int32, (events, LANES), 0) + 1)
        place = lax.broadcasted_iota(jnp.int32, (slots, events), 0)
        slot_lane = slot_of[...]

        def one_region(part, carry):
            hit = as_bf16(place + part * slots == slot_lane)
            high, low = (jnp.dot(hit, digit, preferred_element_type=jnp.float32) for digit in names)
            slot_event[pl.ds(pl.multiple_of(part * slots, slots), slots), :] = high * 128.0 + low - 1.0
            return carry

        lax.fori_loop(0, regions, one_region, 0)

    return pl.pallas_call(
        kernel,
        out_shape=(jax.ShapeDtypeStruct((regions * slots, LANES), jnp.float32),
                   jax.ShapeDtypeStruct((events * nch, LANES), jnp.float32)),
        in_specs=[VMEM_ONLY, SMEM_ONLY, VMEM_ONLY],
        out_specs=(VMEM_ONLY, VMEM_ONLY),
        compiler_params=pltpu.CompilerParams(vmem_limit_bytes=grant(regions * slots + 2 * events * nch)),
        name="describe",
    )(station_mask, station, slot_of)


def grant(rows):
    return min(rows * LANES * 4 * 5 // 4 + (4 << 20), 60 * 1024 * 1024)


def correlate(regions, per_block, pair_cap, segment, slots, nch):
    rows = 2 * nch
    tiles = segment // LANES + 2
    events = regions * per_block
    half = 2 * LANES
    cols = pair_cap // LANES
    per_row = min(per_block, LANES)
    batch = regions if regions <= 4 else 1
    digits = digit_count(events)

    def kernel(recv, slot_event, weight_rows, table, weights, kept, given, shifted, windows, spec, prod,
               index_vmem, index, profile, sem):
        def field(part, k):
            lane = segment + k // 4 * pair_cap
            return recv[part, :, lane : lane + pair_cap].astype(jnp.float32)[k % 4 : k % 4 + 1]

        def listed(part, k):
            if digits == 1:
                return field(part, k)
            return field(part, 2 * k) * 128.0 + field(part, 2 * k + 1)

        for part in range(regions):
            rows_out = []
            for k in range(2):
                event = listed(part, k).astype(jnp.int32) * (2 * rows)
                rows_out += [event[:, c * LANES : (c + 1) * LANES] for c in range(cols)]
            scalars = field(part, 2 * digits + 1).astype(jnp.int32)
            rows_out += [scalars[:, c * LANES : (c + 1) * LANES] for c in range(2)]
            for row, value in enumerate(rows_out):
                index_vmem[part, row : row + 1, :] = value
        copy = pltpu.make_async_copy(index_vmem, index, sem)
        copy.start()

        def widen(part, carry):
            for k in range(tiles + 2):
                data = recv[part, :, k * LANES : (k + 1) * LANES].astype(jnp.float32)
                if k < tiles:
                    shifted[part, k, pl.ds(0, nch, stride=2), :] = data
                if k >= 2:
                    shifted[part, k - 2, pl.ds(1, nch, stride=2), :] = data
            return carry

        lax.fori_loop(0, regions, widen, 0)

        copy.wait()

        lane = lax.broadcasted_iota(jnp.int32, (rows, LANES), 1)
        sublane = lax.broadcasted_iota(jnp.int32, (rows, LANES), 0)
        count = per_block * nch
        inside = lax.broadcasted_iota(jnp.int32, (count, LANES), 1) < WIN - half - LANES

        def one_segment(part, slot):
            for event in range(per_block):
                base = index[part, 2 * cols, event]
                off = index[part, 2 * cols, per_block + event]
                turn = (LANES - off) & (LANES - 1)
                data = [shifted[part, base + k] for k in range(3)]
                later = lane >= off
                row = event * rows
                windows[slot, 0, row : row + rows, :] = pltpu.roll(jnp.where(later, data[0], data[1]), turn, 1)
                windows[slot, 1, row : row + rows, :] = pltpu.roll(jnp.where(later, data[1], data[2]), turn, 1)
            pieces = [[jnp.concatenate([windows[slot, t, pl.ds(2 * c + k, per_block, stride=rows), :] for c in range(nch)])
                       for t in range(2)] for k in range(2)]
            squares = pieces[0][0] * pieces[0][0] + pieces[0][1] * pieces[0][1] + pieces[1][0] * pieces[1][0]
            squares += jnp.where(inside, pieces[1][1] * pieces[1][1], 0.0)
            energy = jnp.sum(squares, axis=1, keepdims=True)
            early, late = (jnp.concatenate(piece, axis=1).astype(jnp.bfloat16) for piece in pieces)
            coefs = jnp.dot(early, table[:half, :], preferred_element_type=jnp.float32)
            coefs += jnp.dot(late, table[half:, :], preferred_element_type=jnp.float32)
            place = part * count if batch == regions else pl.multiple_of(part * count, count)
            factor = weight_rows[pl.ds(place, count), :] * lax.rsqrt(energy + WIN * 1e-05)
            for s in range(2):
                for k in range(2):
                    column = s * BINS + k * LANES
                    piece = (coefs[:, column : column + LANES] * factor).astype(jnp.bfloat16).astype(jnp.float32)
                    for c in range(nch):
                        row = 2 * rows * per_block * part + s * rows + 2 * c + k
                        spec[pl.ds(row, per_block, stride=2 * rows), :] = piece[c * per_block : (c + 1) * per_block]

        def looped_segment(part, carry):
            one_segment(part, 0)
            return carry

        if batch == regions:
            for part in range(regions):
                one_segment(part, part)
        else:
            lax.fori_loop(0, regions, looped_segment, 0)

        chan = lax.axis_index("chan")
        special = (sublane % 2 == 0) & (lane == 0)
        upper = sublane < nch
        profile[...] = jnp.zeros_like(profile)

        def one_group(group, carry):
            def some_pairs(member, row):
                part = group * batch + member
                for step in range(LANES):
                    a = pl.multiple_of(index[part, row, step], 2 * rows)
                    b = pl.multiple_of(index[part, cols + row, step], 2 * rows)
                    cos_a, sin_a = spec[pl.ds(a, rows), :], spec[pl.ds(a + rows, rows), :]
                    cos_b, sin_b = spec[pl.ds(b, rows), :], spec[pl.ds(b + rows, rows), :]
                    sines = sin_a * sin_b
                    even = cos_a * cos_b + sines
                    odd = jnp.where(special, sines, sin_a * cos_b - cos_a * sin_b)
                    even += pltpu.roll(even, nch, 0)
                    odd += pltpu.roll(odd, nch, 0)
                    place = pl.multiple_of(((member * cols + row) * LANES + step) * rows, rows)
                    prod[pl.ds(place, rows), :] = jnp.where(upper, even, odd)
                return member

            def pairs_of(member, inner):
                part = group * batch + member
                pairs = index[part, 2 * cols + 1, 0] * LANES + index[part, 2 * cols + 1, per_block]
                lax.fori_loop(0, jnp.minimum((pairs + LANES - 1) // LANES, cols), lambda row, m: some_pairs(m, row),
                              member)
                return inner

            lax.fori_loop(0, batch, pairs_of, 0)
            for member in range(batch):
                part = group * batch + member
                first_row = member * pair_cap * rows
                sums = []
                for k in (0, 1, nch, nch + 1):
                    total = prod[pl.ds(first_row + k, pair_cap, stride=rows), :]
                    for c in range(1, nch // 2):
                        total += prod[pl.ds(first_row + k + 2 * c, pair_cap, stride=rows), :]
                    sums.append(total.astype(jnp.bfloat16))
                both = lax.dot_general(weights[chan], jnp.concatenate(sums, axis=1), NT,
                                       preferred_element_type=jnp.float32)
                cross = both[:LANES] + both[LANES:]
                code = field(part, 2 * digits)
                live = jnp.maximum((code - 1.0) * COMP, 1.0)
                stack = jnp.where(code > 0.0, cross * lax.rsqrt(live), 0.0)
                kept[part, :, :pair_cap] = stack[:HALF_ROWS]
                given[part, :, :pair_cap] = stack[HALF_ROWS:LAG_ROWS].astype(jnp.bfloat16)
                first, second = listed(part, 0), listed(part, 1)
                stack = stack.astype(jnp.bfloat16)

                def gathered(owner, event):
                    column = slot_event[pl.ds(pl.multiple_of(owner * slots, slots), slots), :]
                    hot = as_bf16(jnp.concatenate([column] * cols, axis=1) == event)
                    return lax.dot_general(stack, hot, NT, preferred_element_type=jnp.float32)

                profile[0, part] += gathered(part, first)
                profile[1, part] += gathered(part, second)
                after = (part + 1) % regions
                profile[1, after] += gathered(after, second)
            return carry

        lax.fori_loop(0, regions // batch, one_group, 0)
        def lag_of(axis):
            row = lax.broadcasted_iota(jnp.int32, (LANES, LANES), axis)
            return jnp.where(row < HALF_ROWS, row + chan * HALF_ROWS, row - chan * HALF_ROWS)

        mirror = as_bf16(lag_of(0) + lag_of(1) == LAGS - 1)

        def finish(part, carry):
            value = profile[1, part]
            high = value.astype(jnp.bfloat16)
            low = (value - high.astype(jnp.float32)).astype(jnp.bfloat16)
            flipped = jnp.dot(mirror, high, preferred_element_type=jnp.float32) + jnp.dot(
                mirror, low, preferred_element_type=jnp.float32)
            total = profile[0, part] + flipped
            kept[part, :, pair_cap:] = total[:HALF_ROWS]
            given[part, :, pair_cap:] = total[HALF_ROWS:LAG_ROWS].astype(jnp.bfloat16)
            return carry

        lax.fori_loop(0, regions, finish, 0)

    shape = (regions, HALF_ROWS, pair_cap + slots)
    index_rows = 8 * -(-(2 * cols + 2) // 8)
    width = (pair_cap + slots) // LANES
    used = regions * (tiles * rows + LAG_ROWS * width + 2 * LANES + index_rows + 4 * tiles + slots)
    used += (2 * per_block * batch + 2 * events + batch * pair_cap) * rows + events * nch + 3 * NFFT
    return pl.pallas_call(
        kernel,
        out_shape=(jax.ShapeDtypeStruct(shape, jnp.float32), jax.ShapeDtypeStruct(shape, jnp.bfloat16)),
        in_specs=[VMEM_ONLY] * 5,
        out_specs=(VMEM_ONLY, VMEM_ONLY),
        scratch_shapes=[
            pltpu.VMEM((regions, tiles, rows, LANES), jnp.float32),
            pltpu.VMEM((batch, 2, per_block * rows, LANES), jnp.float32),
            pltpu.VMEM((2 * events * rows, LANES), jnp.float32),
            pltpu.VMEM((batch * pair_cap * rows, LANES), jnp.float32),
            pltpu.VMEM((regions, index_rows, LANES), jnp.int32),
            pltpu.SMEM((regions, index_rows, LANES), jnp.int32),
            pltpu.VMEM((2, regions, LANES, slots), jnp.float32),
            pltpu.SemaphoreType.DMA(()),
        ],
        compiler_params=pltpu.CompilerParams(vmem_limit_bytes=grant(used)),
        name="correlate",
    )


def on_device(archive, starts, event_owner, station_mask, pair_first, pair_second, pair_count):
    regions = lax.axis_size("region")
    chans = lax.axis_size("chan")
    chan_index = lax.axis_index("chan")
    per_block = starts.shape[0]
    pair_cap = pair_first.shape[0]
    stations = archive.shape[0]
    segment = archive.shape[2]
    bucket = max(2, 2 * per_block // regions)
    slots = regions * bucket
    share = station_share(stations, chans)
    nch = 4 * -(-share * COMP // (4 * regions))

    mask = station_mask.T
    payload = pack(archive, starts.reshape(1, -1), mask, pair_first.reshape(1, -1),
                   pair_second.reshape(1, -1), pair_count, regions, chans, nch)
    received = lax.all_to_all(payload, "region", split_axis=0, concat_axis=0, tiled=True)

    slot_of = slot_table(event_owner, regions, per_block, bucket, slots).reshape(1, -1)
    channel = lax.axis_index("region") * nch + jnp.arange(nch, dtype=jnp.int32)
    local = jnp.minimum(chan_index * share, stations - share) + channel // COMP
    used = (channel < share * COMP) & (local >= chan_index * share)
    station = jnp.where(used, lax.axis_index("stn") * stations + local, -1)

    slot_event, weight_rows = describe(mask, station, slot_of, regions, slots, nch)
    kept, given = correlate(regions, per_block, pair_cap, segment, slots, nch)(
        received, slot_event, weight_rows, forward_table(), lag_table())

    swap = [(0, 1), (1, 0)]
    kept = kept + lax.ppermute(given, "chan", swap).astype(jnp.float32)
    spread = lax.all_to_all(kept.astype(jnp.bfloat16), "region", split_axis=0, concat_axis=0, tiled=True)
    here = lax.axis_index("region")
    whole = lax.optimization_barrier(lax.dynamic_index_in_dim(kept, here, keepdims=False))
    others = jnp.arange(regions, dtype=jnp.int32) != here
    whole = whole + jnp.sum(jnp.where(others[:, None, None], spread.astype(jnp.float32), 0.0), axis=0)
    count = lax.axis_size("stn")
    step = 1
    while step < count:
        sent = whole.astype(jnp.bfloat16)
        other = lax.ppermute(sent, "stn", [(i, i ^ step) for i in range(count)])
        whole = sent.astype(jnp.float32) + other.astype(jnp.float32)
        step *= 2
    other = lax.ppermute(whole, "chan", swap)
    low = jnp.where(chan_index == 0, whole, other)
    high = jnp.where(chan_index == 0, other, whole)
    full = jnp.concatenate([low, high], axis=0)[:LAGS]
    return full[:, :pair_cap], full[:, pair_cap:]


def solution(mesh):
    placed = (
        P("stn", None, ("groups", "region")),
        P(("groups", "region")),
        P("groups"),
        P("groups", None),
        P(("groups", "region")),
        P(("groups", "region")),
        P(("groups", "region")),
    )
    return jax.shard_map(
        on_device,
        mesh=mesh,
        in_specs=placed,
        out_specs=(P(None, ("groups", "region")), P(None, ("groups", "region"))),
        check_vma=False,
    )
```

```python
import math

import jax
import jax.numpy as jnp
import numpy as np
from jax import lax
from jax.experimental import pallas as pl
from jax.experimental.pallas import tpu as pltpu
from jax.sharding import PartitionSpec as P

COMP = 3
WIN = 400
MAXLAG = 50
NFFT = 512
LAGS = 101
BINS = NFFT // 2
LANES = 128
LAG_ROWS = 112
HALF_ROWS = LAG_ROWS // 2
VMEM_ONLY = pl.BlockSpec(memory_space=pltpu.VMEM)
SMEM_ONLY = pl.BlockSpec(memory_space=pltpu.SMEM)
NT = (((1,), (1,)), ((), ()))
TN = (((0,), (0,)), ((), ()))


def forward_table():
    sample = np.arange(NFFT)[:, None]
    freq = np.arange(BINS)[None, :]
    angle = (sample * freq % NFFT) * (2.0 * math.pi / NFFT)
    sine = np.sin(angle)
    sine[:, 0] = np.cos(math.pi * (np.arange(NFFT) % 2))
    table = np.concatenate([np.cos(angle), sine], axis=1)
    table[WIN:] = 0.0
    return jnp.asarray(table, jnp.float32).astype(jnp.bfloat16)


def lag_table():
    shift = np.arange(LAG_ROWS)[:, None] - MAXLAG
    freq = np.arange(BINS)[None, :]
    angle = (freq * shift % NFFT) * (2.0 * math.pi / NFFT)
    weight = np.where(freq == 0, 1.0 / NFFT, 2.0 / NFFT)
    even = weight * np.cos(angle)
    odd = -weight * np.sin(angle)
    odd[:, 0] = (np.cos(math.pi * (shift[:, 0] % 2)) - 1.0) / NFFT
    table = np.concatenate([even, odd], axis=1) * math.sqrt(WIN)
    table[LAGS:] = 0.0
    filler = np.zeros((LANES - LAG_ROWS, NFFT))
    halves = table[:HALF_ROWS], table[HALF_ROWS:]
    table = np.stack([np.concatenate([halves[c], halves[1 - c], filler]) for c in range(2)])
    table = jnp.asarray(table, jnp.float32)
    high = table.astype(jnp.bfloat16)
    return jnp.concatenate([high, (table - high.astype(jnp.float32)).astype(jnp.bfloat16)], axis=1)


def slot_table(event_owner, regions, per_block, bucket, slots):
    blocks = event_owner.reshape(regions, per_block)
    owned = blocks[:, :, None] == jnp.arange(regions, dtype=jnp.int32)[None, None, :]
    onehot = owned.astype(jnp.int32)
    before = jnp.cumsum(onehot, axis=1) - onehot
    ranking = jnp.sum(before * onehot, axis=2)
    block_index = jnp.arange(regions, dtype=jnp.int32)[:, None]
    return (blocks * slots + block_index * bucket + ranking).reshape(-1)


def as_bf16(flags):
    return flags.astype(jnp.float32).astype(jnp.bfloat16)


def digits_of(value):
    return (value >> 7).astype(jnp.float32).astype(jnp.bfloat16), (value & 127).astype(jnp.float32).astype(jnp.bfloat16)


def digit_count(events):
    return 1 if events <= 256 else 2


def field_width(events, pair_cap):
    return -(-(2 * digit_count(events) + 2) // 4) * pair_cap


def separate(regions):
    return regions <= 4


def block_shapes(regions, shape, dtype):
    if separate(regions):
        return [jax.ShapeDtypeStruct(shape, dtype)] * regions
    return [jax.ShapeDtypeStruct((regions,) + shape, dtype)]


def exchange(blocks, regions):
    if separate(regions):
        masks = range(regions - 1, 0, -1)
        moved = {m: lax.ppermute(blocks[m], "region", [(i, i ^ m) for i in range(regions)]) for m in masks}
        return [blocks[0]] + [moved[m] for m in range(1, regions)]
    order = jnp.arange(regions, dtype=jnp.int32) ^ lax.axis_index("region")
    moved = lax.all_to_all(jnp.take(blocks[0], order, axis=0), "region", split_axis=0, concat_axis=0, tiled=True)
    return [jnp.take(moved, order, axis=0)]


def station_share(stations, chans):
    return -(-stations // chans)


def pack(archive, starts, station_mask, pair_first, pair_second, pair_count, regions, chans, nch):
    stations, _, segment = archive.shape
    events = station_mask.shape[1]
    per_block = starts.shape[1]
    pair_cap = pair_first.shape[1]
    share = station_share(stations, chans)

    def kernel(archive, starts, mask, first, second, count, *rest):
        outs, flat = rest[:-1], rest[-1]
        region = lax.axis_index("region")
        chan = lax.axis_index("chan")
        base = jnp.minimum(chan * share, stations - share)
        for block in range(share * COMP // nch, regions):
            flat[block] = jnp.zeros((nch, segment), jnp.float32)
        for station in range(share):
            data = archive[base + station].astype(jnp.float32)
            row = station * COMP
            while row < (station + 1) * COMP:
                end = min((row // nch + 1) * nch, (station + 1) * COMP)
                flat[row // nch, row % nch : row % nch + end - row, :] = data[row - station * COMP : end - station * COMP]
                row = end
        names = lax.broadcasted_iota(jnp.int32, (events, pair_cap), 0)
        usable = mask[...].astype(jnp.float32).astype(jnp.bfloat16)
        chosen = [jnp.dot(usable, as_bf16(names == ref[...]), preferred_element_type=jnp.float32)
                  for ref in (first, second)]
        common = jnp.sum(chosen[0] * chosen[1], axis=0, keepdims=True)
        position = lax.broadcasted_iota(jnp.int32, (1, pair_cap), 1)
        code = jnp.where(position < count[0], common + 1.0, 0.0).astype(jnp.bfloat16)
        offset = digits_of(starts[...] - region * segment)
        used = [jnp.full((1, per_block), digit, jnp.int32) for digit in (count[0] >> 7, count[0] & 127)]
        used = [digit.astype(jnp.float32).astype(jnp.bfloat16) for digit in used]
        rest = jnp.zeros((1, pair_cap - 4 * per_block), jnp.bfloat16)
        scalars = jnp.concatenate(list(offset) + used + [rest], axis=1)
        if digit_count(events) == 1:
            fields = [first[...].astype(jnp.float32).astype(jnp.bfloat16), second[...].astype(jnp.float32).astype(jnp.bfloat16)]
        else:
            fields = list(digits_of(first[...]) + digits_of(second[...]))
        fields += [code, scalars]
        for m in range(regions):
            out = outs[m] if separate(regions) else outs[0].at[m]
            out[:, :segment] = flat[region ^ m].astype(jnp.bfloat16)
            for k, field in enumerate(fields):
                lane = segment + k // 4 * pair_cap
                out[k % 4 : k % 4 + 1, lane : lane + pair_cap] = field

    return pl.pallas_call(
        kernel,
        out_shape=block_shapes(regions, (nch, segment + field_width(events, pair_cap)), jnp.bfloat16),
        in_specs=[VMEM_ONLY] * 5 + [SMEM_ONLY],
        out_specs=[VMEM_ONLY] * (regions if separate(regions) else 1),
        scratch_shapes=[pltpu.VMEM((regions, nch, segment), jnp.float32)],
        name="pack",
    )(archive, starts, station_mask, pair_first, pair_second, pair_count)


def describe(station_mask, station, slot_of, regions, slots, nch):
    events = station_mask.shape[1]
    per_block = events // regions

    def kernel(mask, station, slot_of, slot_event, weight_rows):
        listed = lax.broadcasted_iota(jnp.int32, (mask.shape[0], LANES), 0)
        usable = mask[...].astype(jnp.float32).astype(jnp.bfloat16)
        for c in range(nch):
            value = lax.dot_general(usable, as_bf16(listed == station[c]), TN, preferred_element_type=jnp.float32)
            for part in range(regions):
                row = (part * nch + c) * per_block
                weight_rows[row : row + per_block, :] = value[part * per_block : (part + 1) * per_block]
        names = digits_of(lax.broadcasted_iota(jnp.int32, (events, LANES), 0) + 1)
        place = lax.broadcasted_iota(jnp.int32, (slots, events), 0)
        slot_lane = slot_of[...]

        def one_region(part, carry):
            hit = as_bf16(place + part * slots == slot_lane)
            high, low = (jnp.dot(hit, digit, preferred_element_type=jnp.float32) for digit in names)
            slot_event[pl.ds(pl.multiple_of(part * slots, slots), slots), :] = high * 128.0 + low - 1.0
            return carry

        lax.fori_loop(0, regions, one_region, 0)

    return pl.pallas_call(
        kernel,
        out_shape=(jax.ShapeDtypeStruct((regions * slots, LANES), jnp.float32),
                   jax.ShapeDtypeStruct((events * nch, LANES), jnp.float32)),
        in_specs=[VMEM_ONLY, SMEM_ONLY, VMEM_ONLY],
        out_specs=(VMEM_ONLY, VMEM_ONLY),
        compiler_params=pltpu.CompilerParams(vmem_limit_bytes=grant(regions * slots + 2 * events * nch)),
        name="describe",
    )(station_mask, station, slot_of)


def grant(rows):
    return min(rows * LANES * 4 * 5 // 4 + (4 << 20), 60 * 1024 * 1024)


def correlate(regions, per_block, pair_cap, segment, slots, nch):
    rows = 2 * nch
    tiles = segment // LANES + 2
    events = regions * per_block
    half = 2 * LANES
    cols = pair_cap // LANES
    per_row = min(per_block, LANES)
    batch = regions if separate(regions) else 1
    digits = digit_count(events)
    static = separate(regions)
    sources = regions if static else 1

    def kernel(*refs):
        received, refs = refs[:sources], refs[sources:]
        (slot_event, weight_rows, table, weights, kept, given, shifted, windows, spec, prod, index_vmem, index, profile,
         sem) = refs
        region = lax.axis_index("region")

        def recv(m):
            return received[m] if static else received[0].at[m]

        def field(part, k):
            lane = segment + k // 4 * pair_cap
            return recv(part)[:, lane : lane + pair_cap].astype(jnp.float32)[k % 4 : k % 4 + 1]

        def listed(part, k):
            if digits == 1:
                return field(part, k)
            return field(part, 2 * k) * 128.0 + field(part, 2 * k + 1)

        for part in range(regions):
            rows_out = []
            for k in range(2):
                event = listed(part, k).astype(jnp.int32) * (2 * rows)
                rows_out += [event[:, c * LANES : (c + 1) * LANES] for c in range(cols)]
            scalars = field(part, 2 * digits + 1).astype(jnp.int32)
            rows_out += [scalars[:, c * LANES : (c + 1) * LANES] for c in range(2)]
            for row, value in enumerate(rows_out):
                index_vmem[part, row : row + 1, :] = value
        copy = pltpu.make_async_copy(index_vmem, index, sem)
        copy.start()

        def widen(part, carry=0):
            for k in range(tiles + 2):
                data = recv(part)[:, k * LANES : (k + 1) * LANES].astype(jnp.float32)
                if k < tiles:
                    shifted[part, k, pl.ds(0, nch, stride=2), :] = data
                if k >= 2:
                    shifted[part, k - 2, pl.ds(1, nch, stride=2), :] = data
            return carry

        if static:
            for m in range(regions):
                widen(m)
        else:
            lax.fori_loop(0, regions, widen, 0)
        copy.wait()

        lane = lax.broadcasted_iota(jnp.int32, (rows, LANES), 1)
        sublane = lax.broadcasted_iota(jnp.int32, (rows, LANES), 0)
        count = per_block * nch
        inside = lax.broadcasted_iota(jnp.int32, (count, LANES), 1) < WIN - half - LANES

        def one_segment(part, slot):
            for event in range(per_block):
                base = index[part, 2 * cols, event]
                off = index[part, 2 * cols, per_block + event]
                turn = (LANES - off) & (LANES - 1)
                data = [shifted[part, base + k] for k in range(3)]
                later = lane >= off
                row = event * rows
                windows[slot, 0, row : row + rows, :] = pltpu.roll(jnp.where(later, data[0], data[1]), turn, 1)
                windows[slot, 1, row : row + rows, :] = pltpu.roll(jnp.where(later, data[1], data[2]), turn, 1)
            pieces = [[jnp.concatenate([windows[slot, t, pl.ds(2 * c + k, per_block, stride=rows), :] for c in range(nch)])
                       for t in range(2)] for k in range(2)]
            squares = pieces[0][0] * pieces[0][0] + pieces[0][1] * pieces[0][1] + pieces[1][0] * pieces[1][0]
            squares += jnp.where(inside, pieces[1][1] * pieces[1][1], 0.0)
            energy = jnp.sum(squares, axis=1, keepdims=True)
            early, late = (jnp.concatenate(piece, axis=1).astype(jnp.bfloat16) for piece in pieces)
            coefs = jnp.dot(early, table[:half, :], preferred_element_type=jnp.float32)
            coefs += jnp.dot(late, table[half:, :], preferred_element_type=jnp.float32)
            place = pl.multiple_of((part ^ region) * count, count)
            factor = weight_rows[pl.ds(place, count), :] * lax.rsqrt(energy + WIN * 1e-05)
            for s in range(2):
                for k in range(2):
                    column = s * BINS + k * LANES
                    piece = (coefs[:, column : column + LANES] * factor).astype(jnp.bfloat16).astype(jnp.float32)
                    for c in range(nch):
                        row = pl.multiple_of((part ^ region) * (2 * rows * per_block), 2 * rows) + s * rows + 2 * c + k
                        spec[pl.ds(row, per_block, stride=2 * rows), :] = piece[c * per_block : (c + 1) * per_block]

        def looped_segment(part, carry):
            one_segment(part, 0)
            return carry

        if static:
            for part in range(regions):
                one_segment(part, part)
        else:
            lax.fori_loop(0, regions, looped_segment, 0)

        chan = lax.axis_index("chan")
        special = (sublane % 2 == 0) & (lane == 0)
        upper = sublane < nch
        profile[...] = jnp.zeros_like(profile)

        def one_group(group, carry):
            def some_pairs(member, row):
                part = group * batch + member
                for step in range(LANES):
                    a = pl.multiple_of(index[part, row, step], 2 * rows)
                    b = pl.multiple_of(index[part, cols + row, step], 2 * rows)
                    cos_a, sin_a = spec[pl.ds(a, rows), :], spec[pl.ds(a + rows, rows), :]
                    cos_b, sin_b = spec[pl.ds(b, rows), :], spec[pl.ds(b + rows, rows), :]
                    sines = sin_a * sin_b
                    even = cos_a * cos_b + sines
                    odd = jnp.where(special, sines, sin_a * cos_b - cos_a * sin_b)
                    even += pltpu.roll(even, nch, 0)
                    odd += pltpu.roll(odd, nch, 0)
                    place = pl.multiple_of(((member * cols + row) * LANES + step) * rows, rows)
                    prod[pl.ds(place, rows), :] = jnp.where(upper, even, odd)
                return member

            def pairs_of(member, inner):
                part = group * batch + member
                pairs = index[part, 2 * cols + 1, 0] * LANES + index[part, 2 * cols + 1, per_block]
                lax.fori_loop(0, jnp.minimum((pairs + LANES - 1) // LANES, cols), lambda row, m: some_pairs(m, row),
                              member)
                return inner

            lax.fori_loop(0, batch, pairs_of, 0)
            for member in range(batch):
                part = group * batch + member
                first_row = member * pair_cap * rows
                sums = []
                for k in (0, 1, nch, nch + 1):
                    total = prod[pl.ds(first_row + k, pair_cap, stride=rows), :]
                    for c in range(1, nch // 2):
                        total += prod[pl.ds(first_row + k + 2 * c, pair_cap, stride=rows), :]
                    sums.append(total.astype(jnp.bfloat16))
                both = lax.dot_general(weights[chan], jnp.concatenate(sums, axis=1), NT,
                                       preferred_element_type=jnp.float32)
                cross = both[:LANES] + both[LANES:]
                code = field(part, 2 * digits)
                live = jnp.maximum((code - 1.0) * COMP, 1.0)
                stack = jnp.where(code > 0.0, cross * lax.rsqrt(live), 0.0)
                kept[part, :, :pair_cap] = stack[:HALF_ROWS]
                given[part, :, :pair_cap] = stack[HALF_ROWS:LAG_ROWS].astype(jnp.bfloat16)
                first, second = listed(part, 0), listed(part, 1)
                stack = stack.astype(jnp.bfloat16)

                def gathered(owner, event):
                    column = slot_event[pl.ds(pl.multiple_of(owner * slots, slots), slots), :]
                    hot = as_bf16(jnp.concatenate([column] * cols, axis=1) == event)
                    return lax.dot_general(stack, hot, NT, preferred_element_type=jnp.float32)

                owner = part ^ region
                after = (owner + 1) & (regions - 1)
                profile[0, part] += gathered(owner, first)
                profile[1, part] += gathered(owner, second)
                profile[1, after ^ region] += gathered(after, second)
            return carry

        if static:
            one_group(0, 0)
        else:
            lax.fori_loop(0, regions, one_group, 0)
        def lag_of(axis):
            row = lax.broadcasted_iota(jnp.int32, (LANES, LANES), axis)
            return jnp.where(row < HALF_ROWS, row + chan * HALF_ROWS, row - chan * HALF_ROWS)

        mirror = as_bf16(lag_of(0) + lag_of(1) == LAGS - 1)

        def finish(part, carry):
            value = profile[1, part]
            high = value.astype(jnp.bfloat16)
            low = (value - high.astype(jnp.float32)).astype(jnp.bfloat16)
            flipped = jnp.dot(mirror, high, preferred_element_type=jnp.float32) + jnp.dot(
                mirror, low, preferred_element_type=jnp.float32)
            total = profile[0, part] + flipped
            kept[part, :, pair_cap:] = total[:HALF_ROWS]
            given[part, :, pair_cap:] = total[HALF_ROWS:LAG_ROWS].astype(jnp.bfloat16)
            return carry

        lax.fori_loop(0, regions, finish, 0)

    shape = (regions, HALF_ROWS, pair_cap + slots)
    index_rows = 8 * -(-(2 * cols + 2) // 8)
    width = (pair_cap + slots) // LANES
    used = regions * (tiles * rows + LAG_ROWS * width + 2 * LANES + index_rows + 4 * tiles + slots)
    used += (2 * per_block * batch + 2 * events + batch * pair_cap) * rows + events * nch + 3 * NFFT
    return pl.pallas_call(
        kernel,
        out_shape=(jax.ShapeDtypeStruct(shape, jnp.float32), jax.ShapeDtypeStruct(shape, jnp.bfloat16)),
        in_specs=[VMEM_ONLY] * (sources + 4),
        out_specs=(VMEM_ONLY, VMEM_ONLY),
        scratch_shapes=[
            pltpu.VMEM((regions, tiles, rows, LANES), jnp.float32),
            pltpu.VMEM((batch, 2, per_block * rows, LANES), jnp.float32),
            pltpu.VMEM((2 * events * rows, LANES), jnp.float32),
            pltpu.VMEM((batch * pair_cap * rows, LANES), jnp.float32),
            pltpu.VMEM((regions, index_rows, LANES), jnp.int32),
            pltpu.SMEM((regions, index_rows, LANES), jnp.int32),
            pltpu.VMEM((2, regions, LANES, slots), jnp.float32),
            pltpu.SemaphoreType.DMA(()),
        ],
        compiler_params=pltpu.CompilerParams(vmem_limit_bytes=grant(used)),
        name="correlate",
    )


def on_device(archive, starts, event_owner, station_mask, pair_first, pair_second, pair_count):
    regions = lax.axis_size("region")
    chans = lax.axis_size("chan")
    chan_index = lax.axis_index("chan")
    per_block = starts.shape[0]
    pair_cap = pair_first.shape[0]
    stations = archive.shape[0]
    segment = archive.shape[2]
    bucket = max(2, 2 * per_block // regions)
    slots = regions * bucket
    share = station_share(stations, chans)
    nch = 4 * -(-share * COMP // (4 * regions))

    mask = station_mask.T
    blocks = pack(archive, starts.reshape(1, -1), mask, pair_first.reshape(1, -1),
                  pair_second.reshape(1, -1), pair_count, regions, chans, nch)
    received = exchange(blocks, regions)

    slot_of = slot_table(event_owner, regions, per_block, bucket, slots).reshape(1, -1)
    channel = lax.axis_index("region") * nch + jnp.arange(nch, dtype=jnp.int32)
    local = jnp.minimum(chan_index * share, stations - share) + channel // COMP
    used = (channel < share * COMP) & (local >= chan_index * share)
    station = jnp.where(used, lax.axis_index("stn") * stations + local, -1)

    slot_event, weight_rows = describe(mask, station, slot_of, regions, slots, nch)
    kept, given = correlate(regions, per_block, pair_cap, segment, slots, nch)(
        *received, slot_event, weight_rows, forward_table(), lag_table())

    swap = [(0, 1), (1, 0)]
    swapped = lax.ppermute(given, "chan", swap)
    if separate(regions):
        sums = [kept[m] + swapped[m].astype(jnp.float32) for m in range(regions)]
        moved = exchange([term.astype(jnp.bfloat16) for term in sums], regions)
        whole = sums[0]
        for term in moved[1:]:
            whole = whole + term.astype(jnp.float32)
    else:
        moved = exchange([(kept + swapped.astype(jnp.float32)).astype(jnp.bfloat16)], regions)
        whole = jnp.sum(moved[0].astype(jnp.float32), axis=0)
    count = lax.axis_size("stn")
    step = 1
    while step < count:
        sent = whole.astype(jnp.bfloat16)
        other = lax.ppermute(sent, "stn", [(i, i ^ step) for i in range(count)])
        whole = sent.astype(jnp.float32) + other.astype(jnp.float32)
        step *= 2
    other = lax.ppermute(whole, "chan", swap)
    low = jnp.where(chan_index == 0, whole, other)
    high = jnp.where(chan_index == 0, other, whole)
    full = jnp.concatenate([low, high], axis=0)[:LAGS]
    return full[:, :pair_cap], full[:, pair_cap:]


def solution(mesh):
    placed = (
        P("stn", None, ("groups", "region")),
        P(("groups", "region")),
        P("groups"),
        P("groups", None),
        P(("groups", "region")),
        P(("groups", "region")),
        P(("groups", "region")),
    )
    return jax.shard_map(
        on_device,
        mesh=mesh,
        in_specs=placed,
        out_specs=(P(None, ("groups", "region")), P(None, ("groups", "region"))),
        check_vma=False,
    )
```

```python
import math

import jax
import jax.numpy as jnp
import numpy as np
from jax import lax
from jax.experimental import pallas as pl
from jax.experimental.pallas import tpu as pltpu
from jax.sharding import PartitionSpec as P

COMP = 3
WIN = 400
MAXLAG = 50
NFFT = 512
LAGS = 101
BINS = NFFT // 2
LANES = 128
LAG_ROWS = 112
HALF_ROWS = LAG_ROWS // 2
VMEM_ONLY = pl.BlockSpec(memory_space=pltpu.VMEM)
SMEM_ONLY = pl.BlockSpec(memory_space=pltpu.SMEM)
NT = (((1,), (1,)), ((), ()))
TN = (((0,), (0,)), ((), ()))


def forward_table():
    sample = np.arange(NFFT)[:, None]
    freq = np.arange(BINS)[None, :]
    angle = (sample * freq % NFFT) * (2.0 * math.pi / NFFT)
    sine = np.sin(angle)
    sine[:, 0] = np.cos(math.pi * (np.arange(NFFT) % 2))
    table = np.concatenate([np.cos(angle), sine], axis=1)
    table[WIN:] = 0.0
    return jnp.asarray(table, jnp.float32).astype(jnp.bfloat16)


def lag_table():
    shift = np.arange(LAG_ROWS)[:, None] - MAXLAG
    freq = np.arange(BINS)[None, :]
    angle = (freq * shift % NFFT) * (2.0 * math.pi / NFFT)
    weight = np.where(freq == 0, 1.0 / NFFT, 2.0 / NFFT)
    even = weight * np.cos(angle)
    odd = -weight * np.sin(angle)
    odd[:, 0] = (np.cos(math.pi * (shift[:, 0] % 2)) - 1.0) / NFFT
    table = np.concatenate([even, odd], axis=1) * math.sqrt(WIN)
    table[LAGS:] = 0.0
    filler = np.zeros((LANES - LAG_ROWS, NFFT))
    halves = table[:HALF_ROWS], table[HALF_ROWS:]
    table = np.stack([np.concatenate([halves[c], halves[1 - c], filler]) for c in range(2)])
    table = jnp.asarray(table, jnp.float32)
    high = table.astype(jnp.bfloat16)
    return jnp.concatenate([high, (table - high.astype(jnp.float32)).astype(jnp.bfloat16)], axis=1)


def slot_table(event_owner, regions, per_block, bucket, slots):
    blocks = event_owner.reshape(regions, per_block)
    owned = blocks[:, :, None] == jnp.arange(regions, dtype=jnp.int32)[None, None, :]
    onehot = owned.astype(jnp.int32)
    before = jnp.cumsum(onehot, axis=1) - onehot
    ranking = jnp.sum(before * onehot, axis=2)
    block_index = jnp.arange(regions, dtype=jnp.int32)[:, None]
    return (blocks * slots + block_index * bucket + ranking).reshape(-1)


def as_bf16(flags):
    return flags.astype(jnp.float32).astype(jnp.bfloat16)


def digits_of(value):
    return (value >> 7).astype(jnp.float32).astype(jnp.bfloat16), (value & 127).astype(jnp.float32).astype(jnp.bfloat16)


def digit_count(events):
    return 1 if events <= 256 else 2


def field_width(events, pair_cap):
    return -(-(2 * digit_count(events) + 2) // 4) * pair_cap


def separate(regions):
    return regions <= 4


def block_shapes(regions, shape, dtype):
    if separate(regions):
        return [jax.ShapeDtypeStruct(shape, dtype)] * regions
    return [jax.ShapeDtypeStruct((regions,) + shape, dtype)]


def exchange(blocks, regions):
    if separate(regions):
        masks = range(regions - 1, 0, -1)
        moved = {m: lax.ppermute(blocks[m], "region", [(i, i ^ m) for i in range(regions)]) for m in masks}
        return [blocks[0]] + [moved[m] for m in range(1, regions)]
    order = jnp.arange(regions, dtype=jnp.int32) ^ lax.axis_index("region")
    moved = lax.all_to_all(jnp.take(blocks[0], order, axis=0), "region", split_axis=0, concat_axis=0, tiled=True)
    return [jnp.take(moved, order, axis=0)]


def station_share(stations, chans):
    return -(-stations // chans)


def pack(archive, starts, station_mask, pair_first, pair_second, pair_count, regions, chans, nch):
    stations, _, segment = archive.shape
    events = station_mask.shape[1]
    per_block = starts.shape[1]
    pair_cap = pair_first.shape[1]
    share = station_share(stations, chans)

    def kernel(archive, starts, mask, first, second, count, *rest):
        outs, flat = rest[:-1], rest[-1]
        region = lax.axis_index("region")
        chan = lax.axis_index("chan")
        base = jnp.minimum(chan * share, stations - share)
        for block in range(share * COMP // nch, regions):
            flat[block] = jnp.zeros((nch, segment), jnp.float32)
        for station in range(share):
            data = archive[base + station].astype(jnp.float32)
            row = station * COMP
            while row < (station + 1) * COMP:
                end = min((row // nch + 1) * nch, (station + 1) * COMP)
                flat[row // nch, row % nch : row % nch + end - row, :] = data[row - station * COMP : end - station * COMP]
                row = end
        names = lax.broadcasted_iota(jnp.int32, (events, pair_cap), 0)
        usable = mask[...].astype(jnp.float32).astype(jnp.bfloat16)
        chosen = [jnp.dot(usable, as_bf16(names == ref[...]), preferred_element_type=jnp.float32)
                  for ref in (first, second)]
        common = jnp.sum(chosen[0] * chosen[1], axis=0, keepdims=True)
        position = lax.broadcasted_iota(jnp.int32, (1, pair_cap), 1)
        code = jnp.where(position < count[0], common + 1.0, 0.0).astype(jnp.bfloat16)
        offset = digits_of(starts[...] - region * segment)
        used = [jnp.full((1, per_block), digit, jnp.int32) for digit in (count[0] >> 7, count[0] & 127)]
        used = [digit.astype(jnp.float32).astype(jnp.bfloat16) for digit in used]
        rest = jnp.zeros((1, pair_cap - 4 * per_block), jnp.bfloat16)
        scalars = jnp.concatenate(list(offset) + used + [rest], axis=1)
        if digit_count(events) == 1:
            fields = [first[...].astype(jnp.float32).astype(jnp.bfloat16), second[...].astype(jnp.float32).astype(jnp.bfloat16)]
        else:
            fields = list(digits_of(first[...]) + digits_of(second[...]))
        fields += [code, scalars]
        for m in range(regions):
            out = outs[m] if separate(regions) else outs[0].at[m]
            out[:, :segment] = flat[region ^ m].astype(jnp.bfloat16)
            for k, field in enumerate(fields):
                lane = segment + k // 4 * pair_cap
                out[k % 4 : k % 4 + 1, lane : lane + pair_cap] = field

    return pl.pallas_call(
        kernel,
        out_shape=block_shapes(regions, (nch, segment + field_width(events, pair_cap)), jnp.bfloat16),
        in_specs=[VMEM_ONLY] * 5 + [SMEM_ONLY],
        out_specs=[VMEM_ONLY] * (regions if separate(regions) else 1),
        scratch_shapes=[pltpu.VMEM((regions, nch, segment), jnp.float32)],
        name="pack",
    )(archive, starts, station_mask, pair_first, pair_second, pair_count)


def describe(station_mask, station, slot_of, regions, slots, nch):
    events = station_mask.shape[1]
    per_block = events // regions

    def kernel(mask, station, slot_of, slot_event, weight_rows):
        region = lax.axis_index("region")
        listed = lax.broadcasted_iota(jnp.int32, (mask.shape[0], LANES), 0)
        usable = mask[...].astype(jnp.float32).astype(jnp.bfloat16)
        for c in range(nch):
            value = lax.dot_general(usable, as_bf16(listed == station[c]), TN, preferred_element_type=jnp.float32)
            for part in range(regions):
                row = pl.multiple_of(((part ^ region) * nch + c) * per_block, per_block)
                weight_rows[pl.ds(row, per_block), :] = value[part * per_block : (part + 1) * per_block]
        names = digits_of(lax.broadcasted_iota(jnp.int32, (events, LANES), 0) + 1)
        place = lax.broadcasted_iota(jnp.int32, (slots, events), 0)
        slot_lane = slot_of[...]

        def one_region(part, carry):
            hit = as_bf16(place + part * slots == slot_lane)
            high, low = (jnp.dot(hit, digit, preferred_element_type=jnp.float32) for digit in names)
            slot_event[pl.ds(pl.multiple_of(part * slots, slots), slots), :] = high * 128.0 + low - 1.0
            return carry

        lax.fori_loop(0, regions, one_region, 0)

    return pl.pallas_call(
        kernel,
        out_shape=(jax.ShapeDtypeStruct((regions * slots, LANES), jnp.float32),
                   jax.ShapeDtypeStruct((events * nch, LANES), jnp.float32)),
        in_specs=[VMEM_ONLY, SMEM_ONLY, VMEM_ONLY],
        out_specs=(VMEM_ONLY, VMEM_ONLY),
        compiler_params=pltpu.CompilerParams(vmem_limit_bytes=grant(regions * slots + 2 * events * nch)),
        name="describe",
    )(station_mask, station, slot_of)


def grant(rows):
    return min(rows * LANES * 4 * 5 // 4 + (4 << 20), 60 * 1024 * 1024)


class Cutter:
    def __init__(self, per_block, segment, nch):
        self.per_block, self.nch = per_block, nch
        self.rows = 2 * nch
        self.tiles = segment // LANES + 2
        self.count = per_block * nch
        self.spec_rows = 2 * self.rows * per_block

    def words(self, scalars, slot):
        tile, lane = scalars[:, : self.per_block], scalars[:, self.per_block : 2 * self.per_block]
        return ((tile + slot * self.tiles) * (256.0 * self.rows) + (LANES - lane)).astype(jnp.int32)

    def widen(self, source, shifted, slot):
        rows, nch = self.rows, self.nch
        first = slot * (self.tiles * rows)
        if not isinstance(slot, int):
            first = pl.multiple_of(first, rows)
        for k in range(self.tiles + 2):
            data = source[:, k * LANES : (k + 1) * LANES].astype(jnp.float32)
            if k < self.tiles:
                shifted[pl.ds(first + k * rows, nch, stride=2), :] = data
            if k >= 2:
                shifted[pl.ds(first + (k - 2) * rows + 1, nch, stride=2), :] = data

    def cut(self, word_of, shifted, windows, slot):
        rows = self.rows
        from_right = LANES - 1 - lax.broadcasted_iota(jnp.int32, (rows, LANES), 1)
        for event in range(self.per_block):
            word = word_of(event)
            first = pl.multiple_of(word >> 8, rows)
            turn = word & (2 * LANES - 1)
            data = [shifted[pl.ds(first + k * rows, rows), :] for k in range(3)]
            later = from_right < turn
            turn = turn & (LANES - 1)
            row = event * rows
            windows[slot, 0, row : row + rows, :] = pltpu.roll(jnp.where(later, data[0], data[1]), turn, 1)
            windows[slot, 1, row : row + rows, :] = pltpu.roll(jnp.where(later, data[1], data[2]), turn, 1)

    def transform(self, windows, slot, weight_rows, block, table, spec, place):
        per_block, nch, rows, count = self.per_block, self.nch, self.rows, self.count
        half = 2 * LANES
        inside = lax.broadcasted_iota(jnp.int32, (count, LANES), 1) < WIN - half - LANES
        pieces = [[jnp.concatenate([windows[slot, t, pl.ds(2 * c + k, per_block, stride=rows), :] for c in range(nch)])
                   for t in range(2)] for k in range(2)]
        squares = pieces[0][0] * pieces[0][0] + pieces[0][1] * pieces[0][1] + pieces[1][0] * pieces[1][0]
        squares += jnp.where(inside, pieces[1][1] * pieces[1][1], 0.0)
        energy = jnp.sum(squares, axis=1, keepdims=True)
        early, late = (jnp.concatenate(piece, axis=1).astype(jnp.bfloat16) for piece in pieces)
        coefs = jnp.dot(early, table[:half, :], preferred_element_type=jnp.float32)
        coefs += jnp.dot(late, table[half:, :], preferred_element_type=jnp.float32)
        first = block * count if isinstance(block, int) else pl.multiple_of(block * count, count)
        factor = weight_rows[pl.ds(first, count), :] * lax.rsqrt(energy + WIN * 1e-05)
        for s in range(2):
            for k in range(2):
                column = s * BINS + k * LANES
                piece = (coefs[:, column : column + LANES] * factor).astype(jnp.bfloat16).astype(jnp.float32)
                for c in range(nch):
                    row = place + s * rows + 2 * c + k
                    spec[pl.ds(row, per_block, stride=2 * rows), :] = piece[c * per_block : (c + 1) * per_block]


def scalar_field(events):
    return 2 * digit_count(events) + 1


def early_spectra(blocks, weight_rows, table, regions, per_block, pair_cap, segment, nch):
    cutter = Cutter(per_block, segment, nch)
    number = len(blocks)
    k = scalar_field(regions * per_block)

    def kernel(*refs):
        sources, refs = refs[:number], refs[number:]
        weight_rows, table, spec, shifted, windows, index_vmem, index, sem = refs
        for slot in range(number):
            lane = segment + k // 4 * pair_cap
            scalars = sources[slot][:, lane : lane + LANES].astype(jnp.float32)[k % 4 : k % 4 + 1]
            index_vmem[slot : slot + 1, :per_block] = cutter.words(scalars, slot)
        copy = pltpu.make_async_copy(index_vmem, index, sem)
        copy.start()
        for slot in range(number):
            cutter.widen(sources[slot], shifted, slot)
        copy.wait()

        def cut(slot, carry):
            cutter.cut(lambda event: index[slot, event], shifted, windows, slot)
            return carry

        lax.fori_loop(0, number, cut, 0)
        for slot in range(number):
            cutter.transform(windows, slot, weight_rows, slot, table, spec, slot * cutter.spec_rows)

    used = number * (cutter.spec_rows + (cutter.tiles + 2 * per_block) * cutter.rows + 2 * segment * nch // LANES)
    return pl.pallas_call(
        kernel,
        out_shape=jax.ShapeDtypeStruct((number * cutter.spec_rows, LANES), jnp.float32),
        in_specs=[VMEM_ONLY] * (number + 2),
        out_specs=VMEM_ONLY,
        scratch_shapes=[
            pltpu.VMEM((number * cutter.tiles * cutter.rows, LANES), jnp.float32),
            pltpu.VMEM((number, 2, per_block * cutter.rows, LANES), jnp.float32),
            pltpu.VMEM((8, LANES), jnp.int32),
            pltpu.SMEM((8, LANES), jnp.int32),
            pltpu.SemaphoreType.DMA(()),
        ],
        compiler_params=pltpu.CompilerParams(vmem_limit_bytes=grant(used + weight_rows.shape[0] + 2 * NFFT)),
        name="early_spectra",
    )(*blocks, weight_rows, table)


def correlate(regions, per_block, pair_cap, segment, slots, nch, ready):
    cutter = Cutter(per_block, segment, nch)
    rows, tiles = cutter.rows, cutter.tiles
    events = regions * per_block
    cols = pair_cap // LANES
    batch = regions if separate(regions) else 1
    digits = digit_count(events)
    static = separate(regions)
    sources = regions if static else 1
    shift = per_block.bit_length() - 1
    assert per_block == 1 << shift

    def kernel(*refs):
        received, refs = refs[:sources], refs[sources:]
        (ready_spec, slot_event, weight_rows, table, weights, kept, given, shifted, windows, spec, prod, index_vmem, index,
         profile, sem) = refs if ready else (None,) + refs
        region = lax.axis_index("region")

        def recv(m):
            return received[m] if static else received[0].at[m]

        def field(part, k):
            lane = segment + k // 4 * pair_cap
            return recv(part)[:, lane : lane + pair_cap].astype(jnp.float32)[k % 4 : k % 4 + 1]

        def listed(part, k):
            if digits == 1:
                return field(part, k)
            return field(part, 2 * k) * 128.0 + field(part, 2 * k + 1)

        for part in range(regions):
            rows_out = []
            for k in range(2):
                event = (listed(part, k).astype(jnp.int32) ^ (region << shift)) * (2 * rows)
                rows_out += [event[:, c * LANES : (c + 1) * LANES] for c in range(cols)]
            scalars = field(part, scalar_field(events))
            rows_out += [scalars[:, LANES : 2 * LANES].astype(jnp.int32)]
            for row, value in enumerate(rows_out):
                index_vmem[part, row : row + 1, :] = value
            slot = part - ready if static else part
            index_vmem[part, 2 * cols + 1 : 2 * cols + 2, :per_block] = cutter.words(scalars, slot)
        copy = pltpu.make_async_copy(index_vmem, index, sem)
        copy.start()
        if static:
            if ready:
                spec[: ready * cutter.spec_rows, :] = ready_spec[...]
            for part in range(ready, regions):
                cutter.widen(recv(part), shifted, part - ready)
        else:
            def widen(part, carry):
                cutter.widen(recv(part), shifted, part)
                return carry

            lax.fori_loop(0, regions, widen, 0)
        profile[...] = jnp.zeros_like(profile)
        copy.wait()

        def cut(slot, carry):
            cutter.cut(lambda event: index[slot + ready, 2 * cols + 1, event], shifted, windows, slot)
            return carry

        def cut_and_transform(part, carry):
            cutter.cut(lambda event: index[part, 2 * cols + 1, event], shifted, windows, 0)
            place = pl.multiple_of(part * cutter.spec_rows, cutter.spec_rows)
            cutter.transform(windows, 0, weight_rows, part, table, spec, place)
            return carry

        if static:
            lax.fori_loop(0, regions - ready, cut, 0)
            for part in range(ready, regions):
                cutter.transform(windows, part - ready, weight_rows, part, table, spec, part * cutter.spec_rows)
        else:
            lax.fori_loop(0, regions, cut_and_transform, 0)

        lane = lax.broadcasted_iota(jnp.int32, (rows, LANES), 1)
        sublane = lax.broadcasted_iota(jnp.int32, (rows, LANES), 0)
        chan = lax.axis_index("chan")
        special = (sublane % 2 == 0) & (lane == 0)
        upper = sublane < nch

        def one_group(group, carry):
            def some_pairs(member, row):
                part = group * batch + member
                for step in range(LANES):
                    a = pl.multiple_of(index[part, row, step], 2 * rows)
                    b = pl.multiple_of(index[part, cols + row, step], 2 * rows)
                    cos_a, sin_a = spec[pl.ds(a, rows), :], spec[pl.ds(a + rows, rows), :]
                    cos_b, sin_b = spec[pl.ds(b, rows), :], spec[pl.ds(b + rows, rows), :]
                    sines = sin_a * sin_b
                    even = cos_a * cos_b + sines
                    odd = jnp.where(special, sines, sin_a * cos_b - cos_a * sin_b)
                    even += pltpu.roll(even, nch, 0)
                    odd += pltpu.roll(odd, nch, 0)
                    place = pl.multiple_of(((member * cols + row) * LANES + step) * rows, rows)
                    prod[pl.ds(place, rows), :] = jnp.where(upper, even, odd)
                return member

            def pairs_of(member, inner):
                part = group * batch + member
                pairs = index[part, 2 * cols, 0] * LANES + index[part, 2 * cols, per_block]
                lax.fori_loop(0, jnp.minimum((pairs + LANES - 1) // LANES, cols), lambda row, m: some_pairs(m, row),
                              member)
                return inner

            lax.fori_loop(0, batch, pairs_of, 0)
            for member in range(batch):
                part = group * batch + member
                first_row = member * pair_cap * rows
                sums = []
                for k in (0, 1, nch, nch + 1):
                    total = prod[pl.ds(first_row + k, pair_cap, stride=rows), :]
                    for c in range(1, nch // 2):
                        total += prod[pl.ds(first_row + k + 2 * c, pair_cap, stride=rows), :]
                    sums.append(total.astype(jnp.bfloat16))
                both = lax.dot_general(weights[chan], jnp.concatenate(sums, axis=1), NT,
                                       preferred_element_type=jnp.float32)
                cross = both[:LANES] + both[LANES:]
                code = field(part, 2 * digits)
                live = jnp.maximum((code - 1.0) * COMP, 1.0)
                stack = jnp.where(code > 0.0, cross * lax.rsqrt(live), 0.0)
                kept[part, :, :pair_cap] = stack[:HALF_ROWS]
                given[part, :, :pair_cap] = stack[HALF_ROWS:LAG_ROWS].astype(jnp.bfloat16)
                first, second = listed(part, 0), listed(part, 1)
                stack = stack.astype(jnp.bfloat16)

                def gathered(owner, event):
                    column = slot_event[pl.ds(pl.multiple_of(owner * slots, slots), slots), :]
                    hot = as_bf16(jnp.concatenate([column] * cols, axis=1) == event)
                    return lax.dot_general(stack, hot, NT, preferred_element_type=jnp.float32)

                owner = part ^ region
                after = (owner + 1) & (regions - 1)
                profile[0, part] += gathered(owner, first)
                profile[1, part] += gathered(owner, second)
                profile[1, after ^ region] += gathered(after, second)
            return carry

        if static:
            one_group(0, 0)
        else:
            lax.fori_loop(0, regions, one_group, 0)
        def lag_of(axis):
            row = lax.broadcasted_iota(jnp.int32, (LANES, LANES), axis)
            return jnp.where(row < HALF_ROWS, row + chan * HALF_ROWS, row - chan * HALF_ROWS)

        mirror = as_bf16(lag_of(0) + lag_of(1) == LAGS - 1)

        def finish(part, carry):
            value = profile[1, part]
            high = value.astype(jnp.bfloat16)
            low = (value - high.astype(jnp.float32)).astype(jnp.bfloat16)
            flipped = jnp.dot(mirror, high, preferred_element_type=jnp.float32) + jnp.dot(
                mirror, low, preferred_element_type=jnp.float32)
            total = profile[0, part] + flipped
            kept[part, :, pair_cap:] = total[:HALF_ROWS]
            given[part, :, pair_cap:] = total[HALF_ROWS:LAG_ROWS].astype(jnp.bfloat16)
            return carry

        lax.fori_loop(0, regions, finish, 0)

    shape = (regions, HALF_ROWS, pair_cap + slots)
    index_rows = 8 * -(-(2 * cols + 2) // 8)
    width = (pair_cap + slots) // LANES
    used = regions * (tiles * rows + LAG_ROWS * width + 2 * LANES + index_rows + 4 * tiles + slots) + ready * cutter.spec_rows
    used += (2 * per_block * batch + 2 * events + batch * pair_cap) * rows + events * nch + 3 * NFFT
    return pl.pallas_call(
        kernel,
        out_shape=(jax.ShapeDtypeStruct(shape, jnp.float32), jax.ShapeDtypeStruct(shape, jnp.bfloat16)),
        in_specs=[VMEM_ONLY] * (sources + 4 + (ready > 0)),
        out_specs=(VMEM_ONLY, VMEM_ONLY),
        scratch_shapes=[
            pltpu.VMEM(((regions - ready) * tiles * rows, LANES), jnp.float32),
            pltpu.VMEM((batch, 2, per_block * rows, LANES), jnp.float32),
            pltpu.VMEM((2 * events * rows, LANES), jnp.float32),
            pltpu.VMEM((batch * pair_cap * rows, LANES), jnp.float32),
            pltpu.VMEM((regions, index_rows, LANES), jnp.int32),
            pltpu.SMEM((regions, index_rows, LANES), jnp.int32),
            pltpu.VMEM((2, regions, LANES, slots), jnp.float32),
            pltpu.SemaphoreType.DMA(()),
        ],
        compiler_params=pltpu.CompilerParams(vmem_limit_bytes=grant(used)),
        name="correlate",
    )


def assemble(whole, other, pair_cap):
    rest = LAGS - HALF_ROWS

    def kernel(whole, other, stack, profile):
        first = lax.axis_index("chan") == 0
        low = jnp.where(first, whole[...], other[...])
        high = jnp.where(first, other[...], whole[...])
        stack[:HALF_ROWS, :] = low[:, :pair_cap]
        stack[HALF_ROWS:, :] = high[:rest, :pair_cap]
        profile[:HALF_ROWS, :] = low[:, pair_cap:]
        profile[HALF_ROWS:, :] = high[:rest, pair_cap:]

    width = whole.shape[1]
    return pl.pallas_call(
        kernel,
        out_shape=(jax.ShapeDtypeStruct((LAGS, pair_cap), jnp.float32),
                   jax.ShapeDtypeStruct((LAGS, width - pair_cap), jnp.float32)),
        in_specs=[VMEM_ONLY] * 2,
        out_specs=(VMEM_ONLY, VMEM_ONLY),
        compiler_params=pltpu.CompilerParams(vmem_limit_bytes=grant(4 * LAG_ROWS * width // LANES)),
        name="assemble",
    )(whole, other)


def on_device(archive, starts, event_owner, station_mask, pair_first, pair_second, pair_count):
    regions = lax.axis_size("region")
    chans = lax.axis_size("chan")
    chan_index = lax.axis_index("chan")
    per_block = starts.shape[0]
    pair_cap = pair_first.shape[0]
    stations = archive.shape[0]
    segment = archive.shape[2]
    bucket = max(2, 2 * per_block // regions)
    slots = regions * bucket
    share = station_share(stations, chans)
    nch = 4 * -(-share * COMP // (4 * regions))

    mask = station_mask.T
    blocks = pack(archive, starts.reshape(1, -1), mask, pair_first.reshape(1, -1),
                  pair_second.reshape(1, -1), pair_count, regions, chans, nch)
    received = exchange(blocks, regions)

    slot_of = slot_table(event_owner, regions, per_block, bucket, slots).reshape(1, -1)
    channel = lax.axis_index("region") * nch + jnp.arange(nch, dtype=jnp.int32)
    local = jnp.minimum(chan_index * share, stations - share) + channel // COMP
    used = (channel < share * COMP) & (local >= chan_index * share)
    station = jnp.where(used, lax.axis_index("stn") * stations + local, -1)

    slot_event, weight_rows = describe(mask, station, slot_of, regions, slots, nch)
    table = forward_table()
    ready = 2 if regions == 4 else 0
    spectra = []
    if ready:
        spectra = [early_spectra(received[:ready], weight_rows, table, regions, per_block, pair_cap, segment, nch)]
    kept, given = correlate(regions, per_block, pair_cap, segment, slots, nch, ready)(
        *received, *spectra, slot_event, weight_rows, table, lag_table())

    swap = [(0, 1), (1, 0)]
    swapped = lax.ppermute(given, "chan", swap)
    if separate(regions):
        sums = [kept[m] + swapped[m].astype(jnp.float32) for m in range(regions)]
        moved = exchange([term.astype(jnp.bfloat16) for term in sums], regions)
        whole = sums[0]
        for term in moved[1:]:
            whole = whole + term.astype(jnp.float32)
    else:
        moved = exchange([(kept + swapped.astype(jnp.float32)).astype(jnp.bfloat16)], regions)
        whole = jnp.sum(moved[0].astype(jnp.float32), axis=0)
    count = lax.axis_size("stn")
    step = 1
    while step < count:
        sent = whole.astype(jnp.bfloat16)
        other = lax.ppermute(sent, "stn", [(i, i ^ step) for i in range(count)])
        whole = sent.astype(jnp.float32) + other.astype(jnp.float32)
        step *= 2
    other = lax.ppermute(whole, "chan", swap)
    return assemble(whole, other, pair_cap)


def solution(mesh):
    placed = (
        P("stn", None, ("groups", "region")),
        P(("groups", "region")),
        P("groups"),
        P("groups", None),
        P(("groups", "region")),
        P(("groups", "region")),
        P(("groups", "region")),
    )
    return jax.shard_map(
        on_device,
        mesh=mesh,
        in_specs=placed,
        out_specs=(P(None, ("groups", "region")), P(None, ("groups", "region"))),
        check_vma=False,
    )
```

```python
import math

import jax
import jax.numpy as jnp
import numpy as np
from jax import lax
from jax.experimental import pallas as pl
from jax.experimental.pallas import tpu as pltpu
from jax.sharding import PartitionSpec as P

COMP = 3
WIN = 400
MAXLAG = 50
NFFT = 512
LAGS = 101
BINS = NFFT // 2
LANES = 128
HALF_LAGS = 51
HALF_ROWS = 56
TILE_ROWS = 48
VMEM_ONLY = pl.BlockSpec(memory_space=pltpu.VMEM)
SMEM_ONLY = pl.BlockSpec(memory_space=pltpu.SMEM)
NT = (((1,), (1,)), ((), ()))
TN = (((0,), (0,)), ((), ()))


def forward_table():
    sample = np.arange(NFFT)[:, None]
    freq = np.arange(BINS)[None, :]
    angle = (sample * freq % NFFT) * (2.0 * math.pi / NFFT)
    sine = np.sin(angle)
    sine[:, 0] = np.cos(math.pi * (np.arange(NFFT) % 2))
    table = np.concatenate([np.cos(angle), sine], axis=1)
    table[WIN:] = 0.0
    return jnp.asarray(table, jnp.float32).astype(jnp.bfloat16)


def lag_table():
    shift = np.arange(2 * HALF_LAGS)[:, None] - MAXLAG
    freq = np.arange(BINS)[None, :]
    angle = (freq * shift % NFFT) * (2.0 * math.pi / NFFT)
    weight = np.where(freq == 0, 1.0 / NFFT, 2.0 / NFFT)
    even = weight * np.cos(angle)
    odd = -weight * np.sin(angle)
    odd[:, 0] = (np.cos(math.pi * (shift[:, 0] % 2)) - 1.0) / NFFT
    table = np.concatenate([even, odd], axis=1) * math.sqrt(WIN)
    table[LAGS:] = 0.0
    gap = np.zeros((HALF_ROWS - HALF_LAGS, NFFT))
    filler = np.zeros((LANES - 2 * HALF_ROWS, NFFT))
    halves = [np.concatenate([table[:HALF_LAGS], gap]), np.concatenate([table[HALF_LAGS:], gap])]
    table = np.stack([np.concatenate([halves[c], halves[1 - c], filler]) for c in range(2)])
    table = jnp.asarray(table, jnp.float32)
    high = table.astype(jnp.bfloat16)
    return jnp.concatenate([high, (table - high.astype(jnp.float32)).astype(jnp.bfloat16)], axis=1)


def slot_table(event_owner, regions, per_block, bucket, slots):
    blocks = event_owner.reshape(regions, per_block)
    owned = blocks[:, :, None] == jnp.arange(regions, dtype=jnp.int32)[None, None, :]
    onehot = owned.astype(jnp.int32)
    before = jnp.cumsum(onehot, axis=1) - onehot
    ranking = jnp.sum(before * onehot, axis=2)
    block_index = jnp.arange(regions, dtype=jnp.int32)[:, None]
    return (blocks * slots + block_index * bucket + ranking).reshape(-1)


def as_bf16(flags):
    return flags.astype(jnp.float32).astype(jnp.bfloat16)


def digits_of(value):
    return (value >> 7).astype(jnp.float32).astype(jnp.bfloat16), (value & 127).astype(jnp.float32).astype(jnp.bfloat16)


def folded_rows(width):
    tiles = width // LANES
    return -(-HALF_LAGS * tiles // 16) * 16


def fold(value, store, first, tiles):
    for k in range(value.shape[1] // LANES):
        piece = value[:HALF_LAGS, k * LANES : (k + 1) * LANES]
        t = first + k
        store[t * TILE_ROWS : (t + 1) * TILE_ROWS, :] = piece[:TILE_ROWS]
        row = tiles * TILE_ROWS + t * (HALF_LAGS - TILE_ROWS)
        store[row : row + HALF_LAGS - TILE_ROWS, :] = piece[TILE_ROWS:]


def digit_count(events):
    return 1 if events <= 256 else 2


def field_width(events, pair_cap):
    return -(-(2 * digit_count(events) + 2) // 4) * pair_cap


def separate(regions):
    return regions <= 4


def block_shapes(regions, shape, dtype):
    if separate(regions):
        return [jax.ShapeDtypeStruct(shape, dtype)] * regions
    return [jax.ShapeDtypeStruct((regions,) + shape, dtype)]


def exchange(blocks, regions):
    if separate(regions):
        masks = range(regions - 1, 0, -1)
        moved = {m: lax.ppermute(blocks[m], "region", [(i, i ^ m) for i in range(regions)]) for m in masks}
        return [blocks[0]] + [moved[m] for m in range(1, regions)]
    order = jnp.arange(regions, dtype=jnp.int32) ^ lax.axis_index("region")
    moved = lax.all_to_all(jnp.take(blocks[0], order, axis=0), "region", split_axis=0, concat_axis=0, tiled=True)
    return [jnp.take(moved, order, axis=0)]


def station_share(stations, chans):
    return -(-stations // chans)


def pack(archive, starts, station_mask, pair_first, pair_second, pair_count, regions, chans, nch):
    stations, _, segment = archive.shape
    events = station_mask.shape[1]
    per_block = starts.shape[1]
    pair_cap = pair_first.shape[1]
    share = station_share(stations, chans)
    number = regions if separate(regions) else 1

    def kernel(*refs):
        sources, count, outs, refs = refs[:5], refs[5], refs[6 : 6 + number], refs[6 + number :]
        flat, archive, starts, mask, first, second, sems = refs
        region = lax.axis_index("region")
        chan = lax.axis_index("chan")
        base = jnp.minimum(chan * share, stations - share)
        sources = (sources[0].at[pl.ds(base, share)],) + sources[1:]
        copies = [pltpu.make_async_copy(source, target, sems.at[k])
                  for k, (source, target) in enumerate(zip(sources, (archive, starts, mask, first, second)))]
        for copy in copies:
            copy.start()
        for copy in copies[1:]:
            copy.wait()
        names = lax.broadcasted_iota(jnp.int32, (events, pair_cap), 0)
        usable = mask[...].astype(jnp.float32).astype(jnp.bfloat16)
        chosen = [jnp.dot(usable, as_bf16(names == ref[...]), preferred_element_type=jnp.float32)
                  for ref in (first, second)]
        common = jnp.sum(chosen[0] * chosen[1], axis=0, keepdims=True)
        position = lax.broadcasted_iota(jnp.int32, (1, pair_cap), 1)
        code = jnp.where(position < count[0], common + 1.0, 0.0).astype(jnp.bfloat16)
        offset = digits_of(starts[...] - region * segment)
        used = [jnp.full((1, per_block), digit, jnp.int32) for digit in (count[0] >> 7, count[0] & 127)]
        used = [digit.astype(jnp.float32).astype(jnp.bfloat16) for digit in used]
        rest = jnp.zeros((1, pair_cap - 4 * per_block), jnp.bfloat16)
        scalars = jnp.concatenate(list(offset) + used + [rest], axis=1)
        if digit_count(events) == 1:
            fields = [first[...].astype(jnp.float32).astype(jnp.bfloat16), second[...].astype(jnp.float32).astype(jnp.bfloat16)]
        else:
            fields = list(digits_of(first[...]) + digits_of(second[...]))
        fields += [code, scalars]
        copies[0].wait()
        for block in range(share * COMP // nch, regions):
            flat[block] = jnp.zeros((nch, segment), jnp.float32)
        for station in range(share):
            data = archive[station].astype(jnp.float32)
            row = station * COMP
            while row < (station + 1) * COMP:
                end = min((row // nch + 1) * nch, (station + 1) * COMP)
                flat[row // nch, row % nch : row % nch + end - row, :] = data[row - station * COMP : end - station * COMP]
                row = end
        for m in range(regions):
            out = outs[m] if separate(regions) else outs[0].at[m]
            out[:, :segment] = flat[region ^ m].astype(jnp.bfloat16)
            for k, field in enumerate(fields):
                lane = segment + k // 4 * pair_cap
                out[k % 4 : k % 4 + 1, lane : lane + pair_cap] = field

    return pl.pallas_call(
        kernel,
        out_shape=block_shapes(regions, (nch, segment + field_width(events, pair_cap)), jnp.bfloat16),
        in_specs=[pl.BlockSpec(memory_space=pltpu.HBM)] * 5 + [SMEM_ONLY],
        out_specs=[VMEM_ONLY] * number,
        scratch_shapes=[
            pltpu.VMEM((regions, nch, segment), jnp.float32),
            pltpu.VMEM((share, COMP, segment), archive.dtype),
            pltpu.VMEM(starts.shape, jnp.int32),
            pltpu.VMEM(station_mask.shape, jnp.int32),
            pltpu.VMEM(pair_first.shape, jnp.int32),
            pltpu.VMEM(pair_first.shape, jnp.int32),
            pltpu.SemaphoreType.DMA((5,)),
        ],
        name="pack",
    )(archive, starts, station_mask, pair_first, pair_second, pair_count)


def describe(station_mask, station, slot_of, regions, slots, nch):
    events = station_mask.shape[1]
    per_block = events // regions

    def kernel(mask, station, slot_of, slot_event, weight_rows):
        region = lax.axis_index("region")
        listed = lax.broadcasted_iota(jnp.int32, (mask.shape[0], LANES), 0)
        usable = mask[...].astype(jnp.float32).astype(jnp.bfloat16)
        for c in range(nch):
            value = lax.dot_general(usable, as_bf16(listed == station[c]), TN, preferred_element_type=jnp.float32)
            for part in range(regions):
                row = pl.multiple_of(((part ^ region) * nch + c) * per_block, per_block)
                weight_rows[pl.ds(row, per_block), :] = value[part * per_block : (part + 1) * per_block]
        names = digits_of(lax.broadcasted_iota(jnp.int32, (events, LANES), 0) + 1)
        place = lax.broadcasted_iota(jnp.int32, (slots, events), 0)
        slot_lane = slot_of[...]

        def one_region(part, carry):
            hit = as_bf16(place + part * slots == slot_lane)
            high, low = (jnp.dot(hit, digit, preferred_element_type=jnp.float32) for digit in names)
            event = high * 128.0 + low - 1.0
            slot_event[pl.ds(pl.multiple_of(part * slots, slots), slots), :] = event.astype(slot_event.dtype)
            return carry

        lax.fori_loop(0, regions, one_region, 0)

    return pl.pallas_call(
        kernel,
        out_shape=(jax.ShapeDtypeStruct((regions * slots, LANES), jnp.bfloat16 if digit_count(events) == 1 else jnp.float32),
                   jax.ShapeDtypeStruct((events * nch, LANES), jnp.float32)),
        in_specs=[VMEM_ONLY, SMEM_ONLY, VMEM_ONLY],
        out_specs=(VMEM_ONLY, VMEM_ONLY),
        compiler_params=pltpu.CompilerParams(vmem_limit_bytes=grant(regions * slots + 2 * events * nch)),
        name="describe",
    )(station_mask, station, slot_of)


def grant(rows):
    return min(rows * LANES * 4 * 5 // 4 + (4 << 20), 60 * 1024 * 1024)


class Cutter:
    def __init__(self, per_block, segment, nch):
        self.per_block, self.nch = per_block, nch
        self.rows = 2 * nch
        self.tiles = segment // LANES + 2
        self.count = per_block * nch
        self.spec_rows = 2 * self.rows * per_block

    def words(self, scalars, slot):
        tile, lane = scalars[:, : self.per_block], scalars[:, self.per_block : 2 * self.per_block]
        return ((tile + slot * self.tiles) * (256.0 * self.rows) + (LANES - lane)).astype(jnp.int32)

    def widen(self, source, shifted, slot):
        rows, nch = self.rows, self.nch
        first = slot * (self.tiles * rows)
        if not isinstance(slot, int):
            first = pl.multiple_of(first, rows)
        for k in range(self.tiles + 2):
            data = source[:, k * LANES : (k + 1) * LANES].astype(jnp.float32)
            if k < self.tiles:
                shifted[pl.ds(first + k * rows, nch, stride=2), :] = data
            if k >= 2:
                shifted[pl.ds(first + (k - 2) * rows + 1, nch, stride=2), :] = data

    def cut(self, word_of, shifted, windows, slot):
        rows = self.rows
        from_right = LANES - 1 - lax.broadcasted_iota(jnp.int32, (rows, LANES), 1)
        for event in range(self.per_block):
            word = word_of(event)
            first = pl.multiple_of(word >> 8, rows)
            turn = word & (2 * LANES - 1)
            data = [shifted[pl.ds(first + k * rows, rows), :] for k in range(3)]
            later = from_right < turn
            turn = turn & (LANES - 1)
            row = event * rows
            windows[slot, 0, row : row + rows, :] = pltpu.roll(jnp.where(later, data[0], data[1]), turn, 1)
            windows[slot, 1, row : row + rows, :] = pltpu.roll(jnp.where(later, data[1], data[2]), turn, 1)

    def transform(self, windows, slot, weight_rows, block, table, spec, place):
        per_block, nch, rows, count = self.per_block, self.nch, self.rows, self.count
        half = 2 * LANES
        inside = lax.broadcasted_iota(jnp.int32, (count, LANES), 1) < WIN - half - LANES
        pieces = [[jnp.concatenate([windows[slot, t, pl.ds(2 * c + k, per_block, stride=rows), :] for c in range(nch)])
                   for t in range(2)] for k in range(2)]
        squares = pieces[0][0] * pieces[0][0] + pieces[0][1] * pieces[0][1] + pieces[1][0] * pieces[1][0]
        squares += jnp.where(inside, pieces[1][1] * pieces[1][1], 0.0)
        energy = jnp.sum(squares, axis=1, keepdims=True)
        early, late = (jnp.concatenate(piece, axis=1).astype(jnp.bfloat16) for piece in pieces)
        coefs = jnp.dot(early, table[:half, :], preferred_element_type=jnp.float32)
        coefs += jnp.dot(late, table[half:, :], preferred_element_type=jnp.float32)
        first = block * count if isinstance(block, int) else pl.multiple_of(block * count, count)
        factor = weight_rows[pl.ds(first, count), :] * lax.rsqrt(energy + WIN * 1e-05)
        for s in range(2):
            for k in range(2):
                column = s * BINS + k * LANES
                piece = (coefs[:, column : column + LANES] * factor).astype(jnp.bfloat16).astype(jnp.float32)
                for c in range(nch):
                    row = place + s * rows + 2 * c + k
                    spec[pl.ds(row, per_block, stride=2 * rows), :] = piece[c * per_block : (c + 1) * per_block]


def scalar_field(events):
    return 2 * digit_count(events) + 1


def early_spectra(blocks, weight_rows, table, regions, per_block, pair_cap, segment, nch):
    cutter = Cutter(per_block, segment, nch)
    number = len(blocks)
    k = scalar_field(regions * per_block)

    def kernel(*refs):
        sources, refs = refs[:number], refs[number:]
        weight_rows, table, spec, shifted, windows, index_vmem, index, sem = refs
        for slot in range(number):
            lane = segment + k // 4 * pair_cap
            scalars = sources[slot][:, lane : lane + LANES].astype(jnp.float32)[k % 4 : k % 4 + 1]
            index_vmem[slot : slot + 1, :per_block] = cutter.words(scalars, slot)
        copy = pltpu.make_async_copy(index_vmem, index, sem)
        copy.start()
        for slot in range(number):
            cutter.widen(sources[slot], shifted, slot)
        copy.wait()

        def cut(slot, carry):
            cutter.cut(lambda event: index[slot, event], shifted, windows, slot)
            return carry

        lax.fori_loop(0, number, cut, 0)
        for slot in range(number):
            cutter.transform(windows, slot, weight_rows, slot, table, spec, slot * cutter.spec_rows)

    used = number * (cutter.spec_rows + (cutter.tiles + 2 * per_block) * cutter.rows + 2 * segment * nch // LANES)
    return pl.pallas_call(
        kernel,
        out_shape=jax.ShapeDtypeStruct((number * cutter.spec_rows, LANES), jnp.float32),
        in_specs=[VMEM_ONLY] * (number + 2),
        out_specs=VMEM_ONLY,
        scratch_shapes=[
            pltpu.VMEM((number * cutter.tiles * cutter.rows, LANES), jnp.float32),
            pltpu.VMEM((number, 2, per_block * cutter.rows, LANES), jnp.float32),
            pltpu.VMEM((8, LANES), jnp.int32),
            pltpu.SMEM((8, LANES), jnp.int32),
            pltpu.SemaphoreType.DMA(()),
        ],
        compiler_params=pltpu.CompilerParams(vmem_limit_bytes=grant(used + weight_rows.shape[0] + 2 * NFFT)),
        name="early_spectra",
    )(*blocks, weight_rows, table)


def correlate(regions, per_block, pair_cap, segment, slots, nch, ready):
    cutter = Cutter(per_block, segment, nch)
    rows, tiles = cutter.rows, cutter.tiles
    events = regions * per_block
    cols = pair_cap // LANES
    width = cols + slots // LANES
    batch = regions if separate(regions) else 1
    digits = digit_count(events)
    static = separate(regions)
    sources = regions if static else 1
    shift = per_block.bit_length() - 1
    assert per_block == 1 << shift

    def kernel(*refs):
        received, refs = refs[:sources], refs[sources:]
        (ready_spec, slot_event, weight_rows, table, weights, kept, given, shifted, windows, spec, prod, index_vmem, index,
         profile, folded, sem) = refs if ready else (None,) + refs
        region = lax.axis_index("region")

        def recv(m):
            return received[m] if static else received[0].at[m]

        def field(part, k):
            lane = segment + k // 4 * pair_cap
            return recv(part)[:, lane : lane + pair_cap].astype(jnp.float32)[k % 4 : k % 4 + 1]

        def listed(part, k):
            if digits == 1:
                return field(part, k)
            return field(part, 2 * k) * 128.0 + field(part, 2 * k + 1)

        for part in range(regions):
            rows_out = []
            for k in range(2):
                event = (listed(part, k).astype(jnp.int32) ^ (region << shift)) * (2 * rows)
                rows_out += [event[:, c * LANES : (c + 1) * LANES] for c in range(cols)]
            scalars = field(part, scalar_field(events))
            rows_out += [scalars[:, LANES : 2 * LANES].astype(jnp.int32)]
            for row, value in enumerate(rows_out):
                index_vmem[part, row : row + 1, :] = value
            slot = part - ready if static else part
            index_vmem[part, 2 * cols + 1 : 2 * cols + 2, :per_block] = cutter.words(scalars, slot)
        copy = pltpu.make_async_copy(index_vmem, index, sem)
        copy.start()
        if static:
            if ready:
                spec[: ready * cutter.spec_rows, :] = ready_spec[...]
            for part in range(ready, regions):
                cutter.widen(recv(part), shifted, part - ready)
        else:
            def widen(part, carry):
                cutter.widen(recv(part), shifted, part)
                return carry

            lax.fori_loop(0, regions, widen, 0)
        copy.wait()

        def cut(slot, carry):
            cutter.cut(lambda event: index[slot + ready, 2 * cols + 1, event], shifted, windows, slot)
            return carry

        def cut_and_transform(part, carry):
            cutter.cut(lambda event: index[part, 2 * cols + 1, event], shifted, windows, 0)
            place = pl.multiple_of(part * cutter.spec_rows, cutter.spec_rows)
            cutter.transform(windows, 0, weight_rows, part, table, spec, place)
            return carry

        if static:
            lax.fori_loop(0, regions - ready, cut, 0)
            for part in range(ready, regions):
                cutter.transform(windows, part - ready, weight_rows, part, table, spec, part * cutter.spec_rows)
        else:
            lax.fori_loop(0, regions, cut_and_transform, 0)

        lane = lax.broadcasted_iota(jnp.int32, (rows, LANES), 1)
        sublane = lax.broadcasted_iota(jnp.int32, (rows, LANES), 0)
        chan = lax.axis_index("chan")
        special = (sublane % 2 == 0) & (lane == 0)
        upper = sublane < nch

        def one_group(group, carry):
            def some_pairs(member, row):
                part = group * batch + member
                for step in range(LANES):
                    a = pl.multiple_of(index[part, row, step], 2 * rows)
                    b = pl.multiple_of(index[part, cols + row, step], 2 * rows)
                    cos_a, sin_a = spec[pl.ds(a, rows), :], spec[pl.ds(a + rows, rows), :]
                    cos_b, sin_b = spec[pl.ds(b, rows), :], spec[pl.ds(b + rows, rows), :]
                    sines = sin_a * sin_b
                    even = cos_a * cos_b + sines
                    odd = jnp.where(special, sines, sin_a * cos_b - cos_a * sin_b)
                    even += pltpu.roll(even, nch, 0)
                    odd += pltpu.roll(odd, nch, 0)
                    place = pl.multiple_of(((member * cols + row) * LANES + step) * rows, rows)
                    prod[pl.ds(place, rows), :] = jnp.where(upper, even, odd)
                return member

            def pairs_of(member, inner):
                part = group * batch + member
                pairs = index[part, 2 * cols, 0] * LANES + index[part, 2 * cols, per_block]
                lax.fori_loop(0, jnp.minimum((pairs + LANES - 1) // LANES, cols), lambda row, m: some_pairs(m, row),
                              member)
                return inner

            lax.fori_loop(0, batch, pairs_of, 0)
            for member in range(batch):
                part = group * batch + member
                first_row = member * pair_cap * rows
                sums = []
                for k in (0, 1, nch, nch + 1):
                    total = prod[pl.ds(first_row + k, pair_cap, stride=rows), :]
                    for c in range(1, nch // 2):
                        total += prod[pl.ds(first_row + k + 2 * c, pair_cap, stride=rows), :]
                    sums.append(total.astype(jnp.bfloat16))
                both = lax.dot_general(weights[chan], jnp.concatenate(sums, axis=1), NT,
                                       preferred_element_type=jnp.float32)
                cross = both[:LANES] + both[LANES:]
                code = field(part, 2 * digits)
                live = jnp.maximum((code - 1.0) * COMP, 1.0)
                stack = jnp.where(code > 0.0, cross * lax.rsqrt(live), 0.0)
                fold(stack[:HALF_ROWS], kept.at[part], 0, width)
                fold(stack[HALF_ROWS:], folded.at[part], 0, width)
                first, second = listed(part, 0), listed(part, 1)
                stack = stack.astype(jnp.bfloat16)

                def hot(owner, event):
                    column = slot_event[pl.ds(pl.multiple_of(owner * slots, slots), slots), :]
                    column = jnp.concatenate([column] * cols, axis=1)
                    if digits > 1:
                        return as_bf16(column == event)
                    event = jnp.broadcast_to(event.astype(jnp.bfloat16), column.shape)
                    return jnp.where(column == event, jnp.ones((), jnp.bfloat16), jnp.zeros((), jnp.bfloat16))

                owner = part ^ region
                after = (owner + 1) & (regions - 1)
                hots = jnp.concatenate([hot(owner, first), hot(owner, second), hot(after, second)], axis=0)
                terms = lax.dot_general(stack, hots, NT, preferred_element_type=jnp.float32)
                profile[0, part] = terms[:, :slots]
                profile[1, part] = terms[:, slots : 2 * slots]
                profile[2, after ^ region] = terms[:, 2 * slots :]
            return carry

        if static:
            one_group(0, 0)
        else:
            lax.fori_loop(0, regions, one_group, 0)
        def lag_of(axis):
            row = lax.broadcasted_iota(jnp.int32, (LANES, LANES), axis)
            return jnp.where(row < HALF_ROWS, row + chan * HALF_LAGS, row - HALF_ROWS + (1 - chan) * HALF_LAGS)

        mirror = as_bf16(lag_of(0) + lag_of(1) == LAGS - 1)

        def finish(part, carry):
            value = profile[1, part] + profile[2, part]
            high = value.astype(jnp.bfloat16)
            low = (value - high.astype(jnp.float32)).astype(jnp.bfloat16)
            flipped = jnp.dot(mirror, high, preferred_element_type=jnp.float32) + jnp.dot(
                mirror, low, preferred_element_type=jnp.float32)
            total = profile[0, part] + flipped
            fold(total[:HALF_ROWS], kept.at[part], cols, width)
            fold(total[HALF_ROWS:], folded.at[part], cols, width)
            given[part] = folded[part].astype(jnp.bfloat16)
            return carry

        lax.fori_loop(0, regions, finish, 0)

    shape = (regions, folded_rows(pair_cap + slots), LANES)
    index_rows = 8 * -(-(2 * cols + 2) // 8)
    used = regions * (tiles * rows + 3 * HALF_ROWS * width + 3 * LANES + index_rows + 4 * tiles + slots) + ready * cutter.spec_rows
    used += (2 * per_block * batch + 2 * events + batch * pair_cap) * rows + events * nch + 3 * NFFT
    return pl.pallas_call(
        kernel,
        out_shape=(jax.ShapeDtypeStruct(shape, jnp.float32), jax.ShapeDtypeStruct(shape, jnp.bfloat16)),
        in_specs=[VMEM_ONLY] * (sources + 4 + (ready > 0)),
        out_specs=(VMEM_ONLY, VMEM_ONLY),
        scratch_shapes=[
            pltpu.VMEM(((regions - ready) * tiles * rows, LANES), jnp.float32),
            pltpu.VMEM((batch, 2, per_block * rows, LANES), jnp.float32),
            pltpu.VMEM((2 * events * rows, LANES), jnp.float32),
            pltpu.VMEM((batch * pair_cap * rows, LANES), jnp.float32),
            pltpu.VMEM((regions, index_rows, LANES), jnp.int32),
            pltpu.SMEM((regions, index_rows, LANES), jnp.int32),
            pltpu.VMEM((3, regions, LANES, slots), jnp.float32),
            pltpu.VMEM(shape, jnp.float32),
            pltpu.SemaphoreType.DMA(()),
        ],
        compiler_params=pltpu.CompilerParams(vmem_limit_bytes=grant(used)),
        name="correlate",
    )


def assemble(whole, other, pair_cap, slots):
    tiles = pair_cap // LANES + slots // LANES

    def kernel(whole, other, stack, profile):
        first = lax.axis_index("chan") == 0
        halves = jnp.where(first, whole[...], other[...]), jnp.where(first, other[...], whole[...])
        for t in range(tiles):
            out, column = (stack, t * LANES) if t * LANES < pair_cap else (profile, t * LANES - pair_cap)
            lanes = pl.ds(column, LANES)
            for h, half in enumerate(halves):
                lag = h * HALF_LAGS
                out[lag : lag + TILE_ROWS, lanes] = half[t * TILE_ROWS : (t + 1) * TILE_ROWS]
                row = tiles * TILE_ROWS + t * (HALF_LAGS - TILE_ROWS)
                count = min(HALF_LAGS, LAGS - lag) - TILE_ROWS
                out[lag + TILE_ROWS : lag + TILE_ROWS + count, lanes] = half[row : row + count]

    return pl.pallas_call(
        kernel,
        out_shape=(jax.ShapeDtypeStruct((LAGS, pair_cap), jnp.float32),
                   jax.ShapeDtypeStruct((LAGS, slots), jnp.float32)),
        in_specs=[VMEM_ONLY] * 2,
        out_specs=(VMEM_ONLY, VMEM_ONLY),
        compiler_params=pltpu.CompilerParams(vmem_limit_bytes=grant(8 * HALF_ROWS * tiles)),
        name="assemble",
    )(whole, other)


def on_device(archive, starts, event_owner, station_mask, pair_first, pair_second, pair_count):
    regions = lax.axis_size("region")
    chans = lax.axis_size("chan")
    chan_index = lax.axis_index("chan")
    per_block = starts.shape[0]
    pair_cap = pair_first.shape[0]
    stations = archive.shape[0]
    segment = archive.shape[2]
    bucket = max(2, 2 * per_block // regions)
    slots = regions * bucket
    share = station_share(stations, chans)
    nch = 4 * -(-share * COMP // (4 * regions))

    mask = station_mask.T
    blocks = pack(archive, starts.reshape(1, -1), mask, pair_first.reshape(1, -1),
                  pair_second.reshape(1, -1), pair_count, regions, chans, nch)
    received = exchange(blocks, regions)

    slot_of = slot_table(event_owner, regions, per_block, bucket, slots).reshape(1, -1)
    channel = lax.axis_index("region") * nch + jnp.arange(nch, dtype=jnp.int32)
    local = jnp.minimum(chan_index * share, stations - share) + channel // COMP
    used = (channel < share * COMP) & (local >= chan_index * share)
    station = jnp.where(used, lax.axis_index("stn") * stations + local, -1)

    slot_event, weight_rows = describe(mask, station, slot_of, regions, slots, nch)
    table = forward_table()
    ready = 2 if regions == 4 else 0
    spectra = []
    if ready:
        spectra = [early_spectra(received[:ready], weight_rows, table, regions, per_block, pair_cap, segment, nch)]
    kept, given = correlate(regions, per_block, pair_cap, segment, slots, nch, ready)(
        *received, *spectra, slot_event, weight_rows, table, lag_table())

    swap = [(0, 1), (1, 0)]
    swapped = lax.ppermute(given, "chan", swap)
    if separate(regions):
        sums = [kept[m] + swapped[m].astype(jnp.float32) for m in range(regions)]
        moved = exchange([term.astype(jnp.bfloat16) for term in sums], regions)
        whole = sums[0]
        for term in moved[1:]:
            whole = whole + term.astype(jnp.float32)
    else:
        moved = exchange([(kept + swapped.astype(jnp.float32)).astype(jnp.bfloat16)], regions)
        whole = jnp.sum(moved[0].astype(jnp.float32), axis=0)
    count = lax.axis_size("stn")
    step = 1
    while step < count:
        sent = whole.astype(jnp.bfloat16)
        other = lax.ppermute(sent, "stn", [(i, i ^ step) for i in range(count)])
        whole = sent.astype(jnp.float32) + other.astype(jnp.float32)
        step *= 2
    other = lax.ppermute(whole, "chan", swap)
    return assemble(whole, other, pair_cap, slots)


def solution(mesh):
    placed = (
        P("stn", None, ("groups", "region")),
        P(("groups", "region")),
        P("groups"),
        P("groups", None),
        P(("groups", "region")),
        P(("groups", "region")),
        P(("groups", "region")),
    )
    return jax.shard_map(
        on_device,
        mesh=mesh,
        in_specs=placed,
        out_specs=(P(None, ("groups", "region")), P(None, ("groups", "region"))),
        check_vma=False,
    )
```

```python
import math

import jax
import jax.numpy as jnp
import numpy as np
from jax import lax
from jax.experimental import pallas as pl
from jax.experimental.pallas import tpu as pltpu
from jax.sharding import PartitionSpec as P


COMP = 3
WIN = 400
MAXLAG = 50
NFFT = 512
LAGS = 101
BINS = NFFT // 2
LANES = 128
HALF_LAGS = 51
HALF_ROWS = 56
TILE_ROWS = 48
VMEM_ONLY = pl.BlockSpec(memory_space=pltpu.VMEM)
SMEM_ONLY = pl.BlockSpec(memory_space=pltpu.SMEM)
NT = (((1,), (1,)), ((), ()))
TN = (((0,), (0,)), ((), ()))


def forward_table():
    sample = np.arange(NFFT)[:, None]
    freq = np.arange(BINS)[None, :]
    angle = (sample * freq % NFFT) * (2.0 * math.pi / NFFT)
    sine = np.sin(angle)
    sine[:, 0] = np.cos(math.pi * (np.arange(NFFT) % 2))
    table = np.concatenate([np.cos(angle), sine], axis=1)
    table[WIN:] = 0.0
    return jnp.asarray(table, jnp.float32).astype(jnp.bfloat16)


def lag_table():
    shift = np.arange(2 * HALF_LAGS)[:, None] - MAXLAG
    freq = np.arange(BINS)[None, :]
    angle = (freq * shift % NFFT) * (2.0 * math.pi / NFFT)
    weight = np.where(freq == 0, 1.0 / NFFT, 2.0 / NFFT)
    even = weight * np.cos(angle)
    odd = -weight * np.sin(angle)
    odd[:, 0] = (np.cos(math.pi * (shift[:, 0] % 2)) - 1.0) / NFFT
    table = np.concatenate([even, odd], axis=1) * math.sqrt(WIN)
    table[LAGS:] = 0.0
    gap = np.zeros((HALF_ROWS - HALF_LAGS, NFFT))
    filler = np.zeros((LANES - 2 * HALF_ROWS, NFFT))
    halves = [np.concatenate([table[:HALF_LAGS], gap]), np.concatenate([table[HALF_LAGS:], gap])]
    table = np.stack([np.concatenate([halves[c], halves[1 - c], filler]) for c in range(2)])
    table = jnp.asarray(table, jnp.float32)
    high = table.astype(jnp.bfloat16)
    return jnp.concatenate([high, (table - high.astype(jnp.float32)).astype(jnp.bfloat16)], axis=1)


def slot_table(event_owner, regions, per_block, bucket, slots):
    blocks = event_owner.reshape(regions, per_block)
    owned = blocks[:, :, None] == jnp.arange(regions, dtype=jnp.int32)[None, None, :]
    onehot = owned.astype(jnp.int32)
    before = jnp.cumsum(onehot, axis=1) - onehot
    ranking = jnp.sum(before * onehot, axis=2)
    block_index = jnp.arange(regions, dtype=jnp.int32)[:, None]
    return (blocks * slots + block_index * bucket + ranking).reshape(-1)


def as_bf16(flags):
    return flags.astype(jnp.float32).astype(jnp.bfloat16)


def digits_of(value):
    return (value >> 7).astype(jnp.float32).astype(jnp.bfloat16), (value & 127).astype(jnp.float32).astype(jnp.bfloat16)


def folded_rows(width):
    tiles = width // LANES
    return -(-HALF_LAGS * tiles // 16) * 16


def fold(value, store, first, tiles):
    for k in range(value.shape[1] // LANES):
        piece = value[:HALF_LAGS, k * LANES : (k + 1) * LANES]
        t = first + k
        store[t * TILE_ROWS : (t + 1) * TILE_ROWS, :] = piece[:TILE_ROWS]
        row = tiles * TILE_ROWS + t * (HALF_LAGS - TILE_ROWS)
        store[row : row + HALF_LAGS - TILE_ROWS, :] = piece[TILE_ROWS:]


def digit_count(events):
    return 1 if events <= 256 else 2


def field_width(events, pair_cap):
    return -(-(2 * digit_count(events) + 2) // 4) * pair_cap


def separate(regions):
    return regions <= 4


def block_shapes(regions, shape, dtype):
    if separate(regions):
        return [jax.ShapeDtypeStruct(shape, dtype)] * regions
    return [jax.ShapeDtypeStruct((regions,) + shape, dtype)]


def exchange(blocks, regions):
    if separate(regions):
        moved = {}
        for m in range(regions - 1, 0, -1):
            moved[m] = lax.ppermute(blocks[m], "region", [(i, i ^ m) for i in range(regions)])
        return [blocks[0]] + [moved[m] for m in range(1, regions)]
    order = jnp.arange(regions, dtype=jnp.int32) ^ lax.axis_index("region")
    moved = lax.all_to_all(jnp.take(blocks[0], order, axis=0), "region", split_axis=0, concat_axis=0, tiled=True)
    return [jnp.take(moved, order, axis=0)]


def station_share(stations, chans):
    return -(-stations // chans)


def pack(archive, starts, station_mask, pair_first, pair_second, pair_count, regions, chans, nch):
    stations, _, segment = archive.shape
    events = station_mask.shape[1]
    per_block = starts.shape[1]
    pair_cap = pair_first.shape[1]
    share = station_share(stations, chans)
    number = regions if separate(regions) else 1

    def kernel(*refs):
        sources, count, outs, refs = refs[:5], refs[5], refs[6 : 6 + number], refs[6 + number :]
        flat, archive, starts, mask, first, second, sems = refs
        region = lax.axis_index("region")
        chan = lax.axis_index("chan")
        base = jnp.minimum(chan * share, stations - share)
        sources = (sources[0].at[pl.ds(base, share)],) + sources[1:]
        copies = [pltpu.make_async_copy(source, target, sems.at[k])
                  for k, (source, target) in enumerate(zip(sources, (archive, starts, mask, first, second)))]
        for copy in copies:
            copy.start()
        for copy in copies[1:]:
            copy.wait()
        names = lax.broadcasted_iota(jnp.int32, (events, pair_cap), 0)
        usable = mask[...].astype(jnp.float32).astype(jnp.bfloat16)
        chosen = [jnp.dot(usable, as_bf16(names == ref[...]), preferred_element_type=jnp.float32)
                  for ref in (first, second)]
        common = jnp.sum(chosen[0] * chosen[1], axis=0, keepdims=True)
        position = lax.broadcasted_iota(jnp.int32, (1, pair_cap), 1)
        code = jnp.where(position < count[0], common + 1.0, 0.0).astype(jnp.bfloat16)
        offset = digits_of(starts[...] - region * segment)
        used = [jnp.full((1, per_block), digit, jnp.int32) for digit in (count[0] >> 7, count[0] & 127)]
        used = [digit.astype(jnp.float32).astype(jnp.bfloat16) for digit in used]
        rest = jnp.zeros((1, pair_cap - 4 * per_block), jnp.bfloat16)
        scalars = jnp.concatenate(list(offset) + used + [rest], axis=1)
        if digit_count(events) == 1:
            fields = [first[...].astype(jnp.float32).astype(jnp.bfloat16), second[...].astype(jnp.float32).astype(jnp.bfloat16)]
        else:
            fields = list(digits_of(first[...]) + digits_of(second[...]))
        fields += [code, scalars]
        copies[0].wait()
        for block in range(share * COMP // nch, regions):
            flat[block] = jnp.zeros((nch, segment), jnp.float32)
        for station in range(share):
            data = archive[station].astype(jnp.float32)
            row = station * COMP
            while row < (station + 1) * COMP:
                end = min((row // nch + 1) * nch, (station + 1) * COMP)
                flat[row // nch, row % nch : row % nch + end - row, :] = data[row - station * COMP : end - station * COMP]
                row = end
        for m in range(regions):
            out = outs[m] if separate(regions) else outs[0].at[m]
            out[:, :segment] = flat[region ^ m].astype(jnp.bfloat16)
            for k, field in enumerate(fields):
                lane = segment + k // 4 * pair_cap
                out[k % 4 : k % 4 + 1, lane : lane + pair_cap] = field

    return pl.pallas_call(
        kernel,
        out_shape=block_shapes(regions, (nch, segment + field_width(events, pair_cap)), jnp.bfloat16),
        in_specs=[pl.BlockSpec(memory_space=pltpu.HBM)] * 5 + [SMEM_ONLY],
        out_specs=[VMEM_ONLY] * number,
        scratch_shapes=[
            pltpu.VMEM((regions, nch, segment), jnp.float32),
            pltpu.VMEM((share, COMP, segment), archive.dtype),
            pltpu.VMEM(starts.shape, jnp.int32),
            pltpu.VMEM(station_mask.shape, jnp.int32),
            pltpu.VMEM(pair_first.shape, jnp.int32),
            pltpu.VMEM(pair_first.shape, jnp.int32),
            pltpu.SemaphoreType.DMA((5,)),
        ],
        name="pack",
    )(archive, starts, station_mask, pair_first, pair_second, pair_count)


def describe(station_mask, station, slot_of, regions, slots, nch):
    events = station_mask.shape[1]
    per_block = events // regions

    def kernel(mask, station, slot_of, slot_event, weight_rows):
        region = lax.axis_index("region")
        listed = lax.broadcasted_iota(jnp.int32, (mask.shape[0], LANES), 0)
        usable = mask[...].astype(jnp.float32).astype(jnp.bfloat16)
        for c in range(nch):
            value = lax.dot_general(usable, as_bf16(listed == station[c]), TN, preferred_element_type=jnp.float32)
            for part in range(regions):
                row = pl.multiple_of(((part ^ region) * nch + c) * per_block, per_block)
                weight_rows[pl.ds(row, per_block), :] = value[part * per_block : (part + 1) * per_block]
        names = digits_of(lax.broadcasted_iota(jnp.int32, (events, LANES), 0) + 1)
        place = lax.broadcasted_iota(jnp.int32, (slots, events), 0)
        slot_lane = slot_of[...]

        def one_region(part, carry):
            hit = as_bf16(place + part * slots == slot_lane)
            high, low = (jnp.dot(hit, digit, preferred_element_type=jnp.float32) for digit in names)
            event = high * 128.0 + low - 1.0
            slot_event[pl.ds(pl.multiple_of(part * slots, slots), slots), :] = event.astype(slot_event.dtype)
            return carry

        lax.fori_loop(0, regions, one_region, 0)

    return pl.pallas_call(
        kernel,
        out_shape=(jax.ShapeDtypeStruct((regions * slots, LANES), jnp.bfloat16 if digit_count(events) == 1 else jnp.float32),
                   jax.ShapeDtypeStruct((events * nch, LANES), jnp.float32)),
        in_specs=[VMEM_ONLY, SMEM_ONLY, VMEM_ONLY],
        out_specs=(VMEM_ONLY, VMEM_ONLY),
        compiler_params=pltpu.CompilerParams(vmem_limit_bytes=grant(regions * slots + 2 * events * nch)),
        name="describe",
    )(station_mask, station, slot_of)


def grant(rows):
    return min(rows * LANES * 4 * 5 // 4 + (4 << 20), 60 * 1024 * 1024)


class Cutter:
    def __init__(self, per_block, segment, nch):
        self.per_block, self.nch = per_block, nch
        self.rows = 2 * nch
        self.tiles = segment // LANES + 2
        self.count = per_block * nch
        self.spec_rows = 2 * self.rows * per_block

    def words(self, scalars, slot):
        tile, lane = scalars[:, : self.per_block], scalars[:, self.per_block : 2 * self.per_block]
        return ((tile + slot * self.tiles) * (256.0 * self.rows) + (LANES - lane)).astype(jnp.int32)

    def widen(self, source, shifted, slot):
        rows, nch = self.rows, self.nch
        first = slot * (self.tiles * rows)
        if not isinstance(slot, int):
            first = pl.multiple_of(first, rows)
        for k in range(self.tiles + 2):
            data = source[:, k * LANES : (k + 1) * LANES].astype(jnp.float32)
            if k < self.tiles:
                shifted[pl.ds(first + k * rows, nch, stride=2), :] = data
            if k >= 2:
                shifted[pl.ds(first + (k - 2) * rows + 1, nch, stride=2), :] = data

    def cut(self, word_of, shifted, windows, slot):
        rows = self.rows
        from_right = LANES - 1 - lax.broadcasted_iota(jnp.int32, (rows, LANES), 1)
        for event in range(self.per_block):
            word = word_of(event)
            first = pl.multiple_of(word >> 8, rows)
            turn = word & (2 * LANES - 1)
            data = [shifted[pl.ds(first + k * rows, rows), :] for k in range(3)]
            later = from_right < turn
            turn = turn & (LANES - 1)
            row = event * rows
            windows[slot, 0, row : row + rows, :] = pltpu.roll(jnp.where(later, data[0], data[1]), turn, 1)
            windows[slot, 1, row : row + rows, :] = pltpu.roll(jnp.where(later, data[1], data[2]), turn, 1)

    def transform(self, windows, slot, weight_rows, block, table, spec, place):
        per_block, nch, rows, count = self.per_block, self.nch, self.rows, self.count
        half = 2 * LANES
        inside = lax.broadcasted_iota(jnp.int32, (count, LANES), 1) < WIN - half - LANES
        pieces = [[jnp.concatenate([windows[slot, t, pl.ds(2 * c + k, per_block, stride=rows), :] for c in range(nch)])
                   for t in range(2)] for k in range(2)]
        squares = pieces[0][0] * pieces[0][0] + pieces[0][1] * pieces[0][1] + pieces[1][0] * pieces[1][0]
        squares += jnp.where(inside, pieces[1][1] * pieces[1][1], 0.0)
        energy = jnp.sum(squares, axis=1, keepdims=True)
        early, late = (jnp.concatenate(piece, axis=1).astype(jnp.bfloat16) for piece in pieces)
        coefs = jnp.dot(early, table[:half, :], preferred_element_type=jnp.float32)
        coefs += jnp.dot(late, table[half:, :], preferred_element_type=jnp.float32)
        first = block * count if isinstance(block, int) else pl.multiple_of(block * count, count)
        factor = weight_rows[pl.ds(first, count), :] * lax.rsqrt(energy + WIN * 1e-05)
        for s in range(2):
            for k in range(2):
                column = s * BINS + k * LANES
                piece = (coefs[:, column : column + LANES] * factor).astype(jnp.bfloat16).astype(jnp.float32)
                for c in range(nch):
                    row = place + s * rows + 2 * c + k
                    spec[pl.ds(row, per_block, stride=2 * rows), :] = piece[c * per_block : (c + 1) * per_block]


def scalar_field(events):
    return 2 * digit_count(events) + 1


def early_spectra(blocks, weight_rows, table, regions, per_block, pair_cap, segment, nch):
    cutter = Cutter(per_block, segment, nch)
    number = len(blocks)
    k = scalar_field(regions * per_block)

    def kernel(*refs):
        sources, refs = refs[:number], refs[number:]
        weight_rows, table, spec, shifted, windows, index_vmem, index, sem = refs
        for slot in range(number):
            lane = segment + k // 4 * pair_cap
            scalars = sources[slot][:, lane : lane + LANES].astype(jnp.float32)[k % 4 : k % 4 + 1]
            index_vmem[slot : slot + 1, :per_block] = cutter.words(scalars, slot)
        copy = pltpu.make_async_copy(index_vmem, index, sem)
        copy.start()
        for slot in range(number):
            cutter.widen(sources[slot], shifted, slot)
        copy.wait()

        def cut(slot, carry):
            cutter.cut(lambda event: index[slot, event], shifted, windows, slot)
            return carry

        lax.fori_loop(0, number, cut, 0)
        for slot in range(number):
            cutter.transform(windows, slot, weight_rows, slot, table, spec, slot * cutter.spec_rows)

    used = number * (cutter.spec_rows + (cutter.tiles + 2 * per_block) * cutter.rows + 2 * segment * nch // LANES)
    return pl.pallas_call(
        kernel,
        out_shape=jax.ShapeDtypeStruct((number * cutter.spec_rows, LANES), jnp.float32),
        in_specs=[VMEM_ONLY] * (number + 2),
        out_specs=VMEM_ONLY,
        scratch_shapes=[
            pltpu.VMEM((number * cutter.tiles * cutter.rows, LANES), jnp.float32),
            pltpu.VMEM((number, 2, per_block * cutter.rows, LANES), jnp.float32),
            pltpu.VMEM((8, LANES), jnp.int32),
            pltpu.SMEM((8, LANES), jnp.int32),
            pltpu.SemaphoreType.DMA(()),
        ],
        compiler_params=pltpu.CompilerParams(vmem_limit_bytes=grant(used + weight_rows.shape[0] + 2 * NFFT)),
        name="early_spectra",
    )(*blocks, weight_rows, table)


def correlate(regions, per_block, pair_cap, segment, slots, nch, ready):
    cutter = Cutter(per_block, segment, nch)
    rows, tiles = cutter.rows, cutter.tiles
    events = regions * per_block
    cols = pair_cap // LANES
    width = cols + slots // LANES
    batch = regions if separate(regions) else 1
    digits = digit_count(events)
    static = separate(regions)
    sources = regions if static else 1
    shift = per_block.bit_length() - 1
    assert per_block == 1 << shift

    def kernel(*refs):
        received, refs = refs[:sources], refs[sources:]
        (ready_spec, slot_event, weight_rows, table, weights, kept, given, shifted, windows, spec, prod, index_vmem, index,
         profile, folded, sem) = refs if ready else (None,) + refs
        region = lax.axis_index("region")

        def recv(m):
            return received[m] if static else received[0].at[m]

        def field(part, k):
            lane = segment + k // 4 * pair_cap
            return recv(part)[:, lane : lane + pair_cap].astype(jnp.float32)[k % 4 : k % 4 + 1]

        def listed(part, k):
            if digits == 1:
                return field(part, k)
            return field(part, 2 * k) * 128.0 + field(part, 2 * k + 1)

        for part in range(regions):
            rows_out = []
            for k in range(2):
                event = (listed(part, k).astype(jnp.int32) ^ (region << shift)) * (2 * rows)
                rows_out += [event[:, c * LANES : (c + 1) * LANES] for c in range(cols)]
            scalars = field(part, scalar_field(events))
            rows_out += [scalars[:, LANES : 2 * LANES].astype(jnp.int32)]
            for row, value in enumerate(rows_out):
                index_vmem[part, row : row + 1, :] = value
            slot = part - ready if static else part
            index_vmem[part, 2 * cols + 1 : 2 * cols + 2, :per_block] = cutter.words(scalars, slot)
        copy = pltpu.make_async_copy(index_vmem, index, sem)
        copy.start()
        if static:
            if ready:
                spec[: ready * cutter.spec_rows, :] = ready_spec[...]
            for part in range(ready, regions):
                cutter.widen(recv(part), shifted, part - ready)
        else:
            def widen(part, carry):
                cutter.widen(recv(part), shifted, part)
                return carry

            lax.fori_loop(0, regions, widen, 0)
        copy.wait()

        def cut(slot, carry):
            cutter.cut(lambda event: index[slot + ready, 2 * cols + 1, event], shifted, windows, slot)
            return carry

        def cut_and_transform(part, carry):
            cutter.cut(lambda event: index[part, 2 * cols + 1, event], shifted, windows, 0)
            place = pl.multiple_of(part * cutter.spec_rows, cutter.spec_rows)
            cutter.transform(windows, 0, weight_rows, part, table, spec, place)
            return carry

        if static:
            lax.fori_loop(0, regions - ready, cut, 0)
            for part in range(ready, regions):
                cutter.transform(windows, part - ready, weight_rows, part, table, spec, part * cutter.spec_rows)
        else:
            lax.fori_loop(0, regions, cut_and_transform, 0)

        lane = lax.broadcasted_iota(jnp.int32, (rows, LANES), 1)
        sublane = lax.broadcasted_iota(jnp.int32, (rows, LANES), 0)
        chan = lax.axis_index("chan")
        special = (sublane % 2 == 0) & (lane == 0)
        upper = sublane < nch

        def one_group(group, carry):
            def some_pairs(member, row):
                part = group * batch + member
                for step in range(LANES):
                    a = pl.multiple_of(index[part, row, step], 2 * rows)
                    b = pl.multiple_of(index[part, cols + row, step], 2 * rows)
                    cos_a, sin_a = spec[pl.ds(a, rows), :], spec[pl.ds(a + rows, rows), :]
                    cos_b, sin_b = spec[pl.ds(b, rows), :], spec[pl.ds(b + rows, rows), :]
                    sines = sin_a * sin_b
                    even = cos_a * cos_b + sines
                    odd = jnp.where(special, sines, sin_a * cos_b - cos_a * sin_b)
                    even += pltpu.roll(even, nch, 0)
                    odd += pltpu.roll(odd, nch, 0)
                    place = pl.multiple_of(((member * cols + row) * LANES + step) * rows, rows)
                    prod[pl.ds(place, rows), :] = jnp.where(upper, even, odd)
                return member

            def pairs_of(member, inner):
                part = group * batch + member
                pairs = index[part, 2 * cols, 0] * LANES + index[part, 2 * cols, per_block]
                lax.fori_loop(0, jnp.minimum((pairs + LANES - 1) // LANES, cols), lambda row, m: some_pairs(m, row),
                              member)
                return inner

            lax.fori_loop(0, batch, pairs_of, 0)
            for member in range(batch):
                part = group * batch + member
                first_row = member * pair_cap * rows
                sums = []
                for k in (0, 1, nch, nch + 1):
                    total = prod[pl.ds(first_row + k, pair_cap, stride=rows), :]
                    for c in range(1, nch // 2):
                        total += prod[pl.ds(first_row + k + 2 * c, pair_cap, stride=rows), :]
                    sums.append(total.astype(jnp.bfloat16))
                both = lax.dot_general(weights[chan], jnp.concatenate(sums, axis=1), NT,
                                       preferred_element_type=jnp.float32)
                cross = both[:LANES] + both[LANES:]
                code = field(part, 2 * digits)
                live = jnp.maximum((code - 1.0) * COMP, 1.0)
                stack = jnp.where(code > 0.0, cross * lax.rsqrt(live), 0.0)
                fold(stack[:HALF_ROWS], kept.at[part], 0, width)
                fold(stack[HALF_ROWS:], folded.at[part], 0, width)
                first, second = listed(part, 0), listed(part, 1)
                stack = stack.astype(jnp.bfloat16)

                def hot(owner, event):
                    column = slot_event[pl.ds(pl.multiple_of(owner * slots, slots), slots), :]
                    column = jnp.concatenate([column] * cols, axis=1)
                    if digits > 1:
                        return as_bf16(column == event)
                    event = jnp.broadcast_to(event.astype(jnp.bfloat16), column.shape)
                    return jnp.where(column == event, jnp.ones((), jnp.bfloat16), jnp.zeros((), jnp.bfloat16))

                owner = part ^ region
                after = (owner + 1) & (regions - 1)
                hots = jnp.concatenate([hot(owner, first), hot(owner, second), hot(after, second)], axis=0)
                terms = lax.dot_general(stack, hots, NT, preferred_element_type=jnp.float32)
                profile[0, part] = terms[:, :slots]
                profile[1, part] = terms[:, slots : 2 * slots]
                profile[2, after ^ region] = terms[:, 2 * slots :]
            return carry

        if static:
            one_group(0, 0)
        else:
            lax.fori_loop(0, regions, one_group, 0)

        def lag_of(axis):
            row = lax.broadcasted_iota(jnp.int32, (LANES, LANES), axis)
            return jnp.where(row < HALF_ROWS, row + chan * HALF_LAGS, row - HALF_ROWS + (1 - chan) * HALF_LAGS)

        mirror = as_bf16(lag_of(0) + lag_of(1) == LAGS - 1)

        def finish(part, carry):
            value = profile[1, part] + profile[2, part]
            high = value.astype(jnp.bfloat16)
            low = (value - high.astype(jnp.float32)).astype(jnp.bfloat16)
            flipped = jnp.dot(mirror, high, preferred_element_type=jnp.float32) + jnp.dot(
                mirror, low, preferred_element_type=jnp.float32)
            total = profile[0, part] + flipped
            fold(total[:HALF_ROWS], kept.at[part], cols, width)
            fold(total[HALF_ROWS:], folded.at[part], cols, width)
            given[part] = folded[part].astype(jnp.bfloat16)
            return carry

        lax.fori_loop(0, regions, finish, 0)

    shape = (regions, folded_rows(pair_cap + slots), LANES)
    index_rows = 8 * -(-(2 * cols + 2) // 8)
    used = regions * (tiles * rows + 3 * HALF_ROWS * width + 3 * LANES + index_rows + 4 * tiles + slots) + ready * cutter.spec_rows
    used += (2 * per_block * batch + 2 * events + batch * pair_cap) * rows + events * nch + 3 * NFFT
    return pl.pallas_call(
        kernel,
        out_shape=(jax.ShapeDtypeStruct(shape, jnp.float32), jax.ShapeDtypeStruct(shape, jnp.bfloat16)),
        in_specs=[VMEM_ONLY] * (sources + 4 + (ready > 0)),
        out_specs=(VMEM_ONLY, VMEM_ONLY),
        scratch_shapes=[
            pltpu.VMEM(((regions - ready) * tiles * rows, LANES), jnp.float32),
            pltpu.VMEM((batch, 2, per_block * rows, LANES), jnp.float32),
            pltpu.VMEM((2 * events * rows, LANES), jnp.float32),
            pltpu.VMEM((batch * pair_cap * rows, LANES), jnp.float32),
            pltpu.VMEM((regions, index_rows, LANES), jnp.int32),
            pltpu.SMEM((regions, index_rows, LANES), jnp.int32),
            pltpu.VMEM((3, regions, LANES, slots), jnp.float32),
            pltpu.VMEM(shape, jnp.float32),
            pltpu.SemaphoreType.DMA(()),
        ],
        compiler_params=pltpu.CompilerParams(vmem_limit_bytes=grant(used)),
        name="correlate",
    )


def assemble(whole, other, pair_cap, slots):
    tiles = pair_cap // LANES + slots // LANES

    def kernel(whole, other, stack, profile):
        first = lax.axis_index("chan") == 0
        halves = jnp.where(first, whole[...], other[...]), jnp.where(first, other[...], whole[...])
        for t in range(tiles):
            out, column = (stack, t * LANES) if t * LANES < pair_cap else (profile, t * LANES - pair_cap)
            lanes = pl.ds(column, LANES)
            for h, half in enumerate(halves):
                lag = h * HALF_LAGS
                out[lag : lag + TILE_ROWS, lanes] = half[t * TILE_ROWS : (t + 1) * TILE_ROWS]
                row = tiles * TILE_ROWS + t * (HALF_LAGS - TILE_ROWS)
                count = min(HALF_LAGS, LAGS - lag) - TILE_ROWS
                out[lag + TILE_ROWS : lag + TILE_ROWS + count, lanes] = half[row : row + count]

    return pl.pallas_call(
        kernel,
        out_shape=(jax.ShapeDtypeStruct((LAGS, pair_cap), jnp.float32),
                   jax.ShapeDtypeStruct((LAGS, slots), jnp.float32)),
        in_specs=[VMEM_ONLY] * 2,
        out_specs=(VMEM_ONLY, VMEM_ONLY),
        compiler_params=pltpu.CompilerParams(vmem_limit_bytes=grant(8 * HALF_ROWS * tiles)),
        name="assemble",
    )(whole, other)


def locate(archive, starts, event_owner, station_mask, pair_first, pair_second, pair_count):
    regions = lax.axis_size("region")
    chans = lax.axis_size("chan")
    chan_index = lax.axis_index("chan")
    per_block = starts.shape[0]
    pair_cap = pair_first.shape[0]
    stations = archive.shape[0]
    segment = archive.shape[2]
    bucket = max(2, 2 * per_block // regions)
    slots = regions * bucket
    share = station_share(stations, chans)
    nch = 4 * -(-share * COMP // (4 * regions))

    mask = station_mask.T
    blocks = pack(archive, starts.reshape(1, -1), mask, pair_first.reshape(1, -1),
                  pair_second.reshape(1, -1), pair_count, regions, chans, nch)
    received = exchange(blocks, regions)

    slot_of = slot_table(event_owner, regions, per_block, bucket, slots).reshape(1, -1)
    channel = lax.axis_index("region") * nch + jnp.arange(nch, dtype=jnp.int32)
    local = jnp.minimum(chan_index * share, stations - share) + channel // COMP
    used = (channel < share * COMP) & (local >= chan_index * share)
    station = jnp.where(used, lax.axis_index("stn") * stations + local, -1)

    slot_event, weight_rows = describe(mask, station, slot_of, regions, slots, nch)
    table = forward_table()
    ready = 1 if separate(regions) else 0
    spectra = []
    if ready:
        spectra = [early_spectra(received[:ready], weight_rows, table, regions, per_block, pair_cap, segment, nch)]
    kept, given = correlate(regions, per_block, pair_cap, segment, slots, nch, ready)(
        *received, *spectra, slot_event, weight_rows, table, lag_table())

    swap = [(0, 1), (1, 0)]
    swapped = lax.ppermute(given, "chan", swap)
    if separate(regions):
        sums = [kept[m] + swapped[m].astype(jnp.float32) for m in range(regions)]
        moved = exchange([term.astype(jnp.bfloat16) for term in sums], regions)
        whole = sums[0]
        for term in moved[1:]:
            whole = whole + term.astype(jnp.float32)
    else:
        moved = exchange([(kept + swapped.astype(jnp.float32)).astype(jnp.bfloat16)], regions)
        whole = jnp.sum(moved[0].astype(jnp.float32), axis=0)
    count = lax.axis_size("stn")
    step = 1
    while step < count:
        sent = whole.astype(jnp.bfloat16)
        other = lax.ppermute(sent, "stn", [(i, i ^ step) for i in range(count)])
        whole = sent.astype(jnp.float32) + other.astype(jnp.float32)
        step *= 2
    other = lax.ppermute(whole, "chan", swap)
    return assemble(whole, other, pair_cap, slots)


def solution(mesh):
    placed = (
        P("stn", None, ("groups", "region")),
        P(("groups", "region")),
        P("groups"),
        P("groups", None),
        P(("groups", "region")),
        P(("groups", "region")),
        P(("groups", "region")),
    )
    return jax.shard_map(
        locate,
        mesh=mesh,
        in_specs=placed,
        out_specs=(P(None, ("groups", "region")), P(None, ("groups", "region"))),
        check_vma=False,
    )
```

```python
import math

import jax
import jax.numpy as jnp
import numpy as np
from jax import lax
from jax.experimental import pallas as pl
from jax.experimental.pallas import tpu as pltpu
from jax.sharding import PartitionSpec as P


COMP = 3
WIN = 400
MAXLAG = 50
NFFT = 512
LAGS = 101
BINS = NFFT // 2
LANES = 128
HALF_LAGS = 51
HALF_ROWS = 56
TILE_ROWS = 48
VMEM_ONLY = pl.BlockSpec(memory_space=pltpu.VMEM)
SMEM_ONLY = pl.BlockSpec(memory_space=pltpu.SMEM)
NT = (((1,), (1,)), ((), ()))
TN = (((0,), (0,)), ((), ()))


def forward_table():
    sample = np.arange(NFFT)[:, None]
    freq = np.arange(BINS)[None, :]
    angle = (sample * freq % NFFT) * (2.0 * math.pi / NFFT)
    sine = np.sin(angle)
    sine[:, 0] = np.cos(math.pi * (np.arange(NFFT) % 2))
    table = np.concatenate([np.cos(angle), sine], axis=1)
    table[WIN:] = 0.0
    return jnp.asarray(table, jnp.float32).astype(jnp.bfloat16)


def lag_table():
    shift = np.arange(2 * HALF_LAGS)[:, None] - MAXLAG
    freq = np.arange(BINS)[None, :]
    angle = (freq * shift % NFFT) * (2.0 * math.pi / NFFT)
    weight = np.where(freq == 0, 1.0 / NFFT, 2.0 / NFFT)
    even = weight * np.cos(angle)
    odd = -weight * np.sin(angle)
    odd[:, 0] = (np.cos(math.pi * (shift[:, 0] % 2)) - 1.0) / NFFT
    table = np.concatenate([even, odd], axis=1) * math.sqrt(WIN)
    table[LAGS:] = 0.0
    gap = np.zeros((HALF_ROWS - HALF_LAGS, NFFT))
    filler = np.zeros((LANES - 2 * HALF_ROWS, NFFT))
    halves = [np.concatenate([table[:HALF_LAGS], gap]), np.concatenate([table[HALF_LAGS:], gap])]
    table = np.stack([np.concatenate([halves[c], halves[1 - c], filler]) for c in range(2)])
    table = jnp.asarray(table, jnp.float32)
    high = table.astype(jnp.bfloat16)
    return jnp.concatenate([high, (table - high.astype(jnp.float32)).astype(jnp.bfloat16)], axis=1)


def as_bf16(flags):
    return flags.astype(jnp.float32).astype(jnp.bfloat16)


def digits_of(value):
    return (value >> 7).astype(jnp.float32).astype(jnp.bfloat16), (value & 127).astype(jnp.float32).astype(jnp.bfloat16)


def folded_rows(width):
    tiles = width // LANES
    return -(-HALF_LAGS * tiles // 16) * 16


def fold(value, store, first, tiles):
    for k in range(value.shape[1] // LANES):
        piece = value[:HALF_LAGS, k * LANES : (k + 1) * LANES]
        t = first + k
        store[t * TILE_ROWS : (t + 1) * TILE_ROWS, :] = piece[:TILE_ROWS]
        row = tiles * TILE_ROWS + t * (HALF_LAGS - TILE_ROWS)
        store[row : row + HALF_LAGS - TILE_ROWS, :] = piece[TILE_ROWS:]


def digit_count(events):
    return 1 if events <= 256 else 2


def field_width(events, pair_cap):
    return -(-(2 * digit_count(events) + 2) // 4) * pair_cap


def separate(regions):
    return regions <= 4


def block_shapes(regions, shape, dtype):
    if separate(regions):
        return [jax.ShapeDtypeStruct(shape, dtype)] * regions
    return [jax.ShapeDtypeStruct((regions,) + shape, dtype)]


def exchange(blocks, regions):
    if separate(regions):
        moved = {}
        for m in range(regions - 1, 0, -1):
            moved[m] = lax.ppermute(blocks[m], "region", [(i, i ^ m) for i in range(regions)])
        return [blocks[0]] + [moved[m] for m in range(1, regions)]
    order = jnp.arange(regions, dtype=jnp.int32) ^ lax.axis_index("region")
    moved = lax.all_to_all(jnp.take(blocks[0], order, axis=0), "region", split_axis=0, concat_axis=0, tiled=True)
    return [jnp.take(moved, order, axis=0)]


def station_share(stations, chans):
    return -(-stations // chans)


def pack(archive, starts, station_mask, pair_first, pair_second, pair_count, regions, chans, nch):
    stations, _, segment = archive.shape
    events = station_mask.shape[1]
    per_block = starts.shape[1]
    pair_cap = pair_first.shape[1]
    share = station_share(stations, chans)
    number = regions if separate(regions) else 1

    def kernel(*refs):
        sources, count, outs, refs = refs[:5], refs[5], refs[6 : 6 + number], refs[6 + number :]
        flat, archive, starts, mask, first, second, sems = refs
        region = lax.axis_index("region")
        chan = lax.axis_index("chan")
        base = jnp.minimum(chan * share, stations - share)
        sources = (sources[0].at[pl.ds(base, share)],) + sources[1:]
        copies = [pltpu.make_async_copy(source, target, sems.at[k])
                  for k, (source, target) in enumerate(zip(sources, (archive, starts, mask, first, second)))]
        for copy in copies:
            copy.start()
        for copy in copies[1:]:
            copy.wait()
        names = lax.broadcasted_iota(jnp.int32, (events, pair_cap), 0)
        usable = mask[...].astype(jnp.float32).astype(jnp.bfloat16)
        chosen = [jnp.dot(usable, as_bf16(names == ref[...]), preferred_element_type=jnp.float32)
                  for ref in (first, second)]
        common = jnp.sum(chosen[0] * chosen[1], axis=0, keepdims=True)
        position = lax.broadcasted_iota(jnp.int32, (1, pair_cap), 1)
        code = jnp.where(position < count[0], common + 1.0, 0.0).astype(jnp.bfloat16)
        offset = digits_of(starts[...] - region * segment)
        used = [jnp.full((1, per_block), digit, jnp.int32) for digit in (count[0] >> 7, count[0] & 127)]
        used = [digit.astype(jnp.float32).astype(jnp.bfloat16) for digit in used]
        rest = jnp.zeros((1, pair_cap - 4 * per_block), jnp.bfloat16)
        scalars = jnp.concatenate(list(offset) + used + [rest], axis=1)
        if digit_count(events) == 1:
            fields = [first[...].astype(jnp.float32).astype(jnp.bfloat16), second[...].astype(jnp.float32).astype(jnp.bfloat16)]
        else:
            fields = list(digits_of(first[...]) + digits_of(second[...]))
        fields += [code, scalars]
        copies[0].wait()
        for block in range(share * COMP // nch, regions):
            flat[block] = jnp.zeros((nch, segment), jnp.float32)
        for station in range(share):
            data = archive[station].astype(jnp.float32)
            row = station * COMP
            while row < (station + 1) * COMP:
                end = min((row // nch + 1) * nch, (station + 1) * COMP)
                flat[row // nch, row % nch : row % nch + end - row, :] = data[row - station * COMP : end - station * COMP]
                row = end
        for m in range(regions):
            out = outs[m] if separate(regions) else outs[0].at[m]
            out[:, :segment] = flat[region ^ m].astype(jnp.bfloat16)
            for k, field in enumerate(fields):
                lane = segment + k // 4 * pair_cap
                out[k % 4 : k % 4 + 1, lane : lane + pair_cap] = field

    return pl.pallas_call(
        kernel,
        out_shape=block_shapes(regions, (nch, segment + field_width(events, pair_cap)), jnp.bfloat16),
        in_specs=[pl.BlockSpec(memory_space=pltpu.HBM)] * 5 + [SMEM_ONLY],
        out_specs=[VMEM_ONLY] * number,
        scratch_shapes=[
            pltpu.VMEM((regions, nch, segment), jnp.float32),
            pltpu.VMEM((share, COMP, segment), archive.dtype),
            pltpu.VMEM(starts.shape, jnp.int32),
            pltpu.VMEM(station_mask.shape, jnp.int32),
            pltpu.VMEM(pair_first.shape, jnp.int32),
            pltpu.VMEM(pair_first.shape, jnp.int32),
            pltpu.SemaphoreType.DMA((5,)),
        ],
        name="pack",
    )(archive, starts, station_mask, pair_first, pair_second, pair_count)


def grant(rows):
    return min(rows * LANES * 4 * 5 // 4 + (4 << 20), 60 * 1024 * 1024)


class Cutter:
    def __init__(self, per_block, segment, nch):
        self.per_block, self.nch = per_block, nch
        self.rows = 2 * nch
        self.tiles = segment // LANES + 2
        self.count = per_block * nch
        self.spec_rows = 2 * self.rows * per_block

    def words(self, scalars, slot):
        tile, lane = scalars[:, : self.per_block], scalars[:, self.per_block : 2 * self.per_block]
        return ((tile + slot * self.tiles) * (256.0 * self.rows) + (LANES - lane)).astype(jnp.int32)

    def widen(self, source, shifted, slot):
        rows, nch = self.rows, self.nch
        first = slot * (self.tiles * rows)
        if not isinstance(slot, int):
            first = pl.multiple_of(first, rows)
        for k in range(self.tiles + 2):
            data = source[:, k * LANES : (k + 1) * LANES].astype(jnp.float32)
            if k < self.tiles:
                shifted[pl.ds(first + k * rows, nch, stride=2), :] = data
            if k >= 2:
                shifted[pl.ds(first + (k - 2) * rows + 1, nch, stride=2), :] = data

    def cut(self, word_of, shifted, windows, slot):
        rows = self.rows
        from_right = LANES - 1 - lax.broadcasted_iota(jnp.int32, (rows, LANES), 1)
        for event in range(self.per_block):
            word = word_of(event)
            first = pl.multiple_of(word >> 8, rows)
            turn = word & (2 * LANES - 1)
            data = [shifted[pl.ds(first + k * rows, rows), :] for k in range(3)]
            later = from_right < turn
            turn = turn & (LANES - 1)
            row = event * rows
            windows[slot, 0, row : row + rows, :] = pltpu.roll(jnp.where(later, data[0], data[1]), turn, 1)
            windows[slot, 1, row : row + rows, :] = pltpu.roll(jnp.where(later, data[1], data[2]), turn, 1)

    def transform(self, windows, slot, weight_rows, block, table, spec, place):
        per_block, nch, rows, count = self.per_block, self.nch, self.rows, self.count
        half = 2 * LANES
        inside = lax.broadcasted_iota(jnp.int32, (count, LANES), 1) < WIN - half - LANES
        pieces = [[jnp.concatenate([windows[slot, t, pl.ds(2 * c + k, per_block, stride=rows), :] for c in range(nch)])
                   for t in range(2)] for k in range(2)]
        squares = pieces[0][0] * pieces[0][0] + pieces[0][1] * pieces[0][1] + pieces[1][0] * pieces[1][0]
        squares += jnp.where(inside, pieces[1][1] * pieces[1][1], 0.0)
        energy = jnp.sum(squares, axis=1, keepdims=True)
        early, late = (jnp.concatenate(piece, axis=1).astype(jnp.bfloat16) for piece in pieces)
        coefs = jnp.dot(early, table[:half, :], preferred_element_type=jnp.float32)
        coefs += jnp.dot(late, table[half:, :], preferred_element_type=jnp.float32)
        first = block * count if isinstance(block, int) else pl.multiple_of(block * count, count)
        factor = weight_rows[pl.ds(first, count), :] * lax.rsqrt(energy + WIN * 1e-05)
        for s in range(2):
            for k in range(2):
                column = s * BINS + k * LANES
                piece = (coefs[:, column : column + LANES] * factor).astype(jnp.bfloat16).astype(jnp.float32)
                for c in range(nch):
                    row = place + s * rows + 2 * c + k
                    spec[pl.ds(row, per_block, stride=2 * rows), :] = piece[c * per_block : (c + 1) * per_block]


def scalar_field(events):
    return 2 * digit_count(events) + 1


def prepare(blocks, station_mask, event_owner, table, regions, chans, stations, per_block, pair_cap, segment, bucket, nch):
    cutter = Cutter(per_block, segment, nch)
    number = len(blocks)
    events = regions * per_block
    slots = regions * bucket
    share = station_share(stations, chans)
    k = scalar_field(events)

    def kernel(*refs):
        sources, refs = refs[:number], refs[number:]
        mask, owners, table, slot_event, weight_rows = refs[:5]
        region = lax.axis_index("region")
        if number:
            spec, shifted, windows, index_vmem, index, sem = refs[5:]
            for slot in range(number):
                lane = segment + k // 4 * pair_cap
                scalars = sources[slot][:, lane : lane + LANES].astype(jnp.float32)[k % 4 : k % 4 + 1]
                index_vmem[slot : slot + 1, :per_block] = cutter.words(scalars, slot)
            copy = pltpu.make_async_copy(index_vmem, index, sem)
            copy.start()
            for slot in range(number):
                cutter.widen(sources[slot], shifted, slot)

        listed = lax.broadcasted_iota(jnp.int32, (mask.shape[0], LANES), 0)
        usable = mask[...].astype(jnp.float32).astype(jnp.bfloat16)
        chan = lax.axis_index("chan")
        for c in range(nch):
            channel = region * nch + c
            local = jnp.minimum(chan * share, stations - share) + channel // COMP
            used = (channel < share * COMP) & (local >= chan * share)
            station = jnp.where(used, lax.axis_index("stn") * stations + local, -1)
            value = lax.dot_general(usable, as_bf16(listed == station), TN, preferred_element_type=jnp.float32)
            for part in range(regions):
                row = pl.multiple_of(((part ^ region) * nch + c) * per_block, per_block)
                weight_rows[pl.ds(row, per_block), :] = value[part * per_block : (part + 1) * per_block]

        owner = owners[...]
        owner = jnp.concatenate([owner[:, s * per_block : (s + 1) * per_block] for s in range(regions)], axis=0)
        earlier = as_bf16(lax.broadcasted_iota(jnp.int32, (per_block, per_block), 0)
                          < lax.broadcasted_iota(jnp.int32, (per_block, per_block), 1))
        rank = jnp.zeros((regions, per_block), jnp.float32)
        for r in range(regions):
            flags = (owner == r).astype(jnp.float32)
            before = jnp.dot(flags.astype(jnp.bfloat16), earlier, preferred_element_type=jnp.float32)
            rank += flags * before
        in_segment = lax.broadcasted_iota(jnp.int32, (regions, per_block), 0) * bucket + rank.astype(jnp.int32)
        slot_of = owner * slots + in_segment
        slot_lane = jnp.concatenate([slot_of[s : s + 1] for s in range(regions)], axis=1)
        names = digits_of(lax.broadcasted_iota(jnp.int32, (events, LANES), 0) + 1)
        place = lax.broadcasted_iota(jnp.int32, (slots, events), 0)

        def one_region(part, carry):
            hit = as_bf16(place + part * slots == slot_lane)
            high, low = (jnp.dot(hit, digit, preferred_element_type=jnp.float32) for digit in names)
            event = high * 128.0 + low - 1.0
            slot_event[pl.ds(pl.multiple_of(part * slots, slots), slots), :] = event.astype(slot_event.dtype)
            return carry

        if separate(regions):
            for part in range(regions):
                one_region(part, 0)
        else:
            lax.fori_loop(0, regions, one_region, 0)
        if number:
            copy.wait()
            for slot in range(number):
                cutter.cut(lambda event, slot=slot: index[slot, event], shifted, windows, slot)
                cutter.transform(windows, slot, weight_rows, slot, table, spec, slot * cutter.spec_rows)

    shapes = [jax.ShapeDtypeStruct((regions * slots, LANES), jnp.bfloat16 if digit_count(events) == 1 else jnp.float32),
              jax.ShapeDtypeStruct((events * nch, LANES), jnp.float32)]
    scratch = []
    if number:
        shapes.append(jax.ShapeDtypeStruct((number * cutter.spec_rows, LANES), jnp.float32))
        scratch = [
            pltpu.VMEM((number * cutter.tiles * cutter.rows, LANES), jnp.float32),
            pltpu.VMEM((number, 2, per_block * cutter.rows, LANES), jnp.float32),
            pltpu.VMEM((8, LANES), jnp.int32),
            pltpu.SMEM((8, LANES), jnp.int32),
            pltpu.SemaphoreType.DMA(()),
        ]
    used = number * (cutter.spec_rows + (cutter.tiles + 2 * per_block) * cutter.rows + 2 * segment * nch // LANES)
    used += regions * slots + 2 * events * nch + 2 * NFFT + (1024 if separate(regions) else 0)
    return pl.pallas_call(
        kernel,
        out_shape=shapes,
        in_specs=[VMEM_ONLY] * (number + 3),
        out_specs=[VMEM_ONLY] * len(shapes),
        scratch_shapes=scratch,
        compiler_params=pltpu.CompilerParams(vmem_limit_bytes=grant(used)),
        name="prepare",
    )(*blocks, station_mask, event_owner, table)


def correlate(regions, per_block, pair_cap, segment, slots, nch, ready):
    cutter = Cutter(per_block, segment, nch)
    rows, tiles = cutter.rows, cutter.tiles
    events = regions * per_block
    cols = pair_cap // LANES
    width = cols + slots // LANES
    batch = regions if separate(regions) else 1
    digits = digit_count(events)
    static = separate(regions)
    sources = regions if static else 1
    shift = per_block.bit_length() - 1
    assert per_block == 1 << shift

    def kernel(*refs):
        received, refs = refs[:sources], refs[sources:]
        (ready_spec, slot_event, weight_rows, table, weights, kept, given, shifted, windows, spec, prod, index_vmem, index,
         profile, folded, sem) = refs if ready else (None,) + refs
        region = lax.axis_index("region")

        def recv(m):
            return received[m] if static else received[0].at[m]

        def field(part, k):
            lane = segment + k // 4 * pair_cap
            return recv(part)[:, lane : lane + pair_cap].astype(jnp.float32)[k % 4 : k % 4 + 1]

        def listed(part, k):
            if digits == 1:
                return field(part, k)
            return field(part, 2 * k) * 128.0 + field(part, 2 * k + 1)

        for part in range(regions):
            rows_out = []
            for k in range(2):
                event = (listed(part, k).astype(jnp.int32) ^ (region << shift)) * (2 * rows)
                rows_out += [event[:, c * LANES : (c + 1) * LANES] for c in range(cols)]
            scalars = field(part, scalar_field(events))
            rows_out += [scalars[:, LANES : 2 * LANES].astype(jnp.int32)]
            for row, value in enumerate(rows_out):
                index_vmem[part, row : row + 1, :] = value
            slot = part - ready if static else part
            index_vmem[part, 2 * cols + 1 : 2 * cols + 2, :per_block] = cutter.words(scalars, slot)
        copy = pltpu.make_async_copy(index_vmem, index, sem)
        copy.start()
        if static:
            if ready:
                spec[: ready * cutter.spec_rows, :] = ready_spec[...]
            for part in range(ready, regions):
                cutter.widen(recv(part), shifted, part - ready)
        else:
            def widen(part, carry):
                cutter.widen(recv(part), shifted, part)
                return carry

            lax.fori_loop(0, regions, widen, 0)
        copy.wait()

        def cut(slot, carry):
            cutter.cut(lambda event: index[slot + ready, 2 * cols + 1, event], shifted, windows, slot)
            return carry

        def cut_and_transform(part, carry):
            cutter.cut(lambda event: index[part, 2 * cols + 1, event], shifted, windows, 0)
            place = pl.multiple_of(part * cutter.spec_rows, cutter.spec_rows)
            cutter.transform(windows, 0, weight_rows, part, table, spec, place)
            return carry

        if static:
            lax.fori_loop(0, regions - ready, cut, 0)
            for part in range(ready, regions):
                cutter.transform(windows, part - ready, weight_rows, part, table, spec, part * cutter.spec_rows)
        else:
            lax.fori_loop(0, regions, cut_and_transform, 0)

        lane = lax.broadcasted_iota(jnp.int32, (rows, LANES), 1)
        sublane = lax.broadcasted_iota(jnp.int32, (rows, LANES), 0)
        chan = lax.axis_index("chan")
        special = (sublane % 2 == 0) & (lane == 0)
        upper = sublane < nch

        def one_group(group, carry):
            def some_pairs(member, row):
                part = group * batch + member
                for step in range(LANES):
                    a = pl.multiple_of(index[part, row, step], 2 * rows)
                    b = pl.multiple_of(index[part, cols + row, step], 2 * rows)
                    cos_a, sin_a = spec[pl.ds(a, rows), :], spec[pl.ds(a + rows, rows), :]
                    cos_b, sin_b = spec[pl.ds(b, rows), :], spec[pl.ds(b + rows, rows), :]
                    sines = sin_a * sin_b
                    even = cos_a * cos_b + sines
                    odd = jnp.where(special, sines, sin_a * cos_b - cos_a * sin_b)
                    even += pltpu.roll(even, nch, 0)
                    odd += pltpu.roll(odd, nch, 0)
                    place = pl.multiple_of(((member * cols + row) * LANES + step) * rows, rows)
                    prod[pl.ds(place, rows), :] = jnp.where(upper, even, odd)
                return member

            def pairs_of(member, inner):
                part = group * batch + member
                pairs = index[part, 2 * cols, 0] * LANES + index[part, 2 * cols, per_block]
                lax.fori_loop(0, jnp.minimum((pairs + LANES - 1) // LANES, cols), lambda row, m: some_pairs(m, row),
                              member)
                return inner

            lax.fori_loop(0, batch, pairs_of, 0)
            for member in range(batch):
                part = group * batch + member
                first_row = member * pair_cap * rows
                sums = []
                for k in (0, 1, nch, nch + 1):
                    total = prod[pl.ds(first_row + k, pair_cap, stride=rows), :]
                    for c in range(1, nch // 2):
                        total += prod[pl.ds(first_row + k + 2 * c, pair_cap, stride=rows), :]
                    sums.append(total.astype(jnp.bfloat16))
                both = lax.dot_general(weights[chan], jnp.concatenate(sums, axis=1), NT,
                                       preferred_element_type=jnp.float32)
                cross = both[:LANES] + both[LANES:]
                code = field(part, 2 * digits)
                live = jnp.maximum((code - 1.0) * COMP, 1.0)
                stack = jnp.where(code > 0.0, cross * lax.rsqrt(live), 0.0)
                fold(stack[:HALF_ROWS], kept.at[part], 0, width)
                fold(stack[HALF_ROWS:], folded.at[part], 0, width)
                first, second = listed(part, 0), listed(part, 1)
                stack = stack.astype(jnp.bfloat16)

                def hot(owner, event):
                    column = slot_event[pl.ds(pl.multiple_of(owner * slots, slots), slots), :]
                    column = jnp.concatenate([column] * cols, axis=1)
                    if digits > 1:
                        return as_bf16(column == event)
                    event = jnp.broadcast_to(event.astype(jnp.bfloat16), column.shape)
                    return jnp.where(column == event, jnp.ones((), jnp.bfloat16), jnp.zeros((), jnp.bfloat16))

                owner = part ^ region
                after = (owner + 1) & (regions - 1)
                hots = jnp.concatenate([hot(owner, first), hot(owner, second), hot(after, second)], axis=0)
                terms = lax.dot_general(stack, hots, NT, preferred_element_type=jnp.float32)
                profile[0, part] = terms[:, :slots]
                profile[1, part] = terms[:, slots : 2 * slots]
                profile[2, after ^ region] = terms[:, 2 * slots :]
            return carry

        if static:
            one_group(0, 0)
        else:
            lax.fori_loop(0, regions, one_group, 0)

        def lag_of(axis):
            row = lax.broadcasted_iota(jnp.int32, (LANES, LANES), axis)
            return jnp.where(row < HALF_ROWS, row + chan * HALF_LAGS, row - HALF_ROWS + (1 - chan) * HALF_LAGS)

        mirror = as_bf16(lag_of(0) + lag_of(1) == LAGS - 1)

        def finish(part, carry):
            value = profile[1, part] + profile[2, part]
            high = value.astype(jnp.bfloat16)
            low = (value - high.astype(jnp.float32)).astype(jnp.bfloat16)
            flipped = jnp.dot(mirror, high, preferred_element_type=jnp.float32) + jnp.dot(
                mirror, low, preferred_element_type=jnp.float32)
            total = profile[0, part] + flipped
            fold(total[:HALF_ROWS], kept.at[part], cols, width)
            fold(total[HALF_ROWS:], folded.at[part], cols, width)
            given[part] = folded[part].astype(jnp.bfloat16)
            return carry

        lax.fori_loop(0, regions, finish, 0)

    shape = (regions, folded_rows(pair_cap + slots), LANES)
    index_rows = 8 * -(-(2 * cols + 2) // 8)
    used = regions * (tiles * rows + 3 * HALF_ROWS * width + 3 * LANES + index_rows + 4 * tiles + slots) + ready * cutter.spec_rows
    used += (2 * per_block * batch + 2 * events + batch * pair_cap) * rows + events * nch + 3 * NFFT
    return pl.pallas_call(
        kernel,
        out_shape=(jax.ShapeDtypeStruct(shape, jnp.float32), jax.ShapeDtypeStruct(shape, jnp.bfloat16)),
        in_specs=[VMEM_ONLY] * (sources + 4 + (ready > 0)),
        out_specs=(VMEM_ONLY, VMEM_ONLY),
        scratch_shapes=[
            pltpu.VMEM(((regions - ready) * tiles * rows, LANES), jnp.float32),
            pltpu.VMEM((batch, 2, per_block * rows, LANES), jnp.float32),
            pltpu.VMEM((2 * events * rows, LANES), jnp.float32),
            pltpu.VMEM((batch * pair_cap * rows, LANES), jnp.float32),
            pltpu.VMEM((regions, index_rows, LANES), jnp.int32),
            pltpu.SMEM((regions, index_rows, LANES), jnp.int32),
            pltpu.VMEM((3, regions, LANES, slots), jnp.float32),
            pltpu.VMEM(shape, jnp.float32),
            pltpu.SemaphoreType.DMA(()),
        ],
        compiler_params=pltpu.CompilerParams(vmem_limit_bytes=grant(used)),
        name="correlate",
    )


def assemble(whole, other, pair_cap, slots):
    tiles = pair_cap // LANES + slots // LANES

    def kernel(whole, other, stack, profile):
        first = lax.axis_index("chan") == 0
        halves = jnp.where(first, whole[...], other[...]), jnp.where(first, other[...], whole[...])
        for t in range(tiles):
            out, column = (stack, t * LANES) if t * LANES < pair_cap else (profile, t * LANES - pair_cap)
            lanes = pl.ds(column, LANES)
            for h, half in enumerate(halves):
                lag = h * HALF_LAGS
                out[lag : lag + TILE_ROWS, lanes] = half[t * TILE_ROWS : (t + 1) * TILE_ROWS]
                row = tiles * TILE_ROWS + t * (HALF_LAGS - TILE_ROWS)
                count = min(HALF_LAGS, LAGS - lag) - TILE_ROWS
                out[lag + TILE_ROWS : lag + TILE_ROWS + count, lanes] = half[row : row + count]

    return pl.pallas_call(
        kernel,
        out_shape=(jax.ShapeDtypeStruct((LAGS, pair_cap), jnp.float32),
                   jax.ShapeDtypeStruct((LAGS, slots), jnp.float32)),
        in_specs=[VMEM_ONLY] * 2,
        out_specs=(VMEM_ONLY, VMEM_ONLY),
        compiler_params=pltpu.CompilerParams(vmem_limit_bytes=grant(8 * HALF_ROWS * tiles)),
        name="assemble",
    )(whole, other)


def locate(archive, starts, event_owner, station_mask, pair_first, pair_second, pair_count):
    regions = lax.axis_size("region")
    chans = lax.axis_size("chan")
    per_block = starts.shape[0]
    pair_cap = pair_first.shape[0]
    stations = archive.shape[0]
    segment = archive.shape[2]
    bucket = max(2, 2 * per_block // regions)
    slots = regions * bucket
    share = station_share(stations, chans)
    nch = 4 * -(-share * COMP // (4 * regions))

    mask = station_mask.T
    blocks = pack(archive, starts.reshape(1, -1), mask, pair_first.reshape(1, -1),
                  pair_second.reshape(1, -1), pair_count, regions, chans, nch)
    received = exchange(blocks, regions)

    table = forward_table()
    ready = 1 if separate(regions) else 0
    slot_event, weight_rows, *spectra = prepare(
        received[:ready], mask, event_owner.reshape(1, -1), table, regions, chans, stations, per_block, pair_cap, segment,
        bucket, nch)
    kept, given = correlate(regions, per_block, pair_cap, segment, slots, nch, ready)(
        *received, *spectra, slot_event, weight_rows, table, lag_table())

    swap = [(0, 1), (1, 0)]
    swapped = lax.ppermute(given, "chan", swap)
    if separate(regions):
        sums = [kept[m] + swapped[m].astype(jnp.float32) for m in range(regions)]
        moved = exchange([term.astype(jnp.bfloat16) for term in sums], regions)
        whole = sums[0]
        for term in moved[1:]:
            whole = whole + term.astype(jnp.float32)
    else:
        moved = exchange([(kept + swapped.astype(jnp.float32)).astype(jnp.bfloat16)], regions)
        whole = jnp.sum(moved[0].astype(jnp.float32), axis=0)
    count = lax.axis_size("stn")
    step = 1
    while step < count:
        sent = whole.astype(jnp.bfloat16)
        other = lax.ppermute(sent, "stn", [(i, i ^ step) for i in range(count)])
        whole = sent.astype(jnp.float32) + other.astype(jnp.float32)
        step *= 2
    other = lax.ppermute(whole, "chan", swap)
    return assemble(whole, other, pair_cap, slots)


def solution(mesh):
    placed = (
        P("stn", None, ("groups", "region")),
        P(("groups", "region")),
        P("groups"),
        P("groups", None),
        P(("groups", "region")),
        P(("groups", "region")),
        P(("groups", "region")),
    )
    return jax.shard_map(
        locate,
        mesh=mesh,
        in_specs=placed,
        out_specs=(P(None, ("groups", "region")), P(None, ("groups", "region"))),
        check_vma=False,
    )
```

```python
import math

import jax
import jax.numpy as jnp
import numpy as np
from jax import lax
from jax.experimental import pallas as pl
from jax.experimental.pallas import tpu as pltpu
from jax.sharding import PartitionSpec as P


COMP = 3
WIN = 400
MAXLAG = 50
NFFT = 512
LAGS = 101
BINS = NFFT // 2
LANES = 128
HALF_LAGS = 51
HALF_ROWS = 56
TILE_ROWS = 48
VMEM_ONLY = pl.BlockSpec(memory_space=pltpu.VMEM)
SMEM_ONLY = pl.BlockSpec(memory_space=pltpu.SMEM)
NT = (((1,), (1,)), ((), ()))
TN = (((0,), (0,)), ((), ()))


def forward_table():
    sample = np.arange(NFFT)[:, None]
    freq = np.arange(BINS)[None, :]
    angle = (sample * freq % NFFT) * (2.0 * math.pi / NFFT)
    sine = np.sin(angle)
    sine[:, 0] = np.cos(math.pi * (np.arange(NFFT) % 2))
    table = np.concatenate([np.cos(angle), sine], axis=1)
    table[WIN:] = 0.0
    return jnp.asarray(table, jnp.float32).astype(jnp.bfloat16)


def lag_table():
    shift = np.arange(2 * HALF_LAGS)[:, None] - MAXLAG
    freq = np.arange(BINS)[None, :]
    angle = (freq * shift % NFFT) * (2.0 * math.pi / NFFT)
    weight = np.where(freq == 0, 1.0 / NFFT, 2.0 / NFFT)
    even = weight * np.cos(angle)
    odd = -weight * np.sin(angle)
    odd[:, 0] = (np.cos(math.pi * (shift[:, 0] % 2)) - 1.0) / NFFT
    table = np.concatenate([even, odd], axis=1) * math.sqrt(WIN)
    table[LAGS:] = 0.0
    gap = np.zeros((HALF_ROWS - HALF_LAGS, NFFT))
    filler = np.zeros((LANES - 2 * HALF_ROWS, NFFT))
    halves = [np.concatenate([table[:HALF_LAGS], gap]), np.concatenate([table[HALF_LAGS:], gap])]
    table = np.stack([np.concatenate([halves[c], halves[1 - c], filler]) for c in range(2)])
    table = jnp.asarray(table, jnp.float32)
    high = table.astype(jnp.bfloat16)
    return jnp.concatenate([high, (table - high.astype(jnp.float32)).astype(jnp.bfloat16)], axis=1)


def as_bf16(flags):
    return flags.astype(jnp.float32).astype(jnp.bfloat16)


def digits_of(value):
    return (value >> 7).astype(jnp.float32).astype(jnp.bfloat16), (value & 127).astype(jnp.float32).astype(jnp.bfloat16)


def folded_rows(width):
    tiles = width // LANES
    return -(-HALF_LAGS * tiles // 16) * 16


def fold(value, store, first, tiles):
    for k in range(value.shape[1] // LANES):
        piece = value[:HALF_LAGS, k * LANES : (k + 1) * LANES]
        t = first + k
        store[t * TILE_ROWS : (t + 1) * TILE_ROWS, :] = piece[:TILE_ROWS]
        row = tiles * TILE_ROWS + t * (HALF_LAGS - TILE_ROWS)
        store[row : row + HALF_LAGS - TILE_ROWS, :] = piece[TILE_ROWS:]


def digit_count(events):
    return 1 if events <= 256 else 2


def field_width(events, pair_cap):
    return -(-(2 * digit_count(events) + 2) // 4) * pair_cap


def separate(regions):
    return regions <= 4


def block_shapes(regions, shape, dtype):
    if separate(regions):
        return [jax.ShapeDtypeStruct(shape, dtype)] * regions
    return [jax.ShapeDtypeStruct((regions,) + shape, dtype)]


def exchange(blocks, regions):
    if separate(regions):
        moved = {}
        for m in range(regions - 1, 0, -1):
            moved[m] = lax.ppermute(blocks[m], "region", [(i, i ^ m) for i in range(regions)])
        return [blocks[0]] + [moved[m] for m in range(1, regions)]
    order = jnp.arange(regions, dtype=jnp.int32) ^ lax.axis_index("region")
    moved = lax.all_to_all(jnp.take(blocks[0], order, axis=0), "region", split_axis=0, concat_axis=0, tiled=True)
    return [jnp.take(moved, order, axis=0)]


def station_share(stations, chans):
    return -(-stations // chans)


def pack(archive, starts, station_mask, pair_first, pair_second, pair_count, regions, chans, nch):
    stations, _, segment = archive.shape
    events = station_mask.shape[1]
    per_block = starts.shape[1]
    pair_cap = pair_first.shape[1]
    share = station_share(stations, chans)
    number = regions if separate(regions) else 1

    def kernel(*refs):
        sources, count, outs, refs = refs[:5], refs[5], refs[6 : 6 + number], refs[6 + number :]
        flat, archive, starts, mask, first, second, sems = refs
        region = lax.axis_index("region")
        chan = lax.axis_index("chan")
        base = jnp.minimum(chan * share, stations - share)
        sources = (sources[0].at[pl.ds(base, share)],) + sources[1:]
        copies = [pltpu.make_async_copy(source, target, sems.at[k])
                  for k, (source, target) in enumerate(zip(sources, (archive, starts, mask, first, second)))]
        for copy in copies:
            copy.start()
        for copy in copies[1:]:
            copy.wait()
        names = lax.broadcasted_iota(jnp.int32, (events, pair_cap), 0)
        usable = mask[...].astype(jnp.float32).astype(jnp.bfloat16)
        chosen = [jnp.dot(usable, as_bf16(names == ref[...]), preferred_element_type=jnp.float32)
                  for ref in (first, second)]
        common = jnp.sum(chosen[0] * chosen[1], axis=0, keepdims=True)
        position = lax.broadcasted_iota(jnp.int32, (1, pair_cap), 1)
        code = jnp.where(position < count[0], common + 1.0, 0.0).astype(jnp.bfloat16)
        offset = digits_of(starts[...] - region * segment)
        used = [jnp.full((1, per_block), digit, jnp.int32) for digit in (count[0] >> 7, count[0] & 127)]
        used = [digit.astype(jnp.float32).astype(jnp.bfloat16) for digit in used]
        rest = jnp.zeros((1, pair_cap - 4 * per_block), jnp.bfloat16)
        scalars = jnp.concatenate(list(offset) + used + [rest], axis=1)
        if digit_count(events) == 1:
            fields = [first[...].astype(jnp.float32).astype(jnp.bfloat16), second[...].astype(jnp.float32).astype(jnp.bfloat16)]
        else:
            fields = list(digits_of(first[...]) + digits_of(second[...]))
        fields += [code, scalars]
        copies[0].wait()
        for block in range(share * COMP // nch, regions):
            flat[block] = jnp.zeros((nch, segment), jnp.float32)
        for station in range(share):
            data = archive[station].astype(jnp.float32)
            row = station * COMP
            while row < (station + 1) * COMP:
                end = min((row // nch + 1) * nch, (station + 1) * COMP)
                flat[row // nch, row % nch : row % nch + end - row, :] = data[row - station * COMP : end - station * COMP]
                row = end
        for m in range(regions):
            out = outs[m] if separate(regions) else outs[0].at[m]
            out[:, :segment] = flat[region ^ m].astype(jnp.bfloat16)
            for k, field in enumerate(fields):
                lane = segment + k // 4 * pair_cap
                out[k % 4 : k % 4 + 1, lane : lane + pair_cap] = field

    return pl.pallas_call(
        kernel,
        out_shape=block_shapes(regions, (nch, segment + field_width(events, pair_cap)), jnp.bfloat16),
        in_specs=[pl.BlockSpec(memory_space=pltpu.HBM)] * 5 + [SMEM_ONLY],
        out_specs=[VMEM_ONLY] * number,
        scratch_shapes=[
            pltpu.VMEM((regions, nch, segment), jnp.float32),
            pltpu.VMEM((share, COMP, segment), archive.dtype),
            pltpu.VMEM(starts.shape, jnp.int32),
            pltpu.VMEM(station_mask.shape, jnp.int32),
            pltpu.VMEM(pair_first.shape, jnp.int32),
            pltpu.VMEM(pair_first.shape, jnp.int32),
            pltpu.SemaphoreType.DMA((5,)),
        ],
        name="pack",
    )(archive, starts, station_mask, pair_first, pair_second, pair_count)


def grant(rows):
    return min(rows * LANES * 4 * 5 // 4 + (4 << 20), 60 * 1024 * 1024)


class Cutter:
    def __init__(self, per_block, segment, nch):
        self.per_block, self.nch = per_block, nch
        self.rows = 2 * nch
        self.tiles = segment // LANES + 2
        self.count = per_block * nch
        self.spec_rows = 2 * self.rows * per_block

    def words(self, scalars, slot):
        tile, lane = scalars[:, : self.per_block], scalars[:, self.per_block : 2 * self.per_block]
        return ((tile + slot * self.tiles) * (256.0 * self.rows) + (LANES - lane)).astype(jnp.int32)

    def widen(self, source, shifted, slot):
        rows, nch = self.rows, self.nch
        first = slot * (self.tiles * rows)
        if not isinstance(slot, int):
            first = pl.multiple_of(first, rows)
        group = self.tiles // 2 if self.tiles % 2 == 0 else self.tiles

        def some_tiles(step, carry):
            for k in range(group):
                tile = step * group + k
                row = pl.multiple_of(first + tile * rows, rows)
                for ahead in range(2):
                    lane = pl.multiple_of((tile + 2 * ahead) * LANES, LANES)
                    shifted[pl.ds(row + ahead, nch, stride=2), :] = source[:, pl.ds(lane, LANES)].astype(jnp.float32)
            return carry

        lax.fori_loop(0, self.tiles // group, some_tiles, 0)

    def cut(self, word_of, shifted, windows, slot):
        rows = self.rows
        from_right = LANES - 1 - lax.broadcasted_iota(jnp.int32, (rows, LANES), 1)
        for event in range(self.per_block):
            word = word_of(event)
            first = pl.multiple_of(word >> 8, rows)
            turn = word & (2 * LANES - 1)
            data = [shifted[pl.ds(first + k * rows, rows), :] for k in range(3)]
            later = from_right < turn
            turn = turn & (LANES - 1)
            row = event * rows
            windows[slot, 0, row : row + rows, :] = pltpu.roll(jnp.where(later, data[0], data[1]), turn, 1)
            windows[slot, 1, row : row + rows, :] = pltpu.roll(jnp.where(later, data[1], data[2]), turn, 1)

    def transform(self, windows, slot, weight_rows, block, table, spec, place):
        per_block, nch, rows, count = self.per_block, self.nch, self.rows, self.count
        half = 2 * LANES
        inside = lax.broadcasted_iota(jnp.int32, (count, LANES), 1) < WIN - half - LANES
        pieces = [[jnp.concatenate([windows[slot, t, pl.ds(2 * c + k, per_block, stride=rows), :] for c in range(nch)])
                   for t in range(2)] for k in range(2)]
        squares = pieces[0][0] * pieces[0][0] + pieces[0][1] * pieces[0][1] + pieces[1][0] * pieces[1][0]
        squares += jnp.where(inside, pieces[1][1] * pieces[1][1], 0.0)
        energy = jnp.sum(squares, axis=1, keepdims=True)
        early, late = (jnp.concatenate(piece, axis=1).astype(jnp.bfloat16) for piece in pieces)
        coefs = jnp.dot(early, table[:half, :], preferred_element_type=jnp.float32)
        coefs += jnp.dot(late, table[half:, :], preferred_element_type=jnp.float32)
        first = block * count if isinstance(block, int) else pl.multiple_of(block * count, count)
        factor = weight_rows[pl.ds(first, count), :] * lax.rsqrt(energy + WIN * 1e-05)
        for s in range(2):
            for k in range(2):
                column = s * BINS + k * LANES
                piece = (coefs[:, column : column + LANES] * factor).astype(jnp.bfloat16).astype(jnp.float32)
                for c in range(nch):
                    row = place + s * rows + 2 * c + k
                    spec[pl.ds(row, per_block, stride=2 * rows), :] = piece[c * per_block : (c + 1) * per_block]


def scalar_field(events):
    return 2 * digit_count(events) + 1


def prepare(blocks, station_mask, event_owner, table, regions, chans, stations, per_block, pair_cap, segment, bucket, nch):
    cutter = Cutter(per_block, segment, nch)
    number = len(blocks)
    events = regions * per_block
    slots = regions * bucket
    share = station_share(stations, chans)
    k = scalar_field(events)

    def kernel(*refs):
        sources, refs = refs[:number], refs[number:]
        mask, owners, table, slot_event, weight_rows = refs[:5]
        region = lax.axis_index("region")
        if number:
            spec, shifted, windows, index_vmem, index, sem = refs[5:]
            for slot in range(number):
                lane = segment + k // 4 * pair_cap
                scalars = sources[slot][:, lane : lane + LANES].astype(jnp.float32)[k % 4 : k % 4 + 1]
                index_vmem[slot : slot + 1, :per_block] = cutter.words(scalars, slot)
            copy = pltpu.make_async_copy(index_vmem, index, sem)
            copy.start()
            for slot in range(number):
                cutter.widen(sources[slot], shifted, slot)

        listed = lax.broadcasted_iota(jnp.int32, (mask.shape[0], LANES), 0)
        usable = mask[...].astype(jnp.float32).astype(jnp.bfloat16)
        chan = lax.axis_index("chan")
        for c in range(nch):
            channel = region * nch + c
            local = jnp.minimum(chan * share, stations - share) + channel // COMP
            used = (channel < share * COMP) & (local >= chan * share)
            station = jnp.where(used, lax.axis_index("stn") * stations + local, -1)
            value = lax.dot_general(usable, as_bf16(listed == station), TN, preferred_element_type=jnp.float32)
            for part in range(regions):
                row = pl.multiple_of(((part ^ region) * nch + c) * per_block, per_block)
                weight_rows[pl.ds(row, per_block), :] = value[part * per_block : (part + 1) * per_block]

        owner = owners[...]
        owner = jnp.concatenate([owner[:, s * per_block : (s + 1) * per_block] for s in range(regions)], axis=0)
        earlier = as_bf16(lax.broadcasted_iota(jnp.int32, (per_block, per_block), 0)
                          < lax.broadcasted_iota(jnp.int32, (per_block, per_block), 1))
        rank = jnp.zeros((regions, per_block), jnp.float32)
        for r in range(regions):
            flags = (owner == r).astype(jnp.float32)
            before = jnp.dot(flags.astype(jnp.bfloat16), earlier, preferred_element_type=jnp.float32)
            rank += flags * before
        in_segment = lax.broadcasted_iota(jnp.int32, (regions, per_block), 0) * bucket + rank.astype(jnp.int32)
        slot_of = owner * slots + in_segment
        slot_lane = jnp.concatenate([slot_of[s : s + 1] for s in range(regions)], axis=1)
        names = digits_of(lax.broadcasted_iota(jnp.int32, (events, LANES), 0) + 1)
        place = lax.broadcasted_iota(jnp.int32, (slots, events), 0)

        def one_region(part, carry):
            hit = as_bf16(place + part * slots == slot_lane)
            high, low = (jnp.dot(hit, digit, preferred_element_type=jnp.float32) for digit in names)
            event = high * 128.0 + low - 1.0
            slot_event[pl.ds(pl.multiple_of(part * slots, slots), slots), :] = event.astype(slot_event.dtype)
            return carry

        if separate(regions):
            for part in range(regions):
                one_region(part, 0)
        else:
            lax.fori_loop(0, regions, one_region, 0)
        if number:
            copy.wait()
            for slot in range(number):
                cutter.cut(lambda event, slot=slot: index[slot, event], shifted, windows, slot)
                cutter.transform(windows, slot, weight_rows, slot, table, spec, slot * cutter.spec_rows)

    shapes = [jax.ShapeDtypeStruct((regions * slots, LANES), jnp.bfloat16 if digit_count(events) == 1 else jnp.float32),
              jax.ShapeDtypeStruct((events * nch, LANES), jnp.float32)]
    scratch = []
    if number:
        shapes.append(jax.ShapeDtypeStruct((number * cutter.spec_rows, LANES), jnp.float32))
        scratch = [
            pltpu.VMEM((number * cutter.tiles * cutter.rows, LANES), jnp.float32),
            pltpu.VMEM((number, 2, per_block * cutter.rows, LANES), jnp.float32),
            pltpu.VMEM((8, LANES), jnp.int32),
            pltpu.SMEM((8, LANES), jnp.int32),
            pltpu.SemaphoreType.DMA(()),
        ]
    used = number * (cutter.spec_rows + (cutter.tiles + 2 * per_block) * cutter.rows + 2 * segment * nch // LANES)
    used += regions * slots + 2 * events * nch + 2 * NFFT + (1024 if separate(regions) else 0)
    return pl.pallas_call(
        kernel,
        out_shape=shapes,
        in_specs=[VMEM_ONLY] * (number + 3),
        out_specs=[VMEM_ONLY] * len(shapes),
        scratch_shapes=scratch,
        compiler_params=pltpu.CompilerParams(vmem_limit_bytes=grant(used)),
        name="prepare",
    )(*blocks, station_mask, event_owner, table)


def correlate(regions, per_block, pair_cap, segment, slots, nch, ready):
    cutter = Cutter(per_block, segment, nch)
    rows, tiles = cutter.rows, cutter.tiles
    events = regions * per_block
    cols = pair_cap // LANES
    width = cols + slots // LANES
    batch = regions if separate(regions) else 1
    digits = digit_count(events)
    static = separate(regions)
    sources = regions if static else 1
    shift = per_block.bit_length() - 1
    assert per_block == 1 << shift

    def kernel(*refs):
        received, refs = refs[:sources], refs[sources:]
        (ready_spec, slot_event, weight_rows, table, weights, kept, given, shifted, windows, spec, prod, index_vmem, index,
         profile, folded, sem) = refs if ready else (None,) + refs
        region = lax.axis_index("region")

        def recv(m):
            return received[m] if static else received[0].at[m]

        def field(part, k):
            lane = segment + k // 4 * pair_cap
            return recv(part)[:, lane : lane + pair_cap].astype(jnp.float32)[k % 4 : k % 4 + 1]

        def listed(part, k):
            if digits == 1:
                return field(part, k)
            return field(part, 2 * k) * 128.0 + field(part, 2 * k + 1)

        for part in range(regions):
            rows_out = []
            for k in range(2):
                event = (listed(part, k).astype(jnp.int32) ^ (region << shift)) * (2 * rows)
                rows_out += [event[:, c * LANES : (c + 1) * LANES] for c in range(cols)]
            scalars = field(part, scalar_field(events))
            rows_out += [scalars[:, LANES : 2 * LANES].astype(jnp.int32)]
            for row, value in enumerate(rows_out):
                index_vmem[part, row : row + 1, :] = value
            slot = part - ready if static else part
            index_vmem[part, 2 * cols + 1 : 2 * cols + 2, :per_block] = cutter.words(scalars, slot)
        copy = pltpu.make_async_copy(index_vmem, index, sem)
        copy.start()
        if static:
            if ready:
                spec[: ready * cutter.spec_rows, :] = ready_spec[...]
            for part in range(ready, regions):
                cutter.widen(recv(part), shifted, part - ready)
        else:
            def widen(part, carry):
                cutter.widen(recv(part), shifted, part)
                return carry

            lax.fori_loop(0, regions, widen, 0)
        copy.wait()

        def cut(slot, carry):
            cutter.cut(lambda event: index[slot + ready, 2 * cols + 1, event], shifted, windows, slot)
            return carry

        def cut_and_transform(part, carry):
            cutter.cut(lambda event: index[part, 2 * cols + 1, event], shifted, windows, 0)
            place = pl.multiple_of(part * cutter.spec_rows, cutter.spec_rows)
            cutter.transform(windows, 0, weight_rows, part, table, spec, place)
            return carry

        if static:
            lax.fori_loop(0, regions - ready, cut, 0)
            for part in range(ready, regions):
                cutter.transform(windows, part - ready, weight_rows, part, table, spec, part * cutter.spec_rows)
        else:
            lax.fori_loop(0, regions, cut_and_transform, 0)

        lane = lax.broadcasted_iota(jnp.int32, (rows, LANES), 1)
        sublane = lax.broadcasted_iota(jnp.int32, (rows, LANES), 0)
        chan = lax.axis_index("chan")
        special = (sublane % 2 == 0) & (lane == 0)
        upper = sublane < nch

        def one_group(group, carry):
            def some_pairs(member, row):
                part = group * batch + member
                for step in range(LANES):
                    a = pl.multiple_of(index[part, row, step], 2 * rows)
                    b = pl.multiple_of(index[part, cols + row, step], 2 * rows)
                    cos_a, sin_a = spec[pl.ds(a, rows), :], spec[pl.ds(a + rows, rows), :]
                    cos_b, sin_b = spec[pl.ds(b, rows), :], spec[pl.ds(b + rows, rows), :]
                    sines = sin_a * sin_b
                    even = cos_a * cos_b + sines
                    odd = jnp.where(special, sines, sin_a * cos_b - cos_a * sin_b)
                    even += pltpu.roll(even, nch, 0)
                    odd += pltpu.roll(odd, nch, 0)
                    place = pl.multiple_of(((member * cols + row) * LANES + step) * rows, rows)
                    prod[pl.ds(place, rows), :] = jnp.where(upper, even, odd)
                return member

            def pairs_of(member, inner):
                part = group * batch + member
                pairs = index[part, 2 * cols, 0] * LANES + index[part, 2 * cols, per_block]
                lax.fori_loop(0, jnp.minimum((pairs + LANES - 1) // LANES, cols), lambda row, m: some_pairs(m, row),
                              member)
                return inner

            lax.fori_loop(0, batch, pairs_of, 0)
            for member in range(batch):
                part = group * batch + member
                first_row = member * pair_cap * rows
                sums = []
                for k in (0, 1, nch, nch + 1):
                    total = prod[pl.ds(first_row + k, pair_cap, stride=rows), :]
                    for c in range(1, nch // 2):
                        total += prod[pl.ds(first_row + k + 2 * c, pair_cap, stride=rows), :]
                    sums.append(total.astype(jnp.bfloat16))
                both = lax.dot_general(weights[chan], jnp.concatenate(sums, axis=1), NT,
                                       preferred_element_type=jnp.float32)
                cross = both[:LANES] + both[LANES:]
                code = field(part, 2 * digits)
                live = jnp.maximum((code - 1.0) * COMP, 1.0)
                stack = jnp.where(code > 0.0, cross * lax.rsqrt(live), 0.0)
                fold(stack[:HALF_ROWS], kept.at[part], 0, width)
                fold(stack[HALF_ROWS:], folded.at[part], 0, width)
                first, second = listed(part, 0), listed(part, 1)
                stack = stack.astype(jnp.bfloat16)

                def hot(owner, event):
                    column = slot_event[pl.ds(pl.multiple_of(owner * slots, slots), slots), :]
                    column = jnp.concatenate([column] * cols, axis=1)
                    if digits > 1:
                        return as_bf16(column == event)
                    event = jnp.broadcast_to(event.astype(jnp.bfloat16), column.shape)
                    return jnp.where(column == event, jnp.ones((), jnp.bfloat16), jnp.zeros((), jnp.bfloat16))

                owner = part ^ region
                after = (owner + 1) & (regions - 1)
                hots = jnp.concatenate([hot(owner, first), hot(owner, second), hot(after, second)], axis=0)
                terms = lax.dot_general(stack, hots, NT, preferred_element_type=jnp.float32)
                profile[0, part] = terms[:, :slots]
                profile[1, part] = terms[:, slots : 2 * slots]
                profile[2, after ^ region] = terms[:, 2 * slots :]
            return carry

        if static:
            one_group(0, 0)
        else:
            lax.fori_loop(0, regions, one_group, 0)

        def lag_of(axis):
            row = lax.broadcasted_iota(jnp.int32, (LANES, LANES), axis)
            return jnp.where(row < HALF_ROWS, row + chan * HALF_LAGS, row - HALF_ROWS + (1 - chan) * HALF_LAGS)

        mirror = as_bf16(lag_of(0) + lag_of(1) == LAGS - 1)

        def finish(part, carry):
            value = profile[1, part] + profile[2, part]
            high = value.astype(jnp.bfloat16)
            low = (value - high.astype(jnp.float32)).astype(jnp.bfloat16)
            flipped = jnp.dot(mirror, high, preferred_element_type=jnp.float32) + jnp.dot(
                mirror, low, preferred_element_type=jnp.float32)
            total = profile[0, part] + flipped
            fold(total[:HALF_ROWS], kept.at[part], cols, width)
            fold(total[HALF_ROWS:], folded.at[part], cols, width)
            given[part] = folded[part].astype(jnp.bfloat16)
            return carry

        lax.fori_loop(0, regions, finish, 0)

    shape = (regions, folded_rows(pair_cap + slots), LANES)
    index_rows = 8 * -(-(2 * cols + 2) // 8)
    used = regions * (tiles * rows + 3 * HALF_ROWS * width + 3 * LANES + index_rows + 4 * tiles + slots) + ready * cutter.spec_rows
    used += (2 * per_block * batch + 2 * events + batch * pair_cap) * rows + events * nch + 3 * NFFT
    return pl.pallas_call(
        kernel,
        out_shape=(jax.ShapeDtypeStruct(shape, jnp.float32), jax.ShapeDtypeStruct(shape, jnp.bfloat16)),
        in_specs=[VMEM_ONLY] * (sources + 4 + (ready > 0)),
        out_specs=(VMEM_ONLY, VMEM_ONLY),
        scratch_shapes=[
            pltpu.VMEM(((regions - ready) * tiles * rows, LANES), jnp.float32),
            pltpu.VMEM((batch, 2, per_block * rows, LANES), jnp.float32),
            pltpu.VMEM((2 * events * rows, LANES), jnp.float32),
            pltpu.VMEM((batch * pair_cap * rows, LANES), jnp.float32),
            pltpu.VMEM((regions, index_rows, LANES), jnp.int32),
            pltpu.SMEM((regions, index_rows, LANES), jnp.int32),
            pltpu.VMEM((3, regions, LANES, slots), jnp.float32),
            pltpu.VMEM(shape, jnp.float32),
            pltpu.SemaphoreType.DMA(()),
        ],
        compiler_params=pltpu.CompilerParams(vmem_limit_bytes=grant(used)),
        name="correlate",
    )


def assemble(whole, other, pair_cap, slots):
    tiles = pair_cap // LANES + slots // LANES

    def kernel(whole, other, stack, profile):
        first = lax.axis_index("chan") == 0
        halves = jnp.where(first, whole[...], other[...]), jnp.where(first, other[...], whole[...])
        for t in range(tiles):
            out, column = (stack, t * LANES) if t * LANES < pair_cap else (profile, t * LANES - pair_cap)
            lanes = pl.ds(column, LANES)
            for h, half in enumerate(halves):
                lag = h * HALF_LAGS
                out[lag : lag + TILE_ROWS, lanes] = half[t * TILE_ROWS : (t + 1) * TILE_ROWS]
                row = tiles * TILE_ROWS + t * (HALF_LAGS - TILE_ROWS)
                count = min(HALF_LAGS, LAGS - lag) - TILE_ROWS
                out[lag + TILE_ROWS : lag + TILE_ROWS + count, lanes] = half[row : row + count]

    return pl.pallas_call(
        kernel,
        out_shape=(jax.ShapeDtypeStruct((LAGS, pair_cap), jnp.float32),
                   jax.ShapeDtypeStruct((LAGS, slots), jnp.float32)),
        in_specs=[VMEM_ONLY] * 2,
        out_specs=(VMEM_ONLY, VMEM_ONLY),
        compiler_params=pltpu.CompilerParams(vmem_limit_bytes=grant(8 * HALF_ROWS * tiles)),
        name="assemble",
    )(whole, other)


def locate(archive, starts, event_owner, station_mask, pair_first, pair_second, pair_count):
    regions = lax.axis_size("region")
    chans = lax.axis_size("chan")
    per_block = starts.shape[0]
    pair_cap = pair_first.shape[0]
    stations = archive.shape[0]
    segment = archive.shape[2]
    bucket = max(2, 2 * per_block // regions)
    slots = regions * bucket
    share = station_share(stations, chans)
    nch = 4 * -(-share * COMP // (4 * regions))

    mask = station_mask.T
    blocks = pack(archive, starts.reshape(1, -1), mask, pair_first.reshape(1, -1),
                  pair_second.reshape(1, -1), pair_count, regions, chans, nch)
    received = exchange(blocks, regions)

    table = forward_table()
    ready = 1 if separate(regions) else 0
    slot_event, weight_rows, *spectra = prepare(
        received[:ready], mask, event_owner.reshape(1, -1), table, regions, chans, stations, per_block, pair_cap, segment,
        bucket, nch)
    kept, given = correlate(regions, per_block, pair_cap, segment, slots, nch, ready)(
        *received, *spectra, slot_event, weight_rows, table, lag_table())

    swap = [(0, 1), (1, 0)]
    swapped = lax.ppermute(given, "chan", swap)
    if separate(regions):
        sums = [kept[m] + swapped[m].astype(jnp.float32) for m in range(regions)]
        moved = exchange([term.astype(jnp.bfloat16) for term in sums], regions)
        whole = sums[0]
        for term in moved[1:]:
            whole = whole + term.astype(jnp.float32)
    else:
        moved = exchange([(kept + swapped.astype(jnp.float32)).astype(jnp.bfloat16)], regions)
        whole = jnp.sum(moved[0].astype(jnp.float32), axis=0)
    count = lax.axis_size("stn")
    step = 1
    while step < count:
        sent = whole.astype(jnp.bfloat16)
        other = lax.ppermute(sent, "stn", [(i, i ^ step) for i in range(count)])
        whole = sent.astype(jnp.float32) + other.astype(jnp.float32)
        step *= 2
    other = lax.ppermute(whole, "chan", swap)
    return assemble(whole, other, pair_cap, slots)


def solution(mesh):
    placed = (
        P("stn", None, ("groups", "region")),
        P(("groups", "region")),
        P("groups"),
        P("groups", None),
        P(("groups", "region")),
        P(("groups", "region")),
        P(("groups", "region")),
    )
    return jax.shard_map(
        locate,
        mesh=mesh,
        in_specs=placed,
        out_specs=(P(None, ("groups", "region")), P(None, ("groups", "region"))),
        check_vma=False,
    )
```

```python
import math

import jax
import jax.numpy as jnp
import numpy as np
from jax import lax
from jax.experimental import pallas as pl
from jax.experimental.pallas import tpu as pltpu
from jax.sharding import PartitionSpec as P


COMP = 3
WIN = 400
MAXLAG = 50
NFFT = 512
LAGS = 101
BINS = NFFT // 2
LANES = 128
HALF_LAGS = 51
HALF_ROWS = 56
TILE_ROWS = 48
STEP_BITS = 7
STEP = 1 << STEP_BITS
VMEM_ONLY = pl.BlockSpec(memory_space=pltpu.VMEM)
SMEM_ONLY = pl.BlockSpec(memory_space=pltpu.SMEM)
NT = (((1,), (1,)), ((), ()))
TN = (((0,), (0,)), ((), ()))


def forward_table():
    sample = np.arange(NFFT)[:, None]
    freq = np.arange(BINS)[None, :]
    angle = (sample * freq % NFFT) * (2.0 * math.pi / NFFT)
    sine = np.sin(angle)
    sine[:, 0] = np.cos(math.pi * (np.arange(NFFT) % 2))
    table = np.concatenate([np.cos(angle), sine], axis=1)
    table[WIN:] = 0.0
    return jnp.asarray(table, jnp.float32).astype(jnp.bfloat16)


def lag_table():
    shift = np.arange(2 * HALF_LAGS)[:, None] - MAXLAG
    freq = np.arange(BINS)[None, :]
    angle = (freq * shift % NFFT) * (2.0 * math.pi / NFFT)
    weight = np.where(freq == 0, 1.0 / NFFT, 2.0 / NFFT)
    even = weight * np.cos(angle)
    odd = -weight * np.sin(angle)
    odd[:, 0] = (np.cos(math.pi * (shift[:, 0] % 2)) - 1.0) / NFFT
    table = np.concatenate([even, odd], axis=1) * math.sqrt(WIN)
    table[LAGS:] = 0.0
    gap = np.zeros((HALF_ROWS - HALF_LAGS, NFFT))
    filler = np.zeros((LANES - 2 * HALF_ROWS, NFFT))
    halves = [np.concatenate([table[:HALF_LAGS], gap]), np.concatenate([table[HALF_LAGS:], gap])]
    table = np.stack([np.concatenate([halves[c], halves[1 - c], filler]) for c in range(2)])
    table = jnp.asarray(table, jnp.float32)
    high = table.astype(jnp.bfloat16)
    return jnp.concatenate([high, (table - high.astype(jnp.float32)).astype(jnp.bfloat16)], axis=1)


def as_bf16(flags):
    return flags.astype(jnp.float32).astype(jnp.bfloat16)


def digits_of(value):
    return (value >> 7).astype(jnp.float32).astype(jnp.bfloat16), (value & 127).astype(jnp.float32).astype(jnp.bfloat16)


def folded_rows(width):
    tiles = width // LANES
    return -(-HALF_LAGS * tiles // 16) * 16


def fold(value, store, first, tiles):
    for k in range(value.shape[1] // LANES):
        piece = value[:HALF_LAGS, k * LANES : (k + 1) * LANES]
        t = first + k
        store[t * TILE_ROWS : (t + 1) * TILE_ROWS, :] = piece[:TILE_ROWS]
        row = tiles * TILE_ROWS + t * (HALF_LAGS - TILE_ROWS)
        store[row : row + HALF_LAGS - TILE_ROWS, :] = piece[TILE_ROWS:]


def digit_count(events):
    return 1 if events <= 256 else 2


def field_width(events, pair_cap):
    return -(-(2 * digit_count(events) + 2) // 4) * pair_cap


def separate(regions):
    return regions <= 4


def block_shapes(regions, shape, dtype):
    if separate(regions):
        return [jax.ShapeDtypeStruct(shape, dtype)] * regions
    return [jax.ShapeDtypeStruct((regions,) + shape, dtype)]


def exchange(blocks, regions):
    if separate(regions):
        moved = {}
        for m in range(regions - 1, 0, -1):
            moved[m] = lax.ppermute(blocks[m], "region", [(i, i ^ m) for i in range(regions)])
        return [blocks[0]] + [moved[m] for m in range(1, regions)]
    order = jnp.arange(regions, dtype=jnp.int32) ^ lax.axis_index("region")
    moved = lax.all_to_all(jnp.take(blocks[0], order, axis=0), "region", split_axis=0, concat_axis=0, tiled=True)
    return [jnp.take(moved, order, axis=0)]


def station_share(stations, chans):
    return -(-stations // chans)


def pack(archive, starts, station_mask, pair_first, pair_second, pair_count, regions, chans, nch):
    stations, _, segment = archive.shape
    events = station_mask.shape[1]
    per_block = starts.shape[1]
    pair_cap = pair_first.shape[1]
    share = station_share(stations, chans)
    number = regions if separate(regions) else 1

    def kernel(*refs):
        sources, count, outs, refs = refs[:5], refs[5], refs[6 : 6 + number], refs[6 + number :]
        flat, archive, starts, mask, first, second, sems = refs
        region = lax.axis_index("region")
        chan = lax.axis_index("chan")
        base = jnp.minimum(chan * share, stations - share)
        sources = (sources[0].at[pl.ds(base, share)],) + sources[1:]
        copies = [pltpu.make_async_copy(source, target, sems.at[k])
                  for k, (source, target) in enumerate(zip(sources, (archive, starts, mask, first, second)))]
        for copy in copies:
            copy.start()
        for copy in copies[1:]:
            copy.wait()
        names = lax.broadcasted_iota(jnp.int32, (events, pair_cap), 0)
        usable = mask[...].astype(jnp.float32).astype(jnp.bfloat16)
        chosen = [jnp.dot(usable, as_bf16(names == ref[...]), preferred_element_type=jnp.float32)
                  for ref in (first, second)]
        common = jnp.sum(chosen[0] * chosen[1], axis=0, keepdims=True)
        position = lax.broadcasted_iota(jnp.int32, (1, pair_cap), 1)
        code = jnp.where(position < count[0], common + 1.0, 0.0).astype(jnp.bfloat16)
        offset = digits_of(starts[...] - region * segment)
        used = [jnp.full((1, per_block), digit, jnp.int32) for digit in (count[0] >> 7, count[0] & 127)]
        used = [digit.astype(jnp.float32).astype(jnp.bfloat16) for digit in used]
        rest = jnp.zeros((1, pair_cap - 4 * per_block), jnp.bfloat16)
        scalars = jnp.concatenate(list(offset) + used + [rest], axis=1)
        if digit_count(events) == 1:
            fields = [first[...].astype(jnp.float32).astype(jnp.bfloat16), second[...].astype(jnp.float32).astype(jnp.bfloat16)]
        else:
            fields = list(digits_of(first[...]) + digits_of(second[...]))
        fields += [code, scalars]
        copies[0].wait()
        for block in range(share * COMP // nch, regions):
            flat[block] = jnp.zeros((nch, segment), jnp.float32)
        for station in range(share):
            data = archive[station].astype(jnp.float32)
            row = station * COMP
            while row < (station + 1) * COMP:
                end = min((row // nch + 1) * nch, (station + 1) * COMP)
                flat[row // nch, row % nch : row % nch + end - row, :] = data[row - station * COMP : end - station * COMP]
                row = end
        for m in range(regions):
            out = outs[m] if separate(regions) else outs[0].at[m]
            out[:, :segment] = flat[region ^ m].astype(jnp.bfloat16)
            for k, field in enumerate(fields):
                lane = segment + k // 4 * pair_cap
                out[k % 4 : k % 4 + 1, lane : lane + pair_cap] = field

    return pl.pallas_call(
        kernel,
        out_shape=block_shapes(regions, (nch, segment + field_width(events, pair_cap)), jnp.bfloat16),
        in_specs=[pl.BlockSpec(memory_space=pltpu.HBM)] * 5 + [SMEM_ONLY],
        out_specs=[VMEM_ONLY] * number,
        scratch_shapes=[
            pltpu.VMEM((regions, nch, segment), jnp.float32),
            pltpu.VMEM((share, COMP, segment), archive.dtype),
            pltpu.VMEM(starts.shape, jnp.int32),
            pltpu.VMEM(station_mask.shape, jnp.int32),
            pltpu.VMEM(pair_first.shape, jnp.int32),
            pltpu.VMEM(pair_first.shape, jnp.int32),
            pltpu.SemaphoreType.DMA((5,)),
        ],
        name="pack",
    )(archive, starts, station_mask, pair_first, pair_second, pair_count)


def grant(rows):
    return min(rows * LANES * 4 * 5 // 4 + (4 << 20), 60 * 1024 * 1024)


class Cutter:
    def __init__(self, per_block, segment, nch):
        self.per_block, self.nch = per_block, nch
        self.rows = 2 * nch
        self.tiles = segment // LANES + 2
        self.count = per_block * nch
        self.spec_rows = 2 * self.rows * per_block

    def words(self, scalars, slot):
        tile, lane = scalars[:, : self.per_block], scalars[:, self.per_block : 2 * self.per_block]
        return ((tile + slot * self.tiles) * (256.0 * self.rows) + (LANES - lane)).astype(jnp.int32)

    def widen(self, source, shifted, slot):
        rows, nch = self.rows, self.nch
        first = slot * (self.tiles * rows)
        if not isinstance(slot, int):
            first = pl.multiple_of(first, rows)
        group = self.tiles // 2 if self.tiles % 2 == 0 else self.tiles

        def some_tiles(step, carry):
            for k in range(group):
                tile = step * group + k
                row = pl.multiple_of(first + tile * rows, rows)
                for ahead in range(2):
                    lane = pl.multiple_of((tile + 2 * ahead) * LANES, LANES)
                    shifted[pl.ds(row + ahead, nch, stride=2), :] = source[:, pl.ds(lane, LANES)].astype(jnp.float32)
            return carry

        lax.fori_loop(0, self.tiles // group, some_tiles, 0)

    def cut(self, word_of, shifted, windows, slot):
        rows = self.rows
        from_right = LANES - 1 - lax.broadcasted_iota(jnp.int32, (rows, LANES), 1)
        for event in range(self.per_block):
            word = word_of(event)
            first = pl.multiple_of(word >> 8, rows)
            turn = word & (2 * LANES - 1)
            data = [shifted[pl.ds(first + k * rows, rows), :] for k in range(3)]
            later = from_right < turn
            turn = turn & (LANES - 1)
            row = event * rows
            windows[slot, 0, row : row + rows, :] = pltpu.roll(jnp.where(later, data[0], data[1]), turn, 1)
            windows[slot, 1, row : row + rows, :] = pltpu.roll(jnp.where(later, data[1], data[2]), turn, 1)

    def transform(self, windows, slot, weight_rows, block, table, spec, place):
        per_block, nch, rows, count = self.per_block, self.nch, self.rows, self.count
        half = 2 * LANES
        inside = lax.broadcasted_iota(jnp.int32, (count, LANES), 1) < WIN - half - LANES
        pieces = [[jnp.concatenate([windows[slot, t, pl.ds(2 * c + k, per_block, stride=rows), :] for c in range(nch)])
                   for t in range(2)] for k in range(2)]
        squares = pieces[0][0] * pieces[0][0] + pieces[0][1] * pieces[0][1] + pieces[1][0] * pieces[1][0]
        squares += jnp.where(inside, pieces[1][1] * pieces[1][1], 0.0)
        energy = jnp.sum(squares, axis=1, keepdims=True)
        early, late = (jnp.concatenate(piece, axis=1).astype(jnp.bfloat16) for piece in pieces)
        coefs = jnp.dot(early, table[:half, :], preferred_element_type=jnp.float32)
        coefs += jnp.dot(late, table[half:, :], preferred_element_type=jnp.float32)
        first = block * count if isinstance(block, int) else pl.multiple_of(block * count, count)
        factor = weight_rows[pl.ds(first, count), :] * lax.rsqrt(energy + WIN * 1e-05)
        for s in range(2):
            for k in range(2):
                column = s * BINS + k * LANES
                piece = (coefs[:, column : column + LANES] * factor).astype(jnp.bfloat16).astype(jnp.float32)
                for c in range(nch):
                    row = place + s * rows + 2 * c + k
                    spec[pl.ds(row, per_block, stride=2 * rows), :] = piece[c * per_block : (c + 1) * per_block]


def scalar_field(events):
    return 2 * digit_count(events) + 1


def prepare(blocks, station_mask, event_owner, table, regions, chans, stations, per_block, pair_cap, segment, bucket, nch):
    cutter = Cutter(per_block, segment, nch)
    number = len(blocks)
    events = regions * per_block
    slots = regions * bucket
    share = station_share(stations, chans)
    k = scalar_field(events)

    def kernel(*refs):
        sources, refs = refs[:number], refs[number:]
        mask, owners, table, slot_event, weight_rows = refs[:5]
        region = lax.axis_index("region")
        if number:
            spec, shifted, windows, index_vmem, index, sem = refs[5:]
            for slot in range(number):
                lane = segment + k // 4 * pair_cap
                scalars = sources[slot][:, lane : lane + LANES].astype(jnp.float32)[k % 4 : k % 4 + 1]
                index_vmem[slot : slot + 1, :per_block] = cutter.words(scalars, slot)
            copy = pltpu.make_async_copy(index_vmem, index, sem)
            copy.start()
            for slot in range(number):
                cutter.widen(sources[slot], shifted, slot)

        listed = lax.broadcasted_iota(jnp.int32, (mask.shape[0], LANES), 0)
        usable = mask[...].astype(jnp.float32).astype(jnp.bfloat16)
        chan = lax.axis_index("chan")
        for c in range(nch):
            channel = region * nch + c
            local = jnp.minimum(chan * share, stations - share) + channel // COMP
            used = (channel < share * COMP) & (local >= chan * share)
            station = jnp.where(used, lax.axis_index("stn") * stations + local, -1)
            value = lax.dot_general(usable, as_bf16(listed == station), TN, preferred_element_type=jnp.float32)
            for part in range(regions):
                row = pl.multiple_of(((part ^ region) * nch + c) * per_block, per_block)
                weight_rows[pl.ds(row, per_block), :] = value[part * per_block : (part + 1) * per_block]

        owner = owners[...]
        owner = jnp.concatenate([owner[:, s * per_block : (s + 1) * per_block] for s in range(regions)], axis=0)
        earlier = as_bf16(lax.broadcasted_iota(jnp.int32, (per_block, per_block), 0)
                          < lax.broadcasted_iota(jnp.int32, (per_block, per_block), 1))
        rank = jnp.zeros((regions, per_block), jnp.float32)
        for r in range(regions):
            flags = (owner == r).astype(jnp.float32)
            before = jnp.dot(flags.astype(jnp.bfloat16), earlier, preferred_element_type=jnp.float32)
            rank += flags * before
        in_segment = lax.broadcasted_iota(jnp.int32, (regions, per_block), 0) * bucket + rank.astype(jnp.int32)
        slot_of = owner * slots + in_segment
        slot_lane = jnp.concatenate([slot_of[s : s + 1] for s in range(regions)], axis=1)
        names = digits_of(lax.broadcasted_iota(jnp.int32, (events, LANES), 0) + 1)
        place = lax.broadcasted_iota(jnp.int32, (slots, events), 0)

        def one_region(part, carry):
            hit = as_bf16(place + part * slots == slot_lane)
            high, low = (jnp.dot(hit, digit, preferred_element_type=jnp.float32) for digit in names)
            event = high * 128.0 + low - 1.0
            slot_event[pl.ds(pl.multiple_of(part * slots, slots), slots), :] = event.astype(slot_event.dtype)
            return carry

        if separate(regions):
            for part in range(regions):
                one_region(part, 0)
        else:
            lax.fori_loop(0, regions, one_region, 0)
        if number:
            copy.wait()
            for slot in range(number):
                cutter.cut(lambda event, slot=slot: index[slot, event], shifted, windows, slot)
                cutter.transform(windows, slot, weight_rows, slot, table, spec, slot * cutter.spec_rows)

    shapes = [jax.ShapeDtypeStruct((regions * slots, LANES), jnp.bfloat16 if digit_count(events) == 1 else jnp.float32),
              jax.ShapeDtypeStruct((events * nch, LANES), jnp.float32)]
    scratch = []
    if number:
        shapes.append(jax.ShapeDtypeStruct((number * cutter.spec_rows, LANES), jnp.float32))
        scratch = [
            pltpu.VMEM((number * cutter.tiles * cutter.rows, LANES), jnp.float32),
            pltpu.VMEM((number, 2, per_block * cutter.rows, LANES), jnp.float32),
            pltpu.VMEM((8, LANES), jnp.int32),
            pltpu.SMEM((8, LANES), jnp.int32),
            pltpu.SemaphoreType.DMA(()),
        ]
    used = number * (cutter.spec_rows + (cutter.tiles + 2 * per_block) * cutter.rows + 2 * segment * nch // LANES)
    used += regions * slots + 2 * events * nch + 2 * NFFT + (1024 if separate(regions) else 0)
    return pl.pallas_call(
        kernel,
        out_shape=shapes,
        in_specs=[VMEM_ONLY] * (number + 3),
        out_specs=[VMEM_ONLY] * len(shapes),
        scratch_shapes=scratch,
        compiler_params=pltpu.CompilerParams(vmem_limit_bytes=grant(used)),
        name="prepare",
    )(*blocks, station_mask, event_owner, table)


def correlate(regions, per_block, pair_cap, segment, slots, nch, ready):
    cutter = Cutter(per_block, segment, nch)
    rows, tiles = cutter.rows, cutter.tiles
    events = regions * per_block
    cols = pair_cap // LANES
    lines = pair_cap // STEP
    width = cols + slots // LANES
    batch = regions if separate(regions) else 1
    digits = digit_count(events)
    static = separate(regions)
    sources = regions if static else 1
    shift = per_block.bit_length() - 1
    assert per_block == 1 << shift

    def kernel(*refs):
        received, refs = refs[:sources], refs[sources:]
        (ready_spec, slot_event, weight_rows, table, weights, kept, given, shifted, windows, spec, prod, index_vmem, index,
         profile, folded, sem) = refs if ready else (None,) + refs
        region = lax.axis_index("region")

        def recv(m):
            return received[m] if static else received[0].at[m]

        def field(part, k):
            lane = segment + k // 4 * pair_cap
            return recv(part)[:, lane : lane + pair_cap].astype(jnp.float32)[k % 4 : k % 4 + 1]

        def listed(part, k):
            if digits == 1:
                return field(part, k)
            return field(part, 2 * k) * 128.0 + field(part, 2 * k + 1)

        for part in range(regions):
            rows_out = []
            for k in range(2):
                event = (listed(part, k).astype(jnp.int32) ^ (region << shift)) * (2 * rows)
                rows_out += [event[:, c * STEP : (c + 1) * STEP] for c in range(lines)]
            scalars = field(part, scalar_field(events))
            rows_out += [scalars[:, LANES : 2 * LANES].astype(jnp.int32)]
            for row, value in enumerate(rows_out):
                index_vmem[part, row : row + 1, : value.shape[1]] = value
            slot = part - ready if static else part
            index_vmem[part, 2 * lines + 1 : 2 * lines + 2, :per_block] = cutter.words(scalars, slot)
        copy = pltpu.make_async_copy(index_vmem, index, sem)
        copy.start()
        if static:
            if ready:
                spec[: ready * cutter.spec_rows, :] = ready_spec[...]
            for part in range(ready, regions):
                cutter.widen(recv(part), shifted, part - ready)
        else:
            def widen(part, carry):
                cutter.widen(recv(part), shifted, part)
                return carry

            lax.fori_loop(0, regions, widen, 0)
        copy.wait()

        def cut(slot, carry):
            cutter.cut(lambda event: index[slot + ready, 2 * lines + 1, event], shifted, windows, slot)
            return carry

        def cut_and_transform(part, carry):
            cutter.cut(lambda event: index[part, 2 * lines + 1, event], shifted, windows, 0)
            place = pl.multiple_of(part * cutter.spec_rows, cutter.spec_rows)
            cutter.transform(windows, 0, weight_rows, part, table, spec, place)
            return carry

        if static:
            for slot in range(regions - ready):
                cut(slot, 0)
            for part in range(ready, regions):
                cutter.transform(windows, part - ready, weight_rows, part, table, spec, part * cutter.spec_rows)
        else:
            lax.fori_loop(0, regions, cut_and_transform, 0)

        lane = lax.broadcasted_iota(jnp.int32, (rows, LANES), 1)
        sublane = lax.broadcasted_iota(jnp.int32, (rows, LANES), 0)
        chan = lax.axis_index("chan")
        special = (sublane % 2 == 0) & (lane == 0)
        upper = sublane < nch

        def one_group(group, carry):
            def some_pairs(member, row):
                part = group * batch + member
                for step in range(STEP):
                    a = pl.multiple_of(index[part, row, step], 2 * rows)
                    b = pl.multiple_of(index[part, lines + row, step], 2 * rows)
                    cos_a, sin_a = spec[pl.ds(a, rows), :], spec[pl.ds(a + rows, rows), :]
                    cos_b, sin_b = spec[pl.ds(b, rows), :], spec[pl.ds(b + rows, rows), :]
                    sines = sin_a * sin_b
                    even = cos_a * cos_b + sines
                    odd = jnp.where(special, sines, sin_a * cos_b - cos_a * sin_b)
                    even += pltpu.roll(even, nch, 0)
                    odd += pltpu.roll(odd, nch, 0)
                    place = pl.multiple_of((member * pair_cap + row * STEP + step) * rows, rows)
                    prod[pl.ds(place, rows), :] = jnp.where(upper, even, odd)
                return member

            def pairs_of(member, inner):
                part = group * batch + member
                pairs = index[part, 2 * lines, 0] * LANES + index[part, 2 * lines, per_block]
                lax.fori_loop(0, jnp.minimum((pairs + STEP - 1) >> STEP_BITS, lines), lambda row, m: some_pairs(m, row),
                              member)
                return inner

            for member in range(batch):
                pairs_of(member, 0)
            for member in range(batch):
                part = group * batch + member
                first_row = member * pair_cap * rows
                sums = []
                for k in (0, 1, nch, nch + 1):
                    total = prod[pl.ds(first_row + k, pair_cap, stride=rows), :]
                    for c in range(1, nch // 2):
                        total += prod[pl.ds(first_row + k + 2 * c, pair_cap, stride=rows), :]
                    sums.append(total.astype(jnp.bfloat16))
                both = lax.dot_general(weights[chan], jnp.concatenate(sums, axis=1), NT,
                                       preferred_element_type=jnp.float32)
                cross = both[:LANES] + both[LANES:]
                code = field(part, 2 * digits)
                live = jnp.maximum((code - 1.0) * COMP, 1.0)
                stack = jnp.where(code > 0.0, cross * lax.rsqrt(live), 0.0)
                fold(stack[:HALF_ROWS], kept.at[part], 0, width)
                fold(stack[HALF_ROWS:], folded.at[part], 0, width)
                first, second = listed(part, 0), listed(part, 1)
                stack = stack.astype(jnp.bfloat16)

                def hot(owner, event):
                    column = slot_event[pl.ds(pl.multiple_of(owner * slots, slots), slots), :]
                    column = jnp.concatenate([column] * cols, axis=1)
                    if digits > 1:
                        return as_bf16(column == event)
                    event = jnp.broadcast_to(event.astype(jnp.bfloat16), column.shape)
                    return jnp.where(column == event, jnp.ones((), jnp.bfloat16), jnp.zeros((), jnp.bfloat16))

                owner = part ^ region
                after = (owner + 1) & (regions - 1)
                hots = jnp.concatenate([hot(owner, first), hot(owner, second), hot(after, second)], axis=0)
                terms = lax.dot_general(stack, hots, NT, preferred_element_type=jnp.float32)
                profile[0, part] = terms[:, :slots]
                profile[1, part] = terms[:, slots : 2 * slots]
                profile[2, after ^ region] = terms[:, 2 * slots :]
            return carry

        if static:
            one_group(0, 0)
        else:
            lax.fori_loop(0, regions, one_group, 0)

        def lag_of(axis):
            row = lax.broadcasted_iota(jnp.int32, (LANES, LANES), axis)
            return jnp.where(row < HALF_ROWS, row + chan * HALF_LAGS, row - HALF_ROWS + (1 - chan) * HALF_LAGS)

        mirror = as_bf16(lag_of(0) + lag_of(1) == LAGS - 1)

        def finish(part, carry):
            value = profile[1, part] + profile[2, part]
            high = value.astype(jnp.bfloat16)
            low = (value - high.astype(jnp.float32)).astype(jnp.bfloat16)
            flipped = jnp.dot(mirror, high, preferred_element_type=jnp.float32) + jnp.dot(
                mirror, low, preferred_element_type=jnp.float32)
            total = profile[0, part] + flipped
            fold(total[:HALF_ROWS], kept.at[part], cols, width)
            fold(total[HALF_ROWS:], folded.at[part], cols, width)
            given[part] = folded[part].astype(jnp.bfloat16)
            return carry

        if static:
            for part in range(regions):
                finish(part, 0)
        else:
            lax.fori_loop(0, regions, finish, 0)

    shape = (regions, folded_rows(pair_cap + slots), LANES)
    index_rows = 8 * -(-(2 * lines + 2) // 8)
    used = regions * (tiles * rows + 3 * HALF_ROWS * width + 3 * LANES + index_rows + 4 * tiles + slots) + ready * cutter.spec_rows
    used += (2 * per_block * batch + 2 * events + batch * pair_cap) * rows + events * nch + 3 * NFFT
    return pl.pallas_call(
        kernel,
        out_shape=(jax.ShapeDtypeStruct(shape, jnp.float32), jax.ShapeDtypeStruct(shape, jnp.bfloat16)),
        in_specs=[VMEM_ONLY] * (sources + 4 + (ready > 0)),
        out_specs=(VMEM_ONLY, VMEM_ONLY),
        scratch_shapes=[
            pltpu.VMEM(((regions - ready) * tiles * rows, LANES), jnp.float32),
            pltpu.VMEM((batch, 2, per_block * rows, LANES), jnp.float32),
            pltpu.VMEM((2 * events * rows, LANES), jnp.float32),
            pltpu.VMEM((batch * pair_cap * rows, LANES), jnp.float32),
            pltpu.VMEM((regions, index_rows, LANES), jnp.int32),
            pltpu.SMEM((regions, index_rows, LANES), jnp.int32),
            pltpu.VMEM((3, regions, LANES, slots), jnp.float32),
            pltpu.VMEM(shape, jnp.float32),
            pltpu.SemaphoreType.DMA(()),
        ],
        compiler_params=pltpu.CompilerParams(vmem_limit_bytes=grant(used)),
        name="correlate",
    )


def assemble(whole, other, pair_cap, slots):
    tiles = pair_cap // LANES + slots // LANES

    def kernel(whole, other, stack, profile):
        first = lax.axis_index("chan") == 0
        halves = jnp.where(first, whole[...], other[...]), jnp.where(first, other[...], whole[...])
        for t in range(tiles):
            out, column = (stack, t * LANES) if t * LANES < pair_cap else (profile, t * LANES - pair_cap)
            lanes = pl.ds(column, LANES)
            for h, half in enumerate(halves):
                lag = h * HALF_LAGS
                out[lag : lag + TILE_ROWS, lanes] = half[t * TILE_ROWS : (t + 1) * TILE_ROWS]
                row = tiles * TILE_ROWS + t * (HALF_LAGS - TILE_ROWS)
                count = min(HALF_LAGS, LAGS - lag) - TILE_ROWS
                out[lag + TILE_ROWS : lag + TILE_ROWS + count, lanes] = half[row : row + count]

    return pl.pallas_call(
        kernel,
        out_shape=(jax.ShapeDtypeStruct((LAGS, pair_cap), jnp.float32),
                   jax.ShapeDtypeStruct((LAGS, slots), jnp.float32)),
        in_specs=[VMEM_ONLY] * 2,
        out_specs=(VMEM_ONLY, VMEM_ONLY),
        compiler_params=pltpu.CompilerParams(vmem_limit_bytes=grant(8 * HALF_ROWS * tiles)),
        name="assemble",
    )(whole, other)


def locate(archive, starts, event_owner, station_mask, pair_first, pair_second, pair_count):
    regions = lax.axis_size("region")
    chans = lax.axis_size("chan")
    per_block = starts.shape[0]
    pair_cap = pair_first.shape[0]
    stations = archive.shape[0]
    segment = archive.shape[2]
    bucket = max(2, 2 * per_block // regions)
    slots = regions * bucket
    share = station_share(stations, chans)
    nch = 4 * -(-share * COMP // (4 * regions))

    mask = station_mask.T
    blocks = pack(archive, starts.reshape(1, -1), mask, pair_first.reshape(1, -1),
                  pair_second.reshape(1, -1), pair_count, regions, chans, nch)
    received = exchange(blocks, regions)

    table = forward_table()
    ready = 1 if separate(regions) else 0
    slot_event, weight_rows, *spectra = prepare(
        received[:ready], mask, event_owner.reshape(1, -1), table, regions, chans, stations, per_block, pair_cap, segment,
        bucket, nch)
    kept, given = correlate(regions, per_block, pair_cap, segment, slots, nch, ready)(
        *received, *spectra, slot_event, weight_rows, table, lag_table())

    swap = [(0, 1), (1, 0)]
    swapped = lax.ppermute(given, "chan", swap)
    if separate(regions):
        sums = [kept[m] + swapped[m].astype(jnp.float32) for m in range(regions)]
        moved = exchange([term.astype(jnp.bfloat16) for term in sums], regions)
        whole = sums[0]
        for term in moved[1:]:
            whole = whole + term.astype(jnp.float32)
    else:
        moved = exchange([(kept + swapped.astype(jnp.float32)).astype(jnp.bfloat16)], regions)
        whole = jnp.sum(moved[0].astype(jnp.float32), axis=0)
    count = lax.axis_size("stn")
    step = 1
    while step < count:
        sent = whole.astype(jnp.bfloat16)
        other = lax.ppermute(sent, "stn", [(i, i ^ step) for i in range(count)])
        whole = sent.astype(jnp.float32) + other.astype(jnp.float32)
        step *= 2
    other = lax.ppermute(whole, "chan", swap)
    return assemble(whole, other, pair_cap, slots)


def solution(mesh):
    placed = (
        P("stn", None, ("groups", "region")),
        P(("groups", "region")),
        P("groups"),
        P("groups", None),
        P(("groups", "region")),
        P(("groups", "region")),
        P(("groups", "region")),
    )
    return jax.shard_map(
        locate,
        mesh=mesh,
        in_specs=placed,
        out_specs=(P(None, ("groups", "region")), P(None, ("groups", "region"))),
        check_vma=False,
    )
```

```python
import functools
import math

import jax
import jax.numpy as jnp
import numpy as np
from jax import lax
from jax.experimental import pallas as pl
from jax.experimental.pallas import tpu as pltpu
from jax.sharding import PartitionSpec as P


COMP = 3
WIN = 400
MAXLAG = 50
NFFT = 512
LAGS = 101
BINS = NFFT // 2
LANES = 128
HALF_LAGS = 51
HALF_ROWS = 56
TILE_ROWS = 48
STEP_BITS = 7
STEP = 1 << STEP_BITS
VMEM_ONLY = pl.BlockSpec(memory_space=pltpu.VMEM)
SMEM_ONLY = pl.BlockSpec(memory_space=pltpu.SMEM)
NT = (((1,), (1,)), ((), ()))
TN = (((0,), (0,)), ((), ()))


def forward_table():
    sample = np.arange(NFFT)[:, None]
    freq = np.arange(BINS)[None, :]
    angle = (sample * freq % NFFT) * (2.0 * math.pi / NFFT)
    sine = np.sin(angle)
    sine[:, 0] = np.cos(math.pi * (np.arange(NFFT) % 2))
    table = np.concatenate([np.cos(angle), sine], axis=1)
    table[WIN:] = 0.0
    return jnp.asarray(table, jnp.float32).astype(jnp.bfloat16)


def lag_table():
    shift = np.arange(2 * HALF_LAGS)[:, None] - MAXLAG
    freq = np.arange(BINS)[None, :]
    angle = (freq * shift % NFFT) * (2.0 * math.pi / NFFT)
    weight = np.where(freq == 0, 1.0 / NFFT, 2.0 / NFFT)
    even = weight * np.cos(angle)
    odd = -weight * np.sin(angle)
    odd[:, 0] = (np.cos(math.pi * (shift[:, 0] % 2)) - 1.0) / NFFT
    table = np.concatenate([even, odd], axis=1) * math.sqrt(WIN)
    table[LAGS:] = 0.0
    gap = np.zeros((HALF_ROWS - HALF_LAGS, NFFT))
    filler = np.zeros((LANES - 2 * HALF_ROWS, NFFT))
    halves = [np.concatenate([table[:HALF_LAGS], gap]), np.concatenate([table[HALF_LAGS:], gap])]
    table = np.stack([np.concatenate([halves[c], halves[1 - c], filler]) for c in range(2)])
    table = jnp.asarray(table, jnp.float32)
    high = table.astype(jnp.bfloat16)
    return jnp.concatenate([high, (table - high.astype(jnp.float32)).astype(jnp.bfloat16)], axis=1)


def as_bf16(flags):
    return flags.astype(jnp.float32).astype(jnp.bfloat16)


def digits_of(value):
    return (value >> 7).astype(jnp.float32).astype(jnp.bfloat16), (value & 127).astype(jnp.float32).astype(jnp.bfloat16)


def folded_rows(width):
    tiles = width // LANES
    return -(-HALF_LAGS * tiles // 16) * 16


def fold(value, store, first, tiles):
    for k in range(value.shape[1] // LANES):
        piece = value[:HALF_LAGS, k * LANES : (k + 1) * LANES]
        t = first + k
        store[t * TILE_ROWS : (t + 1) * TILE_ROWS, :] = piece[:TILE_ROWS]
        row = tiles * TILE_ROWS + t * (HALF_LAGS - TILE_ROWS)
        store[row : row + HALF_LAGS - TILE_ROWS, :] = piece[TILE_ROWS:]


def digit_count(events):
    return 1 if events <= 256 else 2


def field_width(events, pair_cap):
    return -(-(2 * digit_count(events) + 2) // 4) * pair_cap


def separate(regions):
    return regions <= 4


def block_shapes(regions, shape, dtype):
    if separate(regions):
        return [jax.ShapeDtypeStruct(shape, dtype)] * regions
    return [jax.ShapeDtypeStruct((regions,) + shape, dtype)]


def exchange(blocks, regions):
    if separate(regions):
        moved = {}
        for m in range(regions - 1, 0, -1):
            moved[m] = lax.ppermute(blocks[m], "region", [(i, i ^ m) for i in range(regions)])
        return [blocks[0]] + [moved[m] for m in range(1, regions)]
    order = jnp.arange(regions, dtype=jnp.int32) ^ lax.axis_index("region")
    moved = lax.all_to_all(jnp.take(blocks[0], order, axis=0), "region", split_axis=0, concat_axis=0, tiled=True)
    return [jnp.take(moved, order, axis=0)]


def station_share(stations, chans):
    return -(-stations // chans)


def pack(archive, starts, station_mask, pair_first, pair_second, pair_count, regions, chans, nch):
    stations, _, segment = archive.shape
    events = station_mask.shape[1]
    per_block = starts.shape[1]
    pair_cap = pair_first.shape[1]
    share = station_share(stations, chans)
    number = regions if separate(regions) else 1

    def kernel(*refs):
        sources, count, outs, refs = refs[:5], refs[5], refs[6 : 6 + number], refs[6 + number :]
        flat, archive, starts, mask, first, second, sems = refs
        region = lax.axis_index("region")
        chan = lax.axis_index("chan")
        base = jnp.minimum(chan * share, stations - share)
        sources = (sources[0].at[pl.ds(base, share)],) + sources[1:]
        copies = [pltpu.make_async_copy(source, target, sems.at[k])
                  for k, (source, target) in enumerate(zip(sources, (archive, starts, mask, first, second)))]
        for copy in copies:
            copy.start()
        for copy in copies[1:]:
            copy.wait()
        names = lax.broadcasted_iota(jnp.int32, (events, pair_cap), 0)
        usable = mask[...].astype(jnp.float32).astype(jnp.bfloat16)
        chosen = [jnp.dot(usable, as_bf16(names == ref[...]), preferred_element_type=jnp.float32)
                  for ref in (first, second)]
        common = jnp.sum(chosen[0] * chosen[1], axis=0, keepdims=True)
        position = lax.broadcasted_iota(jnp.int32, (1, pair_cap), 1)
        code = jnp.where(position < count[0], common + 1.0, 0.0).astype(jnp.bfloat16)
        offset = digits_of(starts[...] - region * segment)
        used = [jnp.full((1, per_block), digit, jnp.int32) for digit in (count[0] >> 7, count[0] & 127)]
        used = [digit.astype(jnp.float32).astype(jnp.bfloat16) for digit in used]
        rest = jnp.zeros((1, pair_cap - 4 * per_block), jnp.bfloat16)
        scalars = jnp.concatenate(list(offset) + used + [rest], axis=1)
        if digit_count(events) == 1:
            fields = [first[...].astype(jnp.float32).astype(jnp.bfloat16), second[...].astype(jnp.float32).astype(jnp.bfloat16)]
        else:
            fields = list(digits_of(first[...]) + digits_of(second[...]))
        fields += [code, scalars]
        copies[0].wait()
        for block in range(share * COMP // nch, regions):
            flat[block] = jnp.zeros((nch, segment), jnp.float32)
        for station in range(share):
            data = archive[station].astype(jnp.float32)
            row = station * COMP
            while row < (station + 1) * COMP:
                end = min((row // nch + 1) * nch, (station + 1) * COMP)
                flat[row // nch, row % nch : row % nch + end - row, :] = data[row - station * COMP : end - station * COMP]
                row = end
        for m in range(regions):
            out = outs[m] if separate(regions) else outs[0].at[m]
            out[:, :segment] = flat[region ^ m].astype(jnp.bfloat16)
            for k, field in enumerate(fields):
                lane = segment + k // 4 * pair_cap
                out[k % 4 : k % 4 + 1, lane : lane + pair_cap] = field

    return pl.pallas_call(
        kernel,
        out_shape=block_shapes(regions, (nch, segment + field_width(events, pair_cap)), jnp.bfloat16),
        in_specs=[pl.BlockSpec(memory_space=pltpu.HBM)] * 5 + [SMEM_ONLY],
        out_specs=[VMEM_ONLY] * number,
        scratch_shapes=[
            pltpu.VMEM((regions, nch, segment), jnp.float32),
            pltpu.VMEM((share, COMP, segment), archive.dtype),
            pltpu.VMEM(starts.shape, jnp.int32),
            pltpu.VMEM(station_mask.shape, jnp.int32),
            pltpu.VMEM(pair_first.shape, jnp.int32),
            pltpu.VMEM(pair_first.shape, jnp.int32),
            pltpu.SemaphoreType.DMA((5,)),
        ],
        name="pack",
    )(archive, starts, station_mask, pair_first, pair_second, pair_count)


def grant(rows):
    return min(rows * LANES * 4 * 5 // 4 + (4 << 20), 60 * 1024 * 1024)


class Cutter:
    def __init__(self, per_block, segment, nch):
        self.per_block, self.nch = per_block, nch
        self.rows = 2 * nch
        self.tiles = segment // LANES + 2
        self.count = per_block * nch
        self.spec_rows = 2 * self.rows * per_block

    def words(self, scalars, slot):
        tile, lane = scalars[:, : self.per_block], scalars[:, self.per_block : 2 * self.per_block]
        return ((tile + slot * self.tiles) * (256.0 * self.rows) + (LANES - lane)).astype(jnp.int32)

    def widen(self, source, shifted, slot):
        rows, nch = self.rows, self.nch
        first = slot * (self.tiles * rows)
        if not isinstance(slot, int):
            first = pl.multiple_of(first, rows)
        group = self.tiles // 2 if self.tiles % 2 == 0 else self.tiles

        def some_tiles(step, carry):
            for k in range(group):
                tile = step * group + k
                row = pl.multiple_of(first + tile * rows, rows)
                for ahead in range(2):
                    lane = pl.multiple_of((tile + 2 * ahead) * LANES, LANES)
                    shifted[pl.ds(row + ahead, nch, stride=2), :] = source[:, pl.ds(lane, LANES)].astype(jnp.float32)
            return carry

        lax.fori_loop(0, self.tiles // group, some_tiles, 0)

    def cut(self, word_of, shifted, windows, slot):
        rows = self.rows
        from_right = LANES - 1 - lax.broadcasted_iota(jnp.int32, (rows, LANES), 1)
        for event in range(self.per_block):
            word = word_of(event)
            first = pl.multiple_of(word >> 8, rows)
            turn = word & (2 * LANES - 1)
            data = [shifted[pl.ds(first + k * rows, rows), :] for k in range(3)]
            later = from_right < turn
            turn = turn & (LANES - 1)
            row = event * rows
            windows[slot, 0, row : row + rows, :] = pltpu.roll(jnp.where(later, data[0], data[1]), turn, 1)
            windows[slot, 1, row : row + rows, :] = pltpu.roll(jnp.where(later, data[1], data[2]), turn, 1)

    def transform(self, windows, slot, weight_rows, block, table, spec, place):
        per_block, nch, rows, count = self.per_block, self.nch, self.rows, self.count
        half = 2 * LANES
        inside = lax.broadcasted_iota(jnp.int32, (count, LANES), 1) < WIN - half - LANES
        pieces = [[jnp.concatenate([windows[slot, t, pl.ds(2 * c + k, per_block, stride=rows), :] for c in range(nch)])
                   for t in range(2)] for k in range(2)]
        squares = pieces[0][0] * pieces[0][0] + pieces[0][1] * pieces[0][1] + pieces[1][0] * pieces[1][0]
        squares += jnp.where(inside, pieces[1][1] * pieces[1][1], 0.0)
        energy = jnp.sum(squares, axis=1, keepdims=True)
        early, late = (jnp.concatenate(piece, axis=1).astype(jnp.bfloat16) for piece in pieces)
        coefs = jnp.dot(early, table[:half, :], preferred_element_type=jnp.float32)
        coefs += jnp.dot(late, table[half:, :], preferred_element_type=jnp.float32)
        first = block * count if isinstance(block, int) else pl.multiple_of(block * count, count)
        factor = weight_rows[pl.ds(first, count), :] * lax.rsqrt(energy + WIN * 1e-05)
        for s in range(2):
            for k in range(2):
                column = s * BINS + k * LANES
                piece = (coefs[:, column : column + LANES] * factor).astype(jnp.bfloat16).astype(jnp.float32)
                for c in range(nch):
                    row = place + s * rows + 2 * c + k
                    spec[pl.ds(row, per_block, stride=2 * rows), :] = piece[c * per_block : (c + 1) * per_block]


def scalar_field(events):
    return 2 * digit_count(events) + 1


def prepare(blocks, station_mask, event_owner, table, regions, chans, stations, per_block, pair_cap, segment, bucket, nch):
    cutter = Cutter(per_block, segment, nch)
    number = len(blocks)
    events = regions * per_block
    slots = regions * bucket
    share = station_share(stations, chans)
    k = scalar_field(events)

    def kernel(*refs):
        sources, refs = refs[:number], refs[number:]
        mask, owners, table, slot_event, weight_rows = refs[:5]
        region = lax.axis_index("region")
        if number:
            spec, shifted, windows, index_vmem, index, sem = refs[5:]
            for slot in range(number):
                lane = segment + k // 4 * pair_cap
                scalars = sources[slot][:, lane : lane + LANES].astype(jnp.float32)[k % 4 : k % 4 + 1]
                index_vmem[slot : slot + 1, :per_block] = cutter.words(scalars, slot)
            copy = pltpu.make_async_copy(index_vmem, index, sem)
            copy.start()
            for slot in range(number):
                cutter.widen(sources[slot], shifted, slot)

        listed = lax.broadcasted_iota(jnp.int32, (mask.shape[0], LANES), 0)
        usable = mask[...].astype(jnp.float32).astype(jnp.bfloat16)
        chan = lax.axis_index("chan")
        for c in range(nch):
            channel = region * nch + c
            local = jnp.minimum(chan * share, stations - share) + channel // COMP
            used = (channel < share * COMP) & (local >= chan * share)
            station = jnp.where(used, lax.axis_index("stn") * stations + local, -1)
            value = lax.dot_general(usable, as_bf16(listed == station), TN, preferred_element_type=jnp.float32)
            for part in range(regions):
                row = pl.multiple_of(((part ^ region) * nch + c) * per_block, per_block)
                weight_rows[pl.ds(row, per_block), :] = value[part * per_block : (part + 1) * per_block]

        owner = owners[...]
        owner = jnp.concatenate([owner[:, s * per_block : (s + 1) * per_block] for s in range(regions)], axis=0)
        earlier = as_bf16(lax.broadcasted_iota(jnp.int32, (per_block, per_block), 0)
                          < lax.broadcasted_iota(jnp.int32, (per_block, per_block), 1))
        rank = jnp.zeros((regions, per_block), jnp.float32)
        for r in range(regions):
            flags = (owner == r).astype(jnp.float32)
            before = jnp.dot(flags.astype(jnp.bfloat16), earlier, preferred_element_type=jnp.float32)
            rank += flags * before
        in_segment = lax.broadcasted_iota(jnp.int32, (regions, per_block), 0) * bucket + rank.astype(jnp.int32)
        slot_of = owner * slots + in_segment
        slot_lane = jnp.concatenate([slot_of[s : s + 1] for s in range(regions)], axis=1)
        names = digits_of(lax.broadcasted_iota(jnp.int32, (events, LANES), 0) + 1)
        place = lax.broadcasted_iota(jnp.int32, (slots, events), 0)

        def one_region(part, carry):
            hit = as_bf16(place + part * slots == slot_lane)
            high, low = (jnp.dot(hit, digit, preferred_element_type=jnp.float32) for digit in names)
            event = high * 128.0 + low - 1.0
            slot_event[pl.ds(pl.multiple_of(part * slots, slots), slots), :] = event.astype(slot_event.dtype)
            return carry

        if separate(regions):
            for part in range(regions):
                one_region(part, 0)
        else:
            lax.fori_loop(0, regions, one_region, 0)
        if number:
            copy.wait()
            for slot in range(number):
                cutter.cut(lambda event, slot=slot: index[slot, event], shifted, windows, slot)
                cutter.transform(windows, slot, weight_rows, slot, table, spec, slot * cutter.spec_rows)

    shapes = [jax.ShapeDtypeStruct((regions * slots, LANES), jnp.bfloat16 if digit_count(events) == 1 else jnp.float32),
              jax.ShapeDtypeStruct((events * nch, LANES), jnp.float32)]
    scratch = []
    if number:
        shapes.append(jax.ShapeDtypeStruct((number * cutter.spec_rows, LANES), jnp.float32))
        scratch = [
            pltpu.VMEM((number * cutter.tiles * cutter.rows, LANES), jnp.float32),
            pltpu.VMEM((number, 2, per_block * cutter.rows, LANES), jnp.float32),
            pltpu.VMEM((8, LANES), jnp.int32),
            pltpu.SMEM((8, LANES), jnp.int32),
            pltpu.SemaphoreType.DMA(()),
        ]
    used = number * (cutter.spec_rows + (cutter.tiles + 2 * per_block) * cutter.rows + 2 * segment * nch // LANES)
    used += regions * slots + 2 * events * nch + 2 * NFFT + (1024 if separate(regions) else 0)
    return pl.pallas_call(
        kernel,
        out_shape=shapes,
        in_specs=[VMEM_ONLY] * (number + 3),
        out_specs=[VMEM_ONLY] * len(shapes),
        scratch_shapes=scratch,
        compiler_params=pltpu.CompilerParams(vmem_limit_bytes=grant(used)),
        name="prepare",
    )(*blocks, station_mask, event_owner, table)


def correlate(regions, per_block, pair_cap, segment, slots, nch, ready):
    cutter = Cutter(per_block, segment, nch)
    rows, tiles = cutter.rows, cutter.tiles
    events = regions * per_block
    cols = pair_cap // LANES
    lines = pair_cap // STEP
    width = cols + slots // LANES
    batch = regions if separate(regions) else 1
    digits = digit_count(events)
    static = separate(regions)
    sources = regions if static else 1
    shift = per_block.bit_length() - 1
    assert per_block == 1 << shift

    def kernel(*refs):
        received, refs = refs[:sources], refs[sources:]
        (ready_spec, slot_event, weight_rows, table, weights, kept, given, shifted, windows, spec, prod, index_vmem, index,
         profile, folded, sem) = refs if ready else (None,) + refs
        region = lax.axis_index("region")

        def recv(m):
            return received[m] if static else received[0].at[m]

        def field(part, k):
            lane = segment + k // 4 * pair_cap
            return recv(part)[:, lane : lane + pair_cap].astype(jnp.float32)[k % 4 : k % 4 + 1]

        def listed(part, k):
            if digits == 1:
                return field(part, k)
            return field(part, 2 * k) * 128.0 + field(part, 2 * k + 1)

        for part in range(regions):
            rows_out = []
            for k in range(2):
                event = (listed(part, k).astype(jnp.int32) ^ (region << shift)) * (2 * rows)
                rows_out += [event[:, c * STEP : (c + 1) * STEP] for c in range(lines)]
            scalars = field(part, scalar_field(events))
            rows_out += [scalars[:, LANES : 2 * LANES].astype(jnp.int32)]
            for row, value in enumerate(rows_out):
                index_vmem[part, row : row + 1, : value.shape[1]] = value
            slot = part - ready if static else part
            index_vmem[part, 2 * lines + 1 : 2 * lines + 2, :per_block] = cutter.words(scalars, slot)
        copy = pltpu.make_async_copy(index_vmem, index, sem)
        copy.start()
        if static:
            if ready:
                spec[: ready * cutter.spec_rows, :] = ready_spec[...]
            for part in range(ready, regions):
                cutter.widen(recv(part), shifted, part - ready)
        else:
            def widen(part, carry):
                cutter.widen(recv(part), shifted, part)
                return carry

            lax.fori_loop(0, regions, widen, 0)
        copy.wait()

        def cut(slot, carry):
            cutter.cut(lambda event: index[slot + ready, 2 * lines + 1, event], shifted, windows, slot)
            return carry

        def cut_and_transform(part, carry):
            cutter.cut(lambda event: index[part, 2 * lines + 1, event], shifted, windows, 0)
            place = pl.multiple_of(part * cutter.spec_rows, cutter.spec_rows)
            cutter.transform(windows, 0, weight_rows, part, table, spec, place)
            return carry

        if static:
            for slot in range(regions - ready):
                cut(slot, 0)
            for part in range(ready, regions):
                cutter.transform(windows, part - ready, weight_rows, part, table, spec, part * cutter.spec_rows)
        else:
            lax.fori_loop(0, regions, cut_and_transform, 0)

        lane = lax.broadcasted_iota(jnp.int32, (rows, LANES), 1)
        sublane = lax.broadcasted_iota(jnp.int32, (rows, LANES), 0)
        chan = lax.axis_index("chan")
        special = (sublane % 2 == 0) & (lane == 0)
        upper = sublane < nch

        def one_group(group, carry):
            def some_pairs(member, row):
                part = group * batch + member
                for step in range(STEP):
                    a = pl.multiple_of(index[part, row, step], 2 * rows)
                    b = pl.multiple_of(index[part, lines + row, step], 2 * rows)
                    cos_a, sin_a = spec[pl.ds(a, rows), :], spec[pl.ds(a + rows, rows), :]
                    cos_b, sin_b = spec[pl.ds(b, rows), :], spec[pl.ds(b + rows, rows), :]
                    sines = sin_a * sin_b
                    even = cos_a * cos_b + sines
                    odd = jnp.where(special, sines, sin_a * cos_b - cos_a * sin_b)
                    first, other = jnp.where(upper, even, odd), jnp.where(upper, odd, even)
                    place = pl.multiple_of((member * pair_cap + row * STEP + step) * rows, rows)
                    prod[pl.ds(place, rows), :] = first + pltpu.roll(other, nch, 0)
                return None if static else member

            def pairs_of(member, inner):
                part = group * batch + member
                pairs = index[part, 2 * lines, 0] * LANES + index[part, 2 * lines, per_block]
                if static:
                    for row in range(lines):
                        pl.when(row * STEP < pairs)(functools.partial(some_pairs, member, row))
                else:
                    lax.fori_loop(0, jnp.minimum((pairs + STEP - 1) >> STEP_BITS, lines),
                                  lambda row, m: some_pairs(m, row), member)
                return inner

            for member in range(batch):
                pairs_of(member, 0)
            for member in range(batch):
                part = group * batch + member
                first_row = member * pair_cap * rows
                sums = []
                for k in (0, 1, nch, nch + 1):
                    total = prod[pl.ds(first_row + k, pair_cap, stride=rows), :]
                    for c in range(1, nch // 2):
                        total += prod[pl.ds(first_row + k + 2 * c, pair_cap, stride=rows), :]
                    sums.append(total.astype(jnp.bfloat16))
                both = lax.dot_general(weights[chan], jnp.concatenate(sums, axis=1), NT,
                                       preferred_element_type=jnp.float32)
                cross = both[:LANES] + both[LANES:]
                code = field(part, 2 * digits)
                live = jnp.maximum((code - 1.0) * COMP, 1.0)
                stack = jnp.where(code > 0.0, cross * lax.rsqrt(live), 0.0)
                fold(stack[:HALF_ROWS], kept.at[part], 0, width)
                fold(stack[HALF_ROWS:], folded.at[part], 0, width)
                first, second = listed(part, 0), listed(part, 1)
                stack = stack.astype(jnp.bfloat16)

                def hot(owner, event):
                    column = slot_event[pl.ds(pl.multiple_of(owner * slots, slots), slots), :]
                    column = jnp.concatenate([column] * cols, axis=1)
                    if digits > 1:
                        return as_bf16(column == event)
                    event = jnp.broadcast_to(event.astype(jnp.bfloat16), column.shape)
                    return jnp.where(column == event, jnp.ones((), jnp.bfloat16), jnp.zeros((), jnp.bfloat16))

                owner = part ^ region
                after = (owner + 1) & (regions - 1)
                hots = jnp.concatenate([hot(owner, first), hot(owner, second), hot(after, second)], axis=0)
                terms = lax.dot_general(stack, hots, NT, preferred_element_type=jnp.float32)
                profile[0, part] = terms[:, :slots]
                profile[1, part] = terms[:, slots : 2 * slots]
                profile[2, after ^ region] = terms[:, 2 * slots :]
            return carry

        if static:
            one_group(0, 0)
        else:
            lax.fori_loop(0, regions, one_group, 0)

        def lag_of(axis):
            row = lax.broadcasted_iota(jnp.int32, (LANES, LANES), axis)
            return jnp.where(row < HALF_ROWS, row + chan * HALF_LAGS, row - HALF_ROWS + (1 - chan) * HALF_LAGS)

        mirror = as_bf16(lag_of(0) + lag_of(1) == LAGS - 1)

        def finish(part, carry):
            value = profile[1, part] + profile[2, part]
            high = value.astype(jnp.bfloat16)
            low = (value - high.astype(jnp.float32)).astype(jnp.bfloat16)
            flipped = jnp.dot(mirror, high, preferred_element_type=jnp.float32) + jnp.dot(
                mirror, low, preferred_element_type=jnp.float32)
            total = profile[0, part] + flipped
            fold(total[:HALF_ROWS], kept.at[part], cols, width)
            fold(total[HALF_ROWS:], folded.at[part], cols, width)
            given[part] = folded[part].astype(jnp.bfloat16)
            return carry

        if static:
            for part in range(regions):
                finish(part, 0)
        else:
            lax.fori_loop(0, regions, finish, 0)

    shape = (regions, folded_rows(pair_cap + slots), LANES)
    index_rows = 8 * -(-(2 * lines + 2) // 8)
    used = regions * (tiles * rows + 3 * HALF_ROWS * width + 3 * LANES + index_rows + 4 * tiles + slots) + ready * cutter.spec_rows
    used += (2 * per_block * batch + 2 * events + batch * pair_cap) * rows + events * nch + 3 * NFFT
    return pl.pallas_call(
        kernel,
        out_shape=(jax.ShapeDtypeStruct(shape, jnp.float32), jax.ShapeDtypeStruct(shape, jnp.bfloat16)),
        in_specs=[VMEM_ONLY] * (sources + 4 + (ready > 0)),
        out_specs=(VMEM_ONLY, VMEM_ONLY),
        scratch_shapes=[
            pltpu.VMEM(((regions - ready) * tiles * rows, LANES), jnp.float32),
            pltpu.VMEM((batch, 2, per_block * rows, LANES), jnp.float32),
            pltpu.VMEM((2 * events * rows, LANES), jnp.float32),
            pltpu.VMEM((batch * pair_cap * rows, LANES), jnp.float32),
            pltpu.VMEM((regions, index_rows, LANES), jnp.int32),
            pltpu.SMEM((regions, index_rows, LANES), jnp.int32),
            pltpu.VMEM((3, regions, LANES, slots), jnp.float32),
            pltpu.VMEM(shape, jnp.float32),
            pltpu.SemaphoreType.DMA(()),
        ],
        compiler_params=pltpu.CompilerParams(vmem_limit_bytes=grant(used)),
        name="correlate",
    )


def assemble(whole, other, pair_cap, slots):
    tiles = pair_cap // LANES + slots // LANES

    def kernel(whole, other, stack, profile):
        first = lax.axis_index("chan") == 0
        halves = jnp.where(first, whole[...], other[...]), jnp.where(first, other[...], whole[...])
        for t in range(tiles):
            out, column = (stack, t * LANES) if t * LANES < pair_cap else (profile, t * LANES - pair_cap)
            lanes = pl.ds(column, LANES)
            for h, half in enumerate(halves):
                lag = h * HALF_LAGS
                out[lag : lag + TILE_ROWS, lanes] = half[t * TILE_ROWS : (t + 1) * TILE_ROWS]
                row = tiles * TILE_ROWS + t * (HALF_LAGS - TILE_ROWS)
                count = min(HALF_LAGS, LAGS - lag) - TILE_ROWS
                out[lag + TILE_ROWS : lag + TILE_ROWS + count, lanes] = half[row : row + count]

    return pl.pallas_call(
        kernel,
        out_shape=(jax.ShapeDtypeStruct((LAGS, pair_cap), jnp.float32),
                   jax.ShapeDtypeStruct((LAGS, slots), jnp.float32)),
        in_specs=[VMEM_ONLY] * 2,
        out_specs=(VMEM_ONLY, VMEM_ONLY),
        compiler_params=pltpu.CompilerParams(vmem_limit_bytes=grant(8 * HALF_ROWS * tiles)),
        name="assemble",
    )(whole, other)


def locate(archive, starts, event_owner, station_mask, pair_first, pair_second, pair_count):
    regions = lax.axis_size("region")
    chans = lax.axis_size("chan")
    per_block = starts.shape[0]
    pair_cap = pair_first.shape[0]
    stations = archive.shape[0]
    segment = archive.shape[2]
    bucket = max(2, 2 * per_block // regions)
    slots = regions * bucket
    share = station_share(stations, chans)
    nch = 4 * -(-share * COMP // (4 * regions))

    mask = station_mask.T
    blocks = pack(archive, starts.reshape(1, -1), mask, pair_first.reshape(1, -1),
                  pair_second.reshape(1, -1), pair_count, regions, chans, nch)
    received = exchange(blocks, regions)

    table = forward_table()
    ready = 1 if separate(regions) else 0
    slot_event, weight_rows, *spectra = prepare(
        received[:ready], mask, event_owner.reshape(1, -1), table, regions, chans, stations, per_block, pair_cap, segment,
        bucket, nch)
    kept, given = correlate(regions, per_block, pair_cap, segment, slots, nch, ready)(
        *received, *spectra, slot_event, weight_rows, table, lag_table())

    swap = [(0, 1), (1, 0)]
    swapped = lax.ppermute(given, "chan", swap)
    if separate(regions):
        sums = [kept[m] + swapped[m].astype(jnp.float32) for m in range(regions)]
        moved = exchange([term.astype(jnp.bfloat16) for term in sums], regions)
        whole = sums[0]
        for term in moved[1:]:
            whole = whole + term.astype(jnp.float32)
    else:
        moved = exchange([(kept + swapped.astype(jnp.float32)).astype(jnp.bfloat16)], regions)
        whole = jnp.sum(moved[0].astype(jnp.float32), axis=0)
    count = lax.axis_size("stn")
    step = 1
    while step < count:
        sent = whole.astype(jnp.bfloat16)
        other = lax.ppermute(sent, "stn", [(i, i ^ step) for i in range(count)])
        whole = sent.astype(jnp.float32) + other.astype(jnp.float32)
        step *= 2
    other = lax.ppermute(whole, "chan", swap)
    return assemble(whole, other, pair_cap, slots)


def solution(mesh):
    placed = (
        P("stn", None, ("groups", "region")),
        P(("groups", "region")),
        P("groups"),
        P("groups", None),
        P(("groups", "region")),
        P(("groups", "region")),
        P(("groups", "region")),
    )
    return jax.shard_map(
        locate,
        mesh=mesh,
        in_specs=placed,
        out_specs=(P(None, ("groups", "region")), P(None, ("groups", "region"))),
        check_vma=False,
    )
```
